32 devices in a mesh: rep: 4 (over y, x), dom: 8 (over z, core).
Axes of the slice: x: 2, y: 2, z: 4, core: 2. Of those that a mesh axis runs over, the one named last changes fastest.
Arguments:
- positions: float32 [4, 3, 8192], P('rep', None, 'dom'), may hold values from -6 to 6
- velocities: float32 [4, 3, 8192], P('rep', None, 'dom'), may hold values from -6 to 6
- charge: float32 [8192], P('dom'), may hold values from 0.5 to 2
- inverse_mass: float32 [8192], P('dom'), may hold values from 0.5 to 2
- pair_tiles: int32 [64, 6], P('dom'), may hold values from -1 to 11, as said below
- halo_tiles: int32 [8, 2, 2], P('dom'), may hold values from 0 to 7, as said below
- owners: int32 [64, 4], P('dom'), may hold values from 0 to 7, all different within a row; in each aligned block of 8 rows (0 to 7, 8 to 15, ...) at most 5 rows name the same one
- centres: float32 [3, 8192], P(None, 'dom'), may hold values from -6 to 6
- widths: float32 [8192], P('dom'), may hold values from 1 to 4
- map_density: float32 [8192], P('dom'), may hold values from 0.1 to 0.6
- map_error: float32 [8192], P('dom'), may hold values from 0.1 to 0.3
- partner: int32 [4], replicated, may hold values from 0 to 3, as said below
- decision: int32 [4], replicated, may hold values from 0 to 1, as said below
Outputs:
- new_positions: float32 [4, 3, 8192], P('rep', None, 'dom')
- new_velocities: float32 [4, 3, 8192], P('rep', None, 'dom')
- model_map: float32 [8192], P('dom')
The draws below stay inside these ranges and needn't reach their ends.
Inputs may be any that keep to these rules, and one draw needn't show every extreme that they name: `pair_tiles`: entry j of a tile's row names tile j of the same domain if j < 8; tile j - 8 of the upper list (row [d - 1, 1]) of the domain below if j < 10; else tile j - 10 of the lower list (row [d + 1, 0]) of the domain above; domains wrap around. -1 marks an empty entry; live entries of a row are distinct and come first. `halo_tiles`: row [d, 0] lists distinct tiles of domain d for domain d - 1, row [d, 1] distinct tiles for domain d + 1. `owners`: each row names 4 distinct domains; within the 8 rows of one domain no domain is named more than 5 times, a bound that some block reaches. `partner`: a permutation of the replicas; some replica r has partner r + 4 / 2 (counted round) and decision 1. `decision`: the same on all replicas of one cycle of partner; at least one replica is accepted and one is not.
All inputs are finite; a program needn't handle non-finite values.
Results may differ from the reference program's by a relative error of at most 0.0001.
Values sent between devices are 32-bit elements; how exact they have to be, the bound alone decides.
No kernel may reach another device: no remote copies, remote signals or barrier semaphores. Data moves between devices by JAX's collectives and lax.ppermute only.
A program may use at most 64 MiB of HBM per device.

```python
import math
import jax
import jax.numpy as jnp
import numpy as np
from jax import lax

TILE = 128
NB = 6
OWN = 4
STEPS = 2
NT = 8
COMP_DEV = 1024
REPS = 4
DOMS = 8
HALO_T = 2
CAP = 5
ATOMS = 8192
COMPS = 8192


def draw_halo_tiles(key, part):
    scores = jax.random.randint(key, (DOMS, 2, NT), 0, 65536) * NT + jnp.arange(NT, dtype=jnp.int32)
    ordering = jnp.argsort(scores, axis=-1)
    return ordering[:, :, :HALO_T].astype(jnp.int32)


def draw_pair_tiles(key, part):
    extent = NT + 2 * HALO_T
    row_count = DOMS * NT
    first_key, second_key = jax.random.split(key)
    scores = jax.random.randint(first_key, (row_count, extent), 0, 65536) * extent + jnp.arange(extent, dtype=jnp.int32)
    row_ids = jnp.arange(row_count, dtype=jnp.int32)
    column_ids = jnp.arange(extent, dtype=jnp.int32)
    leading = (row_ids[:, None] % NT == 0) & (column_ids[None, :] == extent - 1)
    lowered = (row_ids[:, None] % NT == 1) & (column_ids[None, :] == NT)
    scores = jnp.where(leading | lowered, -1, scores)
    chosen = jnp.argsort(scores, axis=-1)[:, :NB].astype(jnp.int32)
    live_count = jax.random.randint(second_key, (row_count,), max(1, NB // 2), NB + 1)
    live_count = jnp.where(row_ids % NT == 0, NB, live_count)
    live_count = jnp.where(row_ids % NT == 1, max(1, NB // 2), live_count)
    filled = jnp.arange(NB, dtype=jnp.int32)[None, :] < live_count[:, None]
    return jnp.where(filled, chosen, -1).astype(jnp.int32)


def pairing(key):
    folded = jax.random.fold_in(key, 7)
    first_key, second_key, third_key = jax.random.split(folded, 3)
    replica_ids = jnp.arange(REPS, dtype=jnp.int32)
    anchor = jax.random.randint(first_key, (), 0, REPS)
    scores = jax.random.randint(second_key, (REPS,), 0, 65536) * REPS + replica_ids
    scores = jnp.where(replica_ids == anchor, -2, scores)
    scores = jnp.where(replica_ids == (anchor + REPS // 2) % REPS, -1, scores)
    ordering = jnp.argsort(scores).astype(jnp.int32)
    cut = jax.random.randint(third_key, (), min(3, REPS - 1), REPS)
    rest = jnp.maximum(REPS - cut, 1)
    following = jnp.where(replica_ids < cut, (replica_ids + 1) % cut, cut + (replica_ids - cut + 1) % rest)
    mates = jnp.zeros((REPS,), jnp.int32).at[ordering].set(ordering[following])
    accepted = jnp.zeros((REPS,), jnp.int32).at[ordering].set((replica_ids < cut).astype(jnp.int32))
    return (mates.astype(jnp.int32), accepted.astype(jnp.int32))


def draw_partner(key, part):
    return pairing(key)[0]


def draw_decision(key, part):
    return pairing(key)[1]


def shard_levels(key, shape, shards, smallest, top_value):
    gain, own = 1.0, jax.random.fold_in(key, 6)
    for dim, blocks in shards:
        steps = jnp.exp(jax.random.uniform(jax.random.fold_in(own, dim), (blocks,), jnp.float32, smallest / len(shards), top_value / len(shards)))
        gain = gain * jnp.repeat(steps, shape[dim] // blocks).reshape([-1 if axis == dim else 1 for axis in range(len(shape))])
    return gain


def routed_block(own_key, own, number, rows, amount, top, limit, skew):
    sequence = jax.random.permutation(own_key, amount)
    packed, ordinary = portions_of(amount, rows * top, limit, skew, True), portions_of(amount, rows * top, limit, skew, False)
    places = jnp.arange(amount)

    def named(tallies, offset_by):
        used = int((tallies > 0).sum())
        fixed = max(1, used // 4)
        moved = fixed + (places - fixed + offset_by * (used - fixed)) % max(1, amount - fixed)
        return jnp.zeros((amount,), jnp.int32).at[sequence[jnp.where(places < fixed, places, moved)]].set(jnp.asarray(tallies, jnp.int32))

    tallies = jnp.where(number % 4 == 0, named(packed, number // 4), named(ordinary, number - number // 4 - 1))
    mixed = jax.random.permutation(jax.random.fold_in(own, 3), amount)
    source_of, taker = mixed[0:amount // 2 * 2:2], mixed[1:amount // 2 * 2:2]
    margin = jnp.minimum(tallies[source_of] - 1, limit - tallies[taker]) // 2
    margin = jnp.where((source_of == sequence[0]) | (taker == sequence[0]) | (tallies[taker] == 0), 0, jnp.maximum(margin, 0))
    moved = jax.random.randint(jax.random.fold_in(own, 4), (amount // 2,), 0, 1 << 20) % (margin + 1)
    tallies = tallies.at[source_of].add(-moved).at[taker].add(moved)
    labels = jnp.searchsorted(jnp.cumsum(tallies), jnp.arange(rows * top), side="right").astype(jnp.int32)
    table = labels.reshape(top, rows).T
    table = table[jax.random.permutation(jax.random.fold_in(own, 1), rows)]
    offset_by = jax.random.randint(jax.random.fold_in(own, 2), (rows, 1), 0, top)
    return jnp.take_along_axis(table, (jnp.arange(top)[None, :] + offset_by) % top, axis=1)


def portions_of(number_of, total, reach, lean, full):
    weights = [(1 << 20) // math.isqrt(rank ** lean) + 1 for rank in range(1, number_of + 1)]
    largest = reach if full else min(reach, max(-(-total // number_of), total * weights[0] // sum(weights)))
    least = 1 if total - largest >= number_of - 1 else 0
    given, spare = [largest] + [least] * (number_of - 1), total - largest - least * (number_of - 1)
    while spare > 0:
        free = [i for i in range(1, number_of) if given[i] < largest] or [i for i in range(1, number_of) if given[i] < reach]
        mass, left = sum([weights[i] for i in free]), spare
        for i in free:
            extra = min(reach - given[i], max(1, left * weights[i] // mass), spare)
            given[i] = given[i] + extra
            spare = spare - extra
    return np.array(given)


def noise(rng, shape, deviation, bound, shards=(), kind=jnp.bfloat16):
    values = jax.random.normal(rng, shape, jnp.float32) * deviation
    if len(shards) > 0:
        values = shard_levels(rng, shape, shards, -0.22, 0.18) * values
    return jnp.clip(values, min=-bound, max=bound).astype(kind)


def setup_inputs(seed: int = 0) -> dict:
    key_list = jax.random.split(jax.random.key(seed), 14)
    positions = noise(key_list[0], (REPS, 3, ATOMS), 1.0, 6.0, ((0, 4), (2, 8)), jnp.float32)
    velocities = noise(key_list[1], (REPS, 3, ATOMS), 1.0, 6.0, ((0, 4), (2, 8)), jnp.float32)
    charge = jnp.clip(jnp.exp(math.log(2.0) - 1.3862944 * jax.random.uniform(key_list[2], (ATOMS,), jnp.float32) ** shard_levels(key_list[2], (ATOMS,), ((0, 8),), -0.2, 0.2)), 0.5, 2.0)
    inverse_mass = jnp.clip(jnp.exp(math.log(2.0) - 1.3862944 * jax.random.uniform(key_list[3], (ATOMS,), jnp.float32) ** shard_levels(key_list[3], (ATOMS,), ((0, 8),), -0.2, 0.2)), 0.5, 2.0)
    pair_tiles = draw_pair_tiles(jax.random.fold_in(key_list[13], 71), 0)
    halo_tiles = draw_halo_tiles(jax.random.fold_in(key_list[13], 71), 0)
    owners_keys = jax.random.split(jax.random.fold_in(key_list[6], 1), (DOMS * NT) // NT)
    owners_turns = jax.random.permutation(jax.random.fold_in(key_list[6], 3), (DOMS * NT) // NT)
    owners = jax.vmap(lambda own, number: routed_block(jax.random.fold_in(key_list[6], 2), own, number, NT, DOMS, OWN, CAP, 2))(owners_keys, owners_turns).reshape((DOMS * NT, OWN))
    centres = noise(key_list[7], (3, COMPS), 1.0, 6.0, ((1, 8),), jnp.float32)
    widths = jnp.clip(jnp.exp(math.log(4.0) - 1.3862944 * jax.random.uniform(key_list[8], (COMPS,), jnp.float32) ** shard_levels(key_list[8], (COMPS,), ((0, 8),), -0.2, 0.2)), 1.0, 4.0)
    map_density = jnp.clip(0.1 + 0.5 * jax.random.uniform(key_list[9], (COMPS,), jnp.float32) ** shard_levels(key_list[9], (COMPS,), ((0, 8),), -0.2, 0.2), 0.1, 0.6)
    map_error = jnp.clip(jnp.exp(math.log(0.3) - 1.0986123 * jax.random.uniform(key_list[10], (COMPS,), jnp.float32) ** shard_levels(key_list[10], (COMPS,), ((0, 8),), -0.2, 0.2)), 0.1, 0.3)
    partner = draw_partner(jax.random.fold_in(key_list[13], 71), 0)
    decision = draw_decision(jax.random.fold_in(key_list[13], 71), 0)
    return {"positions": positions, "velocities": velocities, "charge": charge, "inverse_mass": inverse_mass, "pair_tiles": pair_tiles, "halo_tiles": halo_tiles, "owners": owners, "centres": centres, "widths": widths, "map_density": map_density, "map_error": map_error, "partner": partner, "decision": decision}


highest = lax.Precision.HIGHEST
time_step = 0.5
pair_width = 1.0
map_scale = 2.0


def pair_force(own_tiles, neighbours, pair_gain):
    squared = jnp.zeros(neighbours.shape[:2] + (own_tiles.shape[2], neighbours.shape[3]), jnp.float32)
    for dim_index in range(3):
        apart = own_tiles[:, None, dim_index, :, None] - neighbours[:, :, dim_index, None, :]
        squared = squared + apart * apart
    weights = jnp.exp(-squared / (2.0 * pair_width)) * neighbours[:, :, 3, None, :]
    weight_sum = jnp.sum(weights, (1, 3))
    pulled = jnp.einsum('bjat,bjct->bca', weights, neighbours[:, :, :3, :], precision=highest)
    return (pair_gain / pair_width) * own_tiles[:, 3, None, :] * (own_tiles[:, :3, :] * weight_sum[:, None, :] - pulled)


def tile_gaussians(coords, centre, extent):
    squared = jnp.zeros((coords.shape[0], centre.shape[1], coords.shape[2], centre.shape[3]), jnp.float32)
    for dim_index in range(3):
        apart = coords[:, None, dim_index, :, None] - centre[:, :, dim_index, None, :]
        squared = squared + apart * apart
    return jnp.exp(-squared / (2.0 * extent[:, :, None, :]))


def neighbour_ids(pair_tiles, halo_tiles):
    domain_ids = jnp.arange(DOMS * NT, dtype=jnp.int32) // NT
    lower_dom = (domain_ids - 1) % DOMS
    upper_dom = (domain_ids + 1) % DOMS
    entries = pair_tiles
    local_ids = domain_ids[:, None] * NT + entries
    lower_list = halo_tiles[lower_dom][:, 1, :]
    upper_list = halo_tiles[upper_dom][:, 0, :]
    lower_index = jnp.clip(entries - NT, 0, HALO_T - 1).astype(jnp.int32)
    upper_index = jnp.clip(entries - NT - HALO_T, 0, HALO_T - 1).astype(jnp.int32)
    from_lower = lower_dom[:, None] * NT + jnp.take_along_axis(lower_list, lower_index, 1)
    from_upper = upper_dom[:, None] * NT + jnp.take_along_axis(upper_list, upper_index, 1)
    global_ids = jnp.where(entries < NT, local_ids, jnp.where(entries < NT + HALO_T, from_lower, from_upper))
    return jnp.where(entries < 0, -1, global_ids).astype(jnp.int32)


def reference(positions, velocities, charge, inverse_mass, pair_tiles, halo_tiles, owners, centres, widths, map_density, map_error, partner, decision):
    tile_count = DOMS * NT
    tile_ids = neighbour_ids(pair_tiles, halo_tiles)
    valid_mask = (tile_ids >= 0).astype(jnp.float32)
    safe_ids = jnp.maximum(tile_ids, 0)
    charges = charge.reshape(tile_count, TILE)
    inverse = inverse_mass.reshape(tile_count, TILE)
    centre_table = centres.reshape(3, DOMS, COMP_DEV).transpose(1, 0, 2)
    width_table = widths.reshape(DOMS, COMP_DEV)
    density_table = map_density.reshape(DOMS, COMP_DEV)
    error_table = map_error.reshape(DOMS, COMP_DEV)
    chosen_centres = centre_table[owners]
    chosen_widths = width_table[owners]
    pair_gain = (NB * TILE) ** -0.5
    intersection_scale = 1.0 / (OWN * NT * TILE)
    map_gain = map_scale / (OWN * COMP_DEV)
    blocks = tile_count // 8

    def blocked(array):
        return array.reshape((blocks, 8) + array.shape[1:])

    def nonbonded(coords):
        stacked = jnp.concatenate([coords, charges[:, None, :]], 1)
        near_tiles = stacked[safe_ids] * valid_mask[:, :, None, None]

        def one_block(pieces):
            return pair_force(pieces[0], pieces[1], pair_gain)

        return lax.map(one_block, (blocked(stacked), blocked(near_tiles))).reshape(tile_count, 3, TILE)

    def intersections(coords):
        def one_block(pieces):
            return jnp.sum(tile_gaussians(pieces[0], pieces[1], pieces[2]), 2) * intersection_scale

        partial_value = lax.map(one_block, (blocked(coords), blocked(chosen_centres), blocked(chosen_widths)))
        return jax.ops.segment_sum(partial_value.reshape(tile_count * OWN, COMP_DEV), owners.reshape(-1), DOMS)

    def map_forces(coords, coefficient):
        chosen_coef = coefficient[owners]

        def one_block(pieces):
            weighted = tile_gaussians(pieces[0], pieces[1], pieces[2]) * pieces[3][:, :, None, :]
            row_sum = jnp.sum(weighted, (1, 3))
            pulled = jnp.einsum('bjak,bjck->bca', weighted, pieces[1], precision=highest)
            return pieces[0] * row_sum[:, None, :] - pulled

        return lax.map(one_block, (blocked(coords), blocked(chosen_centres), blocked(chosen_widths), blocked(chosen_coef))).reshape(tile_count, 3, TILE)

    position = positions.reshape(REPS, 3, tile_count, TILE).transpose(0, 2, 1, 3)
    velocity = velocities.reshape(REPS, 3, tile_count, TILE).transpose(0, 2, 1, 3)
    model_map = jnp.zeros((DOMS, COMP_DEV), jnp.float32)
    for step_index in range(STEPS):
        summed = jnp.sum(lax.map(intersections, position), 0)
        model_map = summed / REPS
        coefficient = map_gain * (model_map - density_table) / (error_table * error_table) / width_table

        def replica_forces(coords):
            return nonbonded(coords) + map_forces(coords, coefficient)

        forces = lax.map(replica_forces, position)
        velocity = velocity + time_step * inverse[None, :, None, :] * forces
        position = position + time_step * velocity
    source = jnp.where(decision == 1, partner, jnp.arange(REPS, dtype=jnp.int32))
    position = position[source].transpose(0, 2, 1, 3).reshape(REPS, 3, tile_count * TILE)
    velocity = velocity[source].transpose(0, 2, 1, 3).reshape(REPS, 3, tile_count * TILE)
    return position, velocity, model_map.reshape(-1)
```

```python
import functools
import math

import jax
import jax.numpy as jnp
from jax import lax
from jax.experimental import pallas as pl
from jax.experimental.pallas import tpu as pltpu
from jax.sharding import Mesh, PartitionSpec as P

STEPS = 2
CORES = 2
DEPTH = 32
ROWS = 16
ONE_PHASE_BYTES = 1 << 20

time_step = 0.5
pair_width = 1.0
map_scale = 2.0
log2e = math.log2(math.e)
f32 = jnp.float32
bf16 = jnp.bfloat16

LEFT_PARTS = (0, 0, 1, 1, 0, 2)
RIGHT_PARTS = (0, 1, 0, 1, 2, 0)


def split3(value):
    high = value.astype(bf16).astype(f32)
    rest = value - high
    middle = rest.astype(bf16).astype(f32)
    return high, middle, rest - middle


def point_rows(coords):
    rows = []
    for coord in coords:
        parts = split3(coord)
        rows += [parts[i] for i in LEFT_PARTS]
    parts = split3(coords[0] * coords[0] + coords[1] * coords[1] + coords[2] * coords[2])
    rows += [parts[i] for i in LEFT_PARTS]
    one = jnp.ones_like(coords[0])
    return rows + [one, one, one]


def centre_rows(coords, extent):
    scale = log2e / extent
    rows = []
    for coord in coords:
        parts = split3(coord * scale)
        rows += [parts[i] for i in RIGHT_PARTS]
    parts = split3(-0.5 * scale)
    rows += [parts[i] for i in RIGHT_PARTS]
    square = coords[0] * coords[0] + coords[1] * coords[1] + coords[2] * coords[2]
    return rows + list(split3(-0.5 * scale * square))


def pull_rows(coords, weight):
    rows = list(split3(weight))
    for coord in coords:
        rows += list(split3(coord * weight))
    return rows


def gaussians(left, right):
    return jnp.exp2(jnp.dot(left, right, preferred_element_type=f32))


def pulled_by(rows, weights):
    dims = (((1,), (1,)), ((), ()))
    high = weights.astype(bf16)
    low = (weights - high.astype(f32)).astype(bf16)
    return lax.dot_general(rows, high, dims, preferred_element_type=f32) + lax.dot_general(
        rows, low, dims, preferred_element_type=f32
    )


def pushes(coords, sums):
    def total(first):
        return sums[first : first + 1] + sums[first + 1 : first + 2] + sums[first + 2 : first + 3]

    strength = total(0)
    return [coords[i] * strength - total(3 + 3 * i) for i in range(3)]


def store_rows(ref, rows):
    for index, row in enumerate(rows):
        ref[:, index, :] = row
    depth = ref.shape[1]
    if len(rows) < depth:
        ref[:, len(rows) : depth, :] = jnp.zeros(
            (ref.shape[0], depth - len(rows), ref.shape[2]), f32
        )


def chunks(total, wanted):
    size = wanted if total % wanted == 0 else total
    return [(start, size) for start in range(0, total, size)]


def intersect_kernel(scale, owners_ref, x_ref, comp_ref, out_ref, left_ref, right_ref, xs, cs, acc):
    domains, _, width = comp_ref.shape
    tiles = x_ref.shape[1]
    owned = owners_ref.shape[0] // tiles
    store_rows(xs, point_rows([x_ref[i] for i in range(3)]))
    store_rows(cs, centre_rows([comp_ref[:, i, :] for i in range(3)], comp_ref[:, 3, :]))
    right_ref[...] = cs[...].astype(bf16)
    acc[...] = jnp.zeros_like(acc)

    def one_tile(tile, carry):
        left = xs[tile].T.astype(bf16)
        left_ref[tile] = left
        for j in range(owned):
            owner = owners_ref[tile * owned + j]
            for start, size in chunks(width, 256):
                g = gaussians(left, right_ref[owner, :, start : start + size])
                acc[owner, :, start : start + size] += jnp.sum(
                    g.reshape(g.shape[0] // 8, 8, size), 0
                )
        return carry

    lax.fori_loop(0, tiles, one_tile, 0)
    total = jnp.sum(acc[...], 1) * scale
    for row in range(out_ref.shape[0]):
        out_ref[row] = total


def push_kernel(
    gain, replicas, owners_ref, core_ref, x_ref, comp_ref, sums_ref, left_ref, right_ref, pair_ref,
    out_ref, mean_ref, rs
):
    domains, _, width = comp_ref.shape
    tiles = x_ref.shape[1]
    owned = owners_ref.shape[0] // tiles
    mean = jnp.sum(sums_ref[...], 0) / replicas
    mean_ref[...] = mean
    error = comp_ref[:, 5, :]
    coefficient = gain * (mean - comp_ref[:, 4, :]) / (error * error) / comp_ref[:, 3, :]
    store_rows(rs, pull_rows([comp_ref[:, i, :] for i in range(3)], coefficient))

    def one_tile(tile, carry):
        left = left_ref[tile]
        sums = jnp.zeros((ROWS, x_ref.shape[2]), f32)
        for j in range(owned):
            owner = owners_ref[tile * owned + j]
            for start, size in chunks(width, 256):
                g = gaussians(left, right_ref[owner, :, start : start + size])
                sums += pulled_by(rs[owner, :, start : start + size].astype(bf16), g)
        coords = [x_ref[i, pl.ds(tile, 1), :] for i in range(3)]
        for i, push in enumerate(pushes(coords, sums)):
            out_ref[i, pl.ds(tile, 1), :] = push
        return carry

    lax.fori_loop(0, tiles, one_tile, 0)
    own = tiles // CORES
    for core in range(CORES):

        @pl.when(core_ref[0] == core)
        def _():
            out_ref[:, core * own : (core + 1) * own, :] += pair_ref[...]


def pair_kernel(
    gain, pairs_ref, lists_ref, core_ref, x_ref, charge_ref, far_ref, left_ref, out_ref, table, cs, rs
):
    own = out_ref.shape[1]
    near = pairs_ref.shape[0] // own
    listed = far_ref.shape[1]
    core = core_ref[0]
    base = core * own
    other = (1 - core) * own
    extent = own + 2 * listed
    table[...] = jnp.zeros_like(table)
    for i in range(4):
        source = charge_ref if i == 3 else x_ref.at[i]
        table[i, 0:own, :] = source[pl.ds(pl.multiple_of(base, own), own), :]
        for k in range(listed):
            local = source[pl.ds(other + lists_ref[k], 1), :]
            distant = far_ref[i, k : k + 1, :]
            low = jnp.where(core == 0, distant, local)
            high = jnp.where(core == 0, local, distant)
            table[i, own + k : own + k + 1, :] = low
            table[i, own + listed + k : own + listed + k + 1, :] = high
    coords = [table[i] for i in range(3)]
    store_rows(cs, centre_rows(coords, jnp.full_like(coords[0], pair_width)))
    store_rows(rs, pull_rows(coords, table[3]))

    def one_tile(tile, carry):
        left = left_ref[base + tile]
        sums = jnp.zeros((ROWS, x_ref.shape[2]), f32)
        for j in range(near):
            entry = pairs_ref[tile * near + j]
            entry = jnp.where(entry < 0, extent, entry)
            g = gaussians(left, cs[entry].astype(bf16))
            sums += pulled_by(rs[entry].astype(bf16), g)
        coords = [x_ref[i, pl.ds(base + tile, 1), :] for i in range(3)]
        strength = gain / pair_width * charge_ref[pl.ds(base + tile, 1), :]
        for i, push in enumerate(pushes(coords, sums)):
            out_ref[i, pl.ds(tile, 1), :] = strength * push
        return carry

    lax.fori_loop(0, own, one_tile, 0)


def vmem(count):
    return [pl.BlockSpec(memory_space=pltpu.VMEM)] * count


def smem(count):
    return [pl.BlockSpec(memory_space=pltpu.SMEM)] * count


def shape(*dims, dtype=f32):
    return jax.ShapeDtypeStruct(dims, dtype)


def intersect(owners, x, comps, copies, scale):
    domains, _, width = comps.shape
    tiles, lanes = x.shape[1:]
    return pl.pallas_call(
        functools.partial(intersect_kernel, scale),
        out_shape=(
            shape(copies, domains, width),
            shape(tiles, lanes, DEPTH, dtype=bf16),
            shape(domains, DEPTH, width, dtype=bf16),
        ),
        in_specs=smem(1) + vmem(2),
        out_specs=tuple(vmem(3)),
        scratch_shapes=[
            pltpu.VMEM((tiles, DEPTH, lanes), f32),
            pltpu.VMEM((domains, DEPTH, width), f32),
            pltpu.VMEM((domains, 8, width), f32),
        ],
        name="intersect",
    )(owners, x, comps)


def push(owners, core, x, comps, sums, left, right, pair, gain, replicas):
    domains, _, width = comps.shape
    tiles, lanes = x.shape[1:]
    return pl.pallas_call(
        functools.partial(push_kernel, gain, replicas),
        out_shape=(shape(3, tiles, lanes), shape(domains, width)),
        in_specs=smem(2) + vmem(6),
        out_specs=tuple(vmem(2)),
        scratch_shapes=[pltpu.VMEM((domains, ROWS, width), f32)],
        name="push",
    )(owners, core, x, comps, sums, left, right, pair)


def pair_push(pairs, lists, core, x, charge, far, left, gain):
    tiles, lanes = x.shape[1:]
    own = tiles // CORES
    listed = far.shape[1]
    padded = -(-(own + 2 * listed + 1) // 8) * 8
    return pl.pallas_call(
        functools.partial(pair_kernel, gain),
        out_shape=shape(3, own, lanes),
        in_specs=smem(3) + vmem(4),
        out_specs=vmem(1)[0],
        scratch_shapes=[
            pltpu.VMEM((4, padded, lanes), f32),
            pltpu.VMEM((padded, DEPTH, lanes), f32),
            pltpu.VMEM((padded, ROWS, lanes), f32),
        ],
        name="pair",
    )(pairs, lists, core, x, charge, far, left)


def swap_cores(value):
    return lax.ppermute(value, "core", [(0, 1), (1, 0)])


def both_cores(mine, theirs, core):
    first = jnp.where(core == 0, mine, theirs)
    second = jnp.where(core == 0, theirs, mine)
    return jnp.concatenate([first, second], 1)


def local(
    positions,
    velocities,
    charge,
    inverse_mass,
    pair_tiles,
    halo_tiles,
    owners,
    centres,
    widths,
    map_density,
    map_error,
    partner,
    decision,
):
    replicas = lax.axis_size("rep")
    heights = lax.axis_size("z")
    domains = heights * CORES
    tile_count, owned = owners.shape
    lanes = positions.shape[2] // tile_count
    components = widths.shape[0]
    half = components // CORES
    core = lax.axis_index("core")
    core_id = core.astype(jnp.int32).reshape(1)
    ids = jnp.arange(replicas, dtype=jnp.int32)
    source = jnp.where(decision == 1, partner, ids)
    mine = source[lax.axis_index("rep")]

    packed = jnp.concatenate(
        [positions[0], velocities[0], charge[None, :], inverse_mass[None, :]], 0
    )
    spread = lax.all_to_all(
        jnp.broadcast_to(packed[None], (replicas,) + packed.shape), "rep", 0, 0, tiled=True
    )
    comp_rows = jnp.stack(
        [centres[0], centres[1], centres[2], widths, map_density, map_error], 0
    )
    comp_send = comp_rows.reshape(6, CORES, half).transpose(1, 0, 2)
    comp_send = jnp.broadcast_to(comp_send[None], (heights, CORES, 6, half)).reshape(
        domains, 6, half
    )
    comps = lax.all_to_all(comp_send, ("z", "core"), 0, 0, tiled=True)
    ints = jnp.concatenate([owners.reshape(-1), halo_tiles.reshape(-1)])
    other_ints = swap_cores(ints)
    count = tile_count * owned
    other_lists = lax.dynamic_index_in_dim(
        other_ints[count:].reshape(halo_tiles.shape[1:]), core, 0, False
    )
    own_list = lax.dynamic_index_in_dim(halo_tiles[0], core, 0, False)
    owners_all = both_cores(ints[None, :count], other_ints[None, :count], core)[0]
    pairs = pair_tiles.reshape(-1)

    state = lax.dynamic_index_in_dim(spread, mine, 0, False)
    other_state = swap_cores(state)
    state = state.reshape(8, tile_count, lanes)
    other_state = other_state.reshape(8, tile_count, lanes)
    full = both_cores(state, other_state, core)
    x, v = full[:3], full[3:6]
    charges, inverse = full[6], full[7]

    map_gain = map_scale / (owned * components)
    scale = 1.0 / (owned * tile_count * lanes)
    pair_gain = (pair_tiles.shape[1] * lanes) ** (-0.5)
    group = replicas * heights
    one_phase = group * domains * half * 4 <= ONE_PHASE_BYTES
    across = [(2 * i + 1, (2 * i + 2) % domains) for i in range(heights)]
    across += [(b, a) for a, b in across]
    base = core * tile_count
    mean = None
    for _ in range(STEPS):
        partial, left, right = intersect(owners_all, x, comps, group if one_phase else 1, scale)
        if one_phase:
            sums = lax.all_to_all(partial, ("rep", "z"), 0, 0, tiled=True)
        else:
            pieces = lax.all_to_all(
                partial.reshape(group, -1), ("rep", "z"), 0, 0, tiled=True
            )
            piece = jnp.sum(pieces, 0)
            sums = lax.all_to_all(
                jnp.broadcast_to(piece[None], (group,) + piece.shape), ("rep", "z"), 0, 0, tiled=True
            ).reshape(1, domains, half)
        own_x = lax.dynamic_slice_in_dim(x, base, tile_count, 1)
        own_q = lax.dynamic_slice_in_dim(charges, base, tile_count, 0)
        rim = jnp.concatenate([own_x, own_q[None]], 0)
        rim = jnp.concatenate(
            [
                lax.dynamic_index_in_dim(rim, own_list[k], 1, True)
                for k in range(own_list.shape[0])
            ],
            1,
        )
        far = lax.ppermute(rim, ("z", "core"), across)
        pair = pair_push(pairs, other_lists, core_id, x, charges, far, left, pair_gain)
        force, mean = push(
            owners_all, core_id, x, comps, sums, left, right, pair, map_gain, float(replicas)
        )
        force = force + swap_cores(force)
        v = v + time_step * inverse[None] * force
        x = x + time_step * v

    new_x = lax.dynamic_slice_in_dim(x, base, tile_count, 1).reshape(1, 3, tile_count * lanes)
    new_v = lax.dynamic_slice_in_dim(v, base, tile_count, 1).reshape(1, 3, tile_count * lanes)
    here = lax.axis_index("z") * CORES
    pair_means = lax.dynamic_slice_in_dim(mean, here, CORES, 0)
    keep = lax.dynamic_index_in_dim(pair_means, core, 0, False)
    give = lax.dynamic_index_in_dim(pair_means, 1 - core, 0, False)
    got = swap_cores(give)
    model_map = jnp.where(
        core == 0, jnp.concatenate([keep, got]), jnp.concatenate([got, keep])
    )
    return (new_x, new_v, model_map)


def solution(mesh):
    replicas, domains = mesh.devices.shape
    split = Mesh(
        mesh.devices.reshape(replicas, domains // CORES, CORES), ("rep", "z", "core")
    )
    dom = ("z", "core")
    placed = (
        P("rep", None, dom),
        P("rep", None, dom),
        P(dom),
        P(dom),
        P(dom, None),
        P(dom, None, None),
        P(dom, None),
        P(None, dom),
        P(dom),
        P(dom),
        P(dom),
        P(),
        P(),
    )
    return jax.shard_map(
        local,
        mesh=split,
        in_specs=placed,
        out_specs=(P("rep", None, dom), P("rep", None, dom), P(dom)),
        check_vma=False,
    )
```

```python
import functools
import math

import jax
import jax.numpy as jnp
from jax import lax
from jax.experimental import pallas as pl
from jax.experimental.pallas import tpu as pltpu
from jax.sharding import Mesh, PartitionSpec as P

STEPS = 2
CORES = 2
DEPTH = 32
ROWS = 16
ONE_PHASE_BYTES = 1 << 20

time_step = 0.5
pair_width = 1.0
map_scale = 2.0
log2e = math.log2(math.e)
f32 = jnp.float32
bf16 = jnp.bfloat16

LEFT_PARTS = (0, 0, 1, 1, 0, 2)
RIGHT_PARTS = (0, 1, 0, 1, 2, 0)


def split3(value):
    high = value.astype(bf16).astype(f32)
    rest = value - high
    middle = rest.astype(bf16).astype(f32)
    return high, middle, rest - middle


def point_rows(coords):
    rows = []
    for coord in coords:
        parts = split3(coord)
        rows += [parts[i] for i in LEFT_PARTS]
    parts = split3(coords[0] * coords[0] + coords[1] * coords[1] + coords[2] * coords[2])
    rows += [parts[i] for i in LEFT_PARTS]
    one = jnp.ones_like(coords[0])
    return rows + [one, one, one]


def centre_rows(coords, extent):
    scale = log2e / extent
    rows = []
    for coord in coords:
        parts = split3(coord * scale)
        rows += [parts[i] for i in RIGHT_PARTS]
    parts = split3(-0.5 * scale)
    rows += [parts[i] for i in RIGHT_PARTS]
    square = coords[0] * coords[0] + coords[1] * coords[1] + coords[2] * coords[2]
    return rows + list(split3(-0.5 * scale * square))


def pull_rows(coords, weight):
    rows = list(split3(weight))
    for coord in coords:
        rows += list(split3(coord * weight))
    return rows


def squeeze_sums(coords, sums):
    def total(first):
        return sums[first : first + 1] + sums[first + 1 : first + 2] + sums[first + 2 : first + 3]

    strength = total(0)
    return [coords[i] * strength - total(3 + 3 * i) for i in range(3)]


def dot(left, right):
    return jnp.dot(left, right, preferred_element_type=f32)


def high_low(value):
    high = value.astype(bf16)
    return high, (value - high.astype(f32)).astype(bf16)


def store_rows(ref, rows):
    for index, row in enumerate(rows):
        ref[:, index, :] = row
    depth = ref.shape[1]
    if len(rows) < depth:
        ref[:, len(rows) : depth, :] = jnp.zeros(
            (ref.shape[0], depth - len(rows), ref.shape[2]), f32
        )


def chunks(total, wanted):
    size = wanted if total % wanted == 0 else total
    return [(start, size) for start in range(0, total, size)]


def pack_kernel(pos_hbm, vel_hbm, charge_hbm, mass_hbm, centre_hbm, width_hbm, density_hbm,
                error_hbm, state_ref, comp_ref, pos_ref, vel_ref, charge_ref, mass_ref, centre_ref,
                width_ref, density_ref, error_ref, sems):
    sources = (pos_hbm, vel_hbm, charge_hbm, mass_hbm, centre_hbm, width_hbm, density_hbm, error_hbm)
    targets = (pos_ref, vel_ref, charge_ref, mass_ref, centre_ref, width_ref, density_ref, error_ref)
    copies = [
        pltpu.make_async_copy(source, target, sems.at[n])
        for n, (source, target) in enumerate(zip(sources, targets))
    ]
    for copy in copies:
        copy.start()
    for copy in copies:
        copy.wait()
    half = comp_ref.shape[2]
    for row in range(state_ref.shape[0]):
        for i in range(3):
            state_ref[row, i : i + 1, :] = pos_ref[i]
            state_ref[row, 3 + i : 4 + i, :] = vel_ref[i]
        state_ref[row, 6:7, :] = charge_ref[...]
        state_ref[row, 7:8, :] = mass_ref[...]
    for row in range(comp_ref.shape[0]):
        part = pl.ds((row % CORES) * half, half)
        comp_ref[row, 0:3, :] = centre_ref[:, part]
        comp_ref[row, 3:4, :] = width_ref[:, part]
        comp_ref[row, 4:5, :] = density_ref[:, part]
        comp_ref[row, 5:6, :] = error_ref[:, part]


def owner_of(plan, mine_ref, theirs_ref, tile, j):
    row = lax.rem(tile, plan.own)
    here = lax.div(tile, plan.own) == lax.axis_index("core")
    return jnp.where(here, mine_ref[row, j], theirs_ref[row, j])


def sum_gaussians(plan, scale, mine_ref, theirs_ref, halo_ref, state_ref, right_ref, points_ref,
                  out_ref, xs, acc, rim):
    tiles, owned, listed = plan.tiles, plan.owned, plan.listed
    store_rows(xs, point_rows([state_ref[i] for i in range(3)]))
    core = lax.axis_index("core")
    for k in range(listed):
        tile = (1 - core) * plan.own + halo_ref[0, 1 - core, k]
        for i, row in enumerate((0, 1, 2, 6)):
            rim[i * listed + k : i * listed + k + 1, :] = state_ref[row, pl.ds(tile, 1), :]
    acc[...] = jnp.zeros_like(acc)

    def one_tile(tile, carry):
        points = xs[tile]
        points_ref[tile] = points.astype(bf16)
        left = points.T.astype(bf16)
        for j in range(owned):
            owner = owner_of(plan, mine_ref, theirs_ref, tile, j)
            for start, size in chunks(right_ref.shape[2], 256):
                g = jnp.exp2(dot(left, right_ref[owner, :, start : start + size]))
                acc[owner, :, start : start + size] += jnp.sum(
                    g.reshape(g.shape[0] // 8, 8, size), 0
                )
        return carry

    lax.fori_loop(0, tiles, one_tile, 0)
    total = jnp.sum(acc[...], 1) * scale
    for row in range(out_ref.shape[0]):
        out_ref[row, 0 : acc.shape[0], 0 : plan.half] = total
        out_ref[row, 0 : rim.shape[0], plan.half :] = rim[...]


def first_kernel(plan, scale, mine_ref, theirs_ref, halo_ref, partner_ref, decision_ref, spread_ref, comp_ref,
                 out_ref, state_ref, points_ref, right_ref, xs, acc, rim, cs):
    store_rows(cs, centre_rows([comp_ref[:, i, :] for i in range(3)], comp_ref[:, 3, :]))
    right_ref[...] = cs[...].astype(bf16)
    row = lax.axis_index("rep")
    source = jnp.where(decision_ref[row] == 1, partner_ref[row], row)
    for core in range(CORES):
        for tile in range(plan.own):
            lanes = slice(tile * plan.lanes, (tile + 1) * plan.lanes)
            state_ref[:, core * plan.own + tile, :] = spread_ref[source * CORES + core, :, lanes]
    sum_gaussians(plan, scale, mine_ref, theirs_ref, halo_ref, state_ref, right_ref, points_ref,
                  out_ref, xs, acc, rim)


def stepped(old_ref, mine_ref, theirs_ref):
    mass = time_step * old_ref[7]
    for i in range(3):
        v = old_ref[3 + i] + mass * (mine_ref[i] + theirs_ref[i])
        yield old_ref[i] + time_step * v, v


def next_kernel(plan, scale, mine_ref, theirs_ref, halo_ref, old_ref, force_ref, swapped_ref, right_ref,
                out_ref, state_ref, points_ref, xs, acc, rim):
    for i, (x, v) in enumerate(stepped(old_ref, force_ref, swapped_ref)):
        state_ref[i] = x
        state_ref[3 + i] = v
    state_ref[6] = old_ref[6]
    state_ref[7] = old_ref[7]
    sum_gaussians(plan, scale, mine_ref, theirs_ref, halo_ref, state_ref, right_ref, points_ref,
                  out_ref, xs, acc, rim)


def finish_kernel(plan, old_ref, mine_ref, theirs_ref, x_ref, v_ref, map_ref, state):
    for i, (x, v) in enumerate(stepped(old_ref, mine_ref, theirs_ref)):
        state[i] = x
        state[3 + i] = v
    core = lax.axis_index("core")
    base = core * plan.own
    for tile in range(plan.own):
        lanes = slice(tile * plan.lanes, (tile + 1) * plan.lanes)
        for i in range(3):
            x_ref[i, :, lanes] = state[i, pl.ds(base + tile, 1), :]
            v_ref[i, :, lanes] = state[3 + i, pl.ds(base + tile, 1), :]
    first = core == 0
    pieces = plan.half // plan.lanes
    for n in range(pieces):
        keep = mine_ref[3, n : n + 1, :]
        got = theirs_ref[3, pieces + n : pieces + n + 1, :]
        low = slice(n * plan.lanes, (n + 1) * plan.lanes)
        high = slice(plan.half + n * plan.lanes, plan.half + (n + 1) * plan.lanes)
        map_ref[:, low] = jnp.where(first, keep, got)
        map_ref[:, high] = jnp.where(first, got, keep)


def fill_kernel(plan, gain, mine_ref, theirs_ref, pairs_ref, halo_ref, state_ref, points_ref, right_ref,
                high_ref, low_ref, pair_ref, turned, table, cs, rs, near_turned, high, low, sems):
    for domain in range(right_ref.shape[0]):
        for start, size in chunks(right_ref.shape[2], 128):
            turned[domain, start : start + size, :] = (
                right_ref[domain, :, start : start + size].astype(f32).T.astype(bf16)
            )

    def leave(tile, part, kept, out):
        blocks = pl.ds(tile * plan.owned, plan.owned)
        return pltpu.make_async_copy(kept.at[blocks], out.at[blocks], sems.at[part, tile])

    def one_tile(tile, carry):
        points = points_ref[tile]
        for j in range(plan.owned):
            block = tile * plan.owned + j
            owner = owner_of(plan, mine_ref, theirs_ref, tile, j)
            for start, size in chunks(turned.shape[1], 256):
                rows = slice(start, start + size)
                g = jnp.exp2(dot(turned[owner, rows, :], points))
                high[block, rows, :], low[block, rows, :] = high_low(g)
        leave(tile, 0, high, high_ref).start()
        leave(tile, 1, low, low_ref).start()
        return carry

    lax.fori_loop(0, plan.tiles, one_tile, 0)
    pair_pushes(plan, gain, pairs_ref, halo_ref, state_ref, points_ref, pair_ref, table, cs, rs, near_turned)

    def settle(tile, carry):
        leave(tile, 0, high, high_ref).wait()
        leave(tile, 1, low, low_ref).wait()
        return carry

    lax.fori_loop(0, plan.tiles, settle, 0)


def pair_pushes(plan, gain, pairs_ref, halo_ref, state_ref, points_ref, out_ref, table, cs, rs, turned):
    own, near, listed = plan.own, plan.near, plan.listed
    core = lax.axis_index("core")
    base = pl.multiple_of(core * own, own)
    extent = own + 2 * listed
    table[...] = jnp.zeros_like(table)
    for i, source in enumerate((0, 1, 2, 6)):
        table[i, 0:own, :] = state_ref[source, pl.ds(base, own), :]
        for k in range(listed):
            listed_tile = (1 - core) * own + halo_ref[0, core, k]
            table[i, pl.ds(own + (1 - core) * listed + k, 1), :] = state_ref[
                source, pl.ds(listed_tile, 1), :
            ]
    coords = [table[i] for i in range(3)]
    store_rows(cs, centre_rows(coords, jnp.full_like(coords[0], pair_width)))
    store_rows(rs, pull_rows(coords, table[3]))
    for entry in range(table.shape[1]):
        turned[entry] = cs[entry].T.astype(bf16)
    for tile in range(own):
        points = points_ref[base + tile]
        sums = jnp.zeros((ROWS, plan.lanes), f32)
        for j in range(near):
            entry = pairs_ref[tile, j]
            entry = jnp.where(entry < 0, extent, entry)
            rows = rs[entry].astype(bf16)
            high, low = high_low(jnp.exp2(dot(turned[entry], points)))
            sums += dot(rows, high) + dot(rows, low)
        coords = [state_ref[i, pl.ds(base + tile, 1), :] for i in range(3)]
        strength = gain / pair_width * state_ref[6, pl.ds(base + tile, 1), :]
        for i, push in enumerate(squeeze_sums(coords, sums)):
            out_ref[i, tile : tile + 1, :] = strength * push


def far_pushes(plan, gain, pairs_ref, state_ref, far, points_ref, out_ref, cs, rs):
    own, near, listed = plan.own, plan.near, plan.listed
    core = lax.axis_index("core")
    base = core * own
    coords = [far[i * listed : (i + 1) * listed] for i in range(3)]
    store_rows(cs, centre_rows(coords, jnp.full_like(coords[0], pair_width)))
    store_rows(rs, pull_rows(coords, far[3 * listed : 4 * listed]))
    turned = [cs[k].T.astype(bf16) for k in range(listed)]
    for tile in range(own):
        points = points_ref[base + tile]
        sums = jnp.zeros((ROWS, plan.lanes), f32)
        for k in range(listed):
            entry = own + core * listed + k
            named = pairs_ref[tile, 0] == entry
            for j in range(1, near):
                named = named | (pairs_ref[tile, j] == entry)
            rows = (rs[k] * jnp.where(named, 1.0, 0.0)).astype(bf16)
            high, low = high_low(jnp.exp2(dot(turned[k], points)))
            sums += dot(rows, high) + dot(rows, low)
        coords = [state_ref[i, pl.ds(base + tile, 1), :] for i in range(3)]
        strength = gain / pair_width * state_ref[6, pl.ds(base + tile, 1), :]
        for i, push in enumerate(squeeze_sums(coords, sums)):
            out_ref[i, pl.ds(base + tile, 1), :] += strength * push


def push_kernel(plan, gain, pair_gain, replicas, mine_ref, theirs_ref, pairs_ref, state_ref, comp_ref,
                sums_ref, far_ref, pair_ref, points_ref, high_ref, low_ref, out_ref, rs, means, far_cs, far_rs,
                high, low, sems):
    def bring(tile, part, source, kept):
        blocks = pl.ds(tile * plan.owned, plan.owned)
        return pltpu.make_async_copy(source.at[blocks], kept.at[blocks], sems.at[part, tile])

    def fetch(tile, carry):
        bring(tile, 0, high_ref, high).start()
        bring(tile, 1, low_ref, low).start()
        return carry

    lax.fori_loop(0, plan.tiles, fetch, 0)
    domains = comp_ref.shape[0]
    mean = jnp.sum(sums_ref[:, 0:domains, 0 : plan.half], 0) / replicas
    for n in range(plan.half // plan.lanes):
        means[n] = mean[:, n * plan.lanes : (n + 1) * plan.lanes]
    error = comp_ref[:, 5, :]
    coefficient = gain * (mean - comp_ref[:, 4, :]) / (error * error) / comp_ref[:, 3, :]
    store_rows(rs, pull_rows([comp_ref[:, i, :] for i in range(3)], coefficient))

    def one_tile(tile, carry):
        bring(tile, 0, high_ref, high).wait()
        bring(tile, 1, low_ref, low).wait()
        sums = jnp.zeros((ROWS, plan.lanes), f32)
        for j in range(plan.owned):
            block = tile * plan.owned + j
            rows = rs[owner_of(plan, mine_ref, theirs_ref, tile, j)].astype(bf16)
            sums += dot(rows, high[block]) + dot(rows, low[block])
        coords = [state_ref[i, pl.ds(tile, 1), :] for i in range(3)]
        for i, push in enumerate(squeeze_sums(coords, sums)):
            out_ref[i, pl.ds(tile, 1), :] = push
        return carry

    lax.fori_loop(0, plan.tiles, one_tile, 0)
    for core in range(CORES):

        @pl.when(lax.axis_index("core") == core)
        def _():
            out_ref[0:3, core * plan.own : (core + 1) * plan.own, :] += pair_ref[...]

    far_rows = 4 * plan.listed
    if plan.one_phase:
        heights = lax.axis_size("z")
        turn = jnp.where(lax.axis_index("core") == 0, heights - 1, 1)
        row = lax.axis_index("rep") * heights + lax.rem(lax.axis_index("z") + turn, heights)
        far = far_ref[row, 0:far_rows, plan.half :]
    else:
        far = far_ref[0, 0:far_rows, plan.half :]
    far_pushes(plan, pair_gain, pairs_ref, state_ref, far, points_ref, out_ref, far_cs, far_rs)

    pieces = plan.half // plan.lanes
    core = lax.axis_index("core")
    here = lax.axis_index("z") * CORES
    out_ref[3] = jnp.zeros_like(out_ref[3])
    for n in range(pieces):
        keep = means[n, pl.ds(here + core, 1), :]
        give = means[n, pl.ds(here + 1 - core, 1), :]
        out_ref[3, n : n + 1, :] = keep
        out_ref[3, pieces + n : pieces + n + 1, :] = give


VMEM = pl.BlockSpec(memory_space=pltpu.VMEM)
SMEM = pl.BlockSpec(memory_space=pltpu.SMEM)
HBM = pl.BlockSpec(memory_space=pltpu.HBM)


def shape(*dims, dtype=f32):
    return jax.ShapeDtypeStruct(dims, dtype)


def with_types(scratch):
    for entry in scratch:
        if not isinstance(entry, tuple):
            yield entry
        else:
            dims, dtype = entry if isinstance(entry[0], tuple) else (entry, f32)
            yield pltpu.VMEM(dims, dtype)


def call(name, kernel, lists, args, outs, scratch=(), limit=12, spaces=None, out_spaces=None):
    many = isinstance(outs, (list, tuple))
    return pl.pallas_call(
        kernel,
        out_shape=tuple(outs) if many else outs,
        in_specs=[SMEM] * len(lists) + (spaces or [VMEM] * len(args)),
        out_specs=tuple(out_spaces or [VMEM] * len(outs)) if many else VMEM,
        scratch_shapes=list(with_types(scratch)),
        compiler_params=pltpu.CompilerParams(vmem_limit_bytes=limit and limit << 20),
        name=name,
    )(*lists, *args)


class Plan:
    pass


def swap_cores(value):
    return lax.ppermute(value, "core", [(0, 1), (1, 0)])


def local(
    positions,
    velocities,
    charge,
    inverse_mass,
    pair_tiles,
    halo_tiles,
    owners,
    centres,
    widths,
    map_density,
    map_error,
    partner,
    decision,
):
    replicas = lax.axis_size("rep")
    heights = lax.axis_size("z")
    domains = heights * CORES
    own, owned = owners.shape
    plan = Plan()
    plan.own, plan.owned, plan.tiles = own, owned, own * CORES
    plan.lanes = positions.shape[2] // own
    plan.near, plan.listed = pair_tiles.shape[1], halo_tiles.shape[2]
    components = widths.shape[0]
    half = plan.half = components // CORES
    tiles, lanes, listed = plan.tiles, plan.lanes, plan.listed

    args = [
        positions.transpose(1, 0, 2),
        velocities.transpose(1, 0, 2),
        charge[None],
        inverse_mass[None],
        centres,
        widths[None],
        map_density[None],
        map_error[None],
    ]
    state_send, comp_send = call(
        "pack",
        pack_kernel,
        [],
        args,
        [shape(replicas * CORES, 8, own * lanes), shape(domains, 6, half)],
        [(arg.shape, f32) for arg in args] + [pltpu.SemaphoreType.DMA((len(args),))],
        limit=None,
        spaces=[HBM] * len(args),
    )
    other_owners, other_halo = swap_cores(owners), swap_cores(halo_tiles)
    both = [owners, other_owners]
    spread = lax.all_to_all(state_send, ("rep", "core"), 0, 0, tiled=True)
    comps = lax.all_to_all(comp_send, ("z", "core"), 0, 0, tiled=True)

    map_gain = map_scale / (owned * components)
    scale = 1.0 / (owned * own * lanes)
    pair_gain = (plan.near * lanes) ** (-0.5)
    group = replicas * heights
    plan.one_phase = group * domains * half * 4 <= ONE_PHASE_BYTES
    copies = group if plan.one_phase else 1
    rim_rows = -(-4 * listed // 8) * 8
    onward = [(2 * i, (2 * i + 2) % domains) for i in range(heights)]
    onward += [((2 * i + 3) % domains, 2 * i + 1) for i in range(heights)]
    padded = -(-(own + 2 * listed + 1) // 8) * 8
    outs = [
        shape(copies, max(domains, rim_rows), half + lanes),
        shape(8, tiles, lanes),
        shape(tiles, DEPTH, lanes, dtype=bf16),
    ]
    scratch = [(tiles, DEPTH, lanes), (domains, 8, half), (rim_rows, lanes)]
    kept = [((tiles * owned, half, lanes), bf16)] * 2 + [pltpu.SemaphoreType.DMA((2, tiles))]
    for step in range(STEPS):
        if step == 0:
            partial, state, points, right = call(
                "first",
                functools.partial(first_kernel, plan, scale),
                both + [other_halo, partner, decision],
                [spread, comps],
                outs + [shape(domains, DEPTH, half, dtype=bf16)],
                scratch + [(domains, DEPTH, half)],
            )
        else:
            partial, state, points = call(
                "next",
                functools.partial(next_kernel, plan, scale),
                both + [other_halo],
                [state, force, swapped, right],
                outs,
                scratch,
            )
        if plan.one_phase:
            sums = far = lax.all_to_all(partial, ("rep", "z"), 0, 0, tiled=True)
        else:
            far = lax.ppermute(partial, ("z", "core"), onward)
            pieces = lax.all_to_all(
                partial[0, :domains, :half].reshape(group, -1), ("rep", "z"), 0, 0, tiled=True
            )
            piece = jnp.sum(pieces, 0)
            sums = lax.all_to_all(
                jnp.broadcast_to(piece[None], (group,) + piece.shape), ("rep", "z"), 0, 0, tiled=True
            ).reshape(1, domains, half)
        high, low, pair = call(
            "fill",
            functools.partial(fill_kernel, plan, pair_gain),
            both + [pair_tiles, other_halo],
            [state, points, right],
            [shape(tiles * owned, half, lanes, dtype=bf16)] * 2 + [shape(3, own, lanes)],
            [((domains, half, DEPTH), bf16), (4, padded, lanes), (padded, DEPTH, lanes),
             (padded, ROWS, lanes), ((padded, lanes, DEPTH), bf16)] + kept,
            limit=56,
            out_spaces=[HBM, HBM, VMEM],
        )
        force = call(
            "push",
            functools.partial(push_kernel, plan, map_gain, pair_gain, float(replicas)),
            both + [pair_tiles],
            [state, comps, sums, far, pair, points, high, low],
            shape(4, tiles, lanes),
            [(domains, ROWS, half), (half // lanes, domains, lanes), (listed, DEPTH, lanes),
             (listed, ROWS, lanes)] + kept,
            limit=56,
            spaces=[VMEM] * 6 + [HBM, HBM],
        )
        swapped = swap_cores(force)

    new_x, new_v, model_map = call(
        "finish",
        functools.partial(finish_kernel, plan),
        [],
        [state, force, swapped],
        [shape(3, 1, own * lanes), shape(3, 1, own * lanes), shape(1, components)],
        [(6, tiles, lanes)],
    )
    return (new_x.transpose(1, 0, 2), new_v.transpose(1, 0, 2), model_map.reshape(components))


def solution(mesh):
    replicas, domains = mesh.devices.shape
    split = Mesh(
        mesh.devices.reshape(replicas, domains // CORES, CORES), ("rep", "z", "core")
    )
    dom = ("z", "core")
    placed = (
        P("rep", None, dom),
        P("rep", None, dom),
        P(dom),
        P(dom),
        P(dom, None),
        P(dom, None, None),
        P(dom, None),
        P(None, dom),
        P(dom),
        P(dom),
        P(dom),
        P(),
        P(),
    )
    return jax.shard_map(
        local,
        mesh=split,
        in_specs=placed,
        out_specs=(P("rep", None, dom), P("rep", None, dom), P(dom)),
        check_vma=False,
    )
```

```python
import functools
import math

import jax
import jax.numpy as jnp
from jax import lax
from jax.experimental import pallas as pl
from jax.experimental.pallas import tpu as pltpu
from jax.sharding import Mesh, PartitionSpec as P

STEPS = 2
CORES = 2
DEPTH = 32
ROWS = 16
ONE_PHASE_BYTES = 1 << 20
UNROLL = 2
FAR_SQUARE = 1048576.0

time_step = 0.5
pair_width = 1.0
map_scale = 2.0
log2e = math.log2(math.e)
f32 = jnp.float32
bf16 = jnp.bfloat16

LEFT_PARTS = (0, 0, 1, 1, 0, 2)
RIGHT_PARTS = (0, 1, 0, 1, 2, 0)


def split3(value):
    high = value.astype(bf16).astype(f32)
    rest = value - high
    middle = rest.astype(bf16).astype(f32)
    return high, middle, rest - middle


def point_rows(coords):
    rows = []
    for coord in coords:
        parts = split3(coord)
        rows += [parts[i] for i in LEFT_PARTS]
    parts = split3(coords[0] * coords[0] + coords[1] * coords[1] + coords[2] * coords[2])
    rows += [parts[i] for i in LEFT_PARTS]
    one = jnp.ones_like(coords[0])
    return rows + [one, one, one]


def nowhere(ref, tile):
    shape = ref.shape[1:]
    row = lax.broadcasted_iota(jnp.int32, shape, 0)
    square = len(LEFT_PARTS) * 3
    ref[tile] = jnp.where(row == square, FAR_SQUARE, 0.0)


def centre_rows(coords, extent):
    scale = log2e / extent
    rows = []
    for coord in coords:
        parts = split3(coord * scale)
        rows += [parts[i] for i in RIGHT_PARTS]
    parts = split3(-0.5 * scale)
    rows += [parts[i] for i in RIGHT_PARTS]
    square = coords[0] * coords[0] + coords[1] * coords[1] + coords[2] * coords[2]
    return rows + list(split3(-0.5 * scale * square))


def pull_rows(coords, weight):
    rows = list(split3(weight))
    for coord in coords:
        rows += list(split3(coord * weight))
    return rows


def squeeze_sums(coords, sums):
    def total(first):
        return sums[first : first + 1] + sums[first + 1 : first + 2] + sums[first + 2 : first + 3]

    strength = total(0)
    return [coords[i] * strength - total(3 + 3 * i) for i in range(3)]


def dot(left, right):
    return jnp.dot(left, right, preferred_element_type=f32)


def high_low(value):
    high = value.astype(bf16)
    return high, (value - high.astype(f32)).astype(bf16)


def store_rows(ref, rows):
    count, depth, width = rows[0].shape[0], ref.shape[1], ref.shape[2]
    for index, row in enumerate(rows):
        ref[0:count, index, :] = row
    if len(rows) < depth:
        ref[0:count, len(rows) : depth, :] = jnp.zeros((count, depth - len(rows), width), f32)


def chunks(total, wanted):
    size = wanted if total % wanted == 0 else total
    return [(start, size) for start in range(0, total, size)]


def pack_kernel(pos_hbm, vel_hbm, charge_hbm, mass_hbm, centre_hbm, width_hbm, density_hbm,
                error_hbm, owners_hbm, halo_hbm, state_ref, comp_ref, ints_ref, pos_ref, vel_ref,
                charge_ref, mass_ref, centre_ref, width_ref, density_ref, error_ref, owners_ref,
                halo_ref, sems):
    sources = (pos_hbm, vel_hbm, charge_hbm, mass_hbm, centre_hbm, width_hbm, density_hbm,
               error_hbm, owners_hbm, halo_hbm)
    targets = (pos_ref, vel_ref, charge_ref, mass_ref, centre_ref, width_ref, density_ref,
               error_ref, owners_ref, halo_ref)
    copies = [
        pltpu.make_async_copy(source, target, sems.at[n])
        for n, (source, target) in enumerate(zip(sources, targets))
    ]
    for copy in copies:
        copy.start()
    for copy in copies:
        copy.wait()
    half = comp_ref.shape[2]
    for i in range(3):
        state_ref[i : i + 1, :] = pos_ref[i]
        state_ref[3 + i : 4 + i, :] = vel_ref[i]
    state_ref[6:7, :] = charge_ref[...]
    state_ref[7:8, :] = mass_ref[...]
    own, owned = owners_ref.shape
    _, sides, listed = halo_ref.shape
    ints_ref[...] = jnp.zeros_like(ints_ref)
    ints_ref[0:own, 0:owned] = owners_ref[...]
    ints_ref[own : own + sides, 0:listed] = halo_ref[0]
    for row in range(comp_ref.shape[0]):
        part = pl.ds((row % CORES) * half, half)
        comp_ref[row, 0:3, :] = centre_ref[:, part]
        comp_ref[row, 3:4, :] = width_ref[:, part]
        comp_ref[row, 4:5, :] = density_ref[:, part]
        comp_ref[row, 5:6, :] = error_ref[:, part]


def choose_kernel(partner_ref, decision_ref, mine_ref, *refs):
    others, out_ref = refs[:-1], refs[-1]
    row = lax.axis_index("rep")
    source = jnp.where(decision_ref[row] == 1, partner_ref[row], row)
    if len(others) == 1:
        out_ref[...] = others[0][source]
        return
    out_ref[...] = mine_ref[...]
    for n, other_ref in enumerate(others):

        @pl.when(source == (row ^ (n + 1)))
        def _():
            out_ref[...] = other_ref[...]


def list_kernel(plan, mine_ref, theirs_ref, pairs_ref, out_ref, waiting):
    core = lax.axis_index("core")

    def clear(domain, carry):
        waiting[domain] = -1
        return carry

    lax.fori_loop(0, plan.domains, clear, 0)

    def one_tile(tile, count):
        row = lax.rem(tile, plan.own)
        here = lax.div(tile, plan.own) == core
        for j in range(plan.owned):
            owner = jnp.where(here, mine_ref[row, j], theirs_ref[row, j])
            first = waiting[owner]
            out_ref[0, count] = owner
            out_ref[1, count] = first
            out_ref[2, count] = tile
            count = count + jnp.where(first < 0, 0, 1)
            waiting[owner] = jnp.where(first < 0, tile, -1)
        return count

    count = lax.fori_loop(0, plan.tiles, one_tile, 0)

    def leftover(domain, count):
        first = waiting[domain]
        out_ref[0, count] = domain
        out_ref[1, count] = first
        out_ref[2, count] = plan.tiles
        return count + jnp.where(first < 0, 0, 1)

    count = lax.fori_loop(0, plan.domains, leftover, count)
    for extra in range(UNROLL - 1):
        out_ref[0, count + extra] = 0
        out_ref[1, count + extra] = plan.tiles
        out_ref[2, count + extra] = plan.tiles
    out_ref[3, 0] = lax.div(count + UNROLL - 1, UNROLL)
    for side in range(2):
        for k in range(plan.listed):
            out_ref[3, 1 + side * plan.listed + k] = theirs_ref[plan.own + side, k]
    for tile in range(plan.own):
        for j in range(plan.near):
            out_ref[4 + j, tile] = pairs_ref[tile, j]


def partner_tile(plan, lists_ref, side, k):
    core = lax.axis_index("core")
    return (1 - core) * plan.own + lists_ref[3, 1 + side * plan.listed + k]


def for_pairs(lists_ref, body):
    def step(n, carry):
        for u in range(UNROLL):
            place = n * UNROLL + u
            body(lists_ref[0, place], lists_ref[1, place], lists_ref[2, place])
        return carry

    lax.fori_loop(0, lists_ref[3, 0], step, 0)


def sum_gaussians(plan, scale, lists_ref, state_ref, right_ref, points_ref, out_ref, xs, acc, rim, left):
    tiles, listed = plan.tiles, plan.listed
    store_rows(xs, point_rows([state_ref[i] for i in range(3)]))
    nowhere(xs, tiles)
    for tile in range(tiles + 1):
        points = xs[tile]
        points_ref[tile] = points.astype(bf16)
        left[tile] = points.T.astype(bf16)
    core = lax.axis_index("core")
    for k in range(listed):
        tile = partner_tile(plan, lists_ref, 1 - core, k)
        for i, row in enumerate((0, 1, 2, 6)):
            rim[i * listed + k : i * listed + k + 1, :] = state_ref[row, pl.ds(tile, 1), :]
    acc[...] = jnp.zeros_like(acc)

    def one_pair(owner, first, second):
        both = jnp.concatenate([left[first], left[second]], 0)
        for start, size in chunks(right_ref.shape[2], 256):
            g = jnp.exp2(dot(both, right_ref[owner, :, start : start + size]))
            acc[owner, :, start : start + size] += jnp.sum(g.reshape(g.shape[0] // 8, 8, size), 0)

    for_pairs(lists_ref, one_pair)
    total = jnp.sum(acc[...], 1) * scale
    for row in range(out_ref.shape[0]):
        out_ref[row, 0 : acc.shape[0], 0 : plan.half] = total
        out_ref[row, 0 : rim.shape[0], plan.half :] = rim[...]


def first_kernel(plan, scale, lists_ref, mine_ref, theirs_ref, comp_ref,
                 out_ref, state_ref, points_ref, right_ref, xs, acc, rim, left, cs):
    core = lax.axis_index("core")
    for tile in range(plan.own):
        lanes = slice(tile * plan.lanes, (tile + 1) * plan.lanes)
        mine, theirs = mine_ref[:, lanes], theirs_ref[:, lanes]
        state_ref[:, tile, :] = jnp.where(core == 0, mine, theirs)
        state_ref[:, plan.own + tile, :] = jnp.where(core == 0, theirs, mine)
    store_rows(cs, centre_rows([comp_ref[:, i, :] for i in range(3)], comp_ref[:, 3, :]))
    right_ref[...] = cs[...].astype(bf16)
    sum_gaussians(plan, scale, lists_ref, state_ref, right_ref, points_ref, out_ref, xs, acc, rim, left)


def stepped(old_ref, mine_ref, theirs_ref):
    mass = time_step * old_ref[7]
    for i in range(3):
        v = old_ref[3 + i] + mass * (mine_ref[i] + theirs_ref[i])
        yield old_ref[i] + time_step * v, v


def next_kernel(plan, scale, lists_ref, old_ref, force_ref, swapped_ref, right_ref,
                out_ref, state_ref, points_ref, xs, acc, rim, left):
    for i, (x, v) in enumerate(stepped(old_ref, force_ref, swapped_ref)):
        state_ref[i] = x
        state_ref[3 + i] = v
    state_ref[6] = old_ref[6]
    state_ref[7] = old_ref[7]
    sum_gaussians(plan, scale, lists_ref, state_ref, right_ref, points_ref, out_ref, xs, acc, rim, left)


def finish_kernel(plan, old_ref, mine_ref, theirs_ref, x_ref, v_ref, map_ref, state):
    for i, (x, v) in enumerate(stepped(old_ref, mine_ref, theirs_ref)):
        state[i] = x
        state[3 + i] = v
    core = lax.axis_index("core")
    base = core * plan.own
    for tile in range(plan.own):
        lanes = slice(tile * plan.lanes, (tile + 1) * plan.lanes)
        for i in range(3):
            x_ref[i, :, lanes] = state[i, pl.ds(base + tile, 1), :]
            v_ref[i, :, lanes] = state[3 + i, pl.ds(base + tile, 1), :]
    first = core == 0
    pieces = plan.half // plan.lanes
    for n in range(pieces):
        keep = mine_ref[3, n : n + 1, :]
        got = theirs_ref[3, pieces + n : pieces + n + 1, :]
        low = slice(n * plan.lanes, (n + 1) * plan.lanes)
        high = slice(plan.half + n * plan.lanes, plan.half + (n + 1) * plan.lanes)
        map_ref[:, low] = jnp.where(first, keep, got)
        map_ref[:, high] = jnp.where(first, got, keep)


def turn_kernel(right_ref, turned_ref):
    for domain in range(right_ref.shape[0]):
        for start, size in chunks(right_ref.shape[2], 128):
            turned_ref[domain, start : start + size, :] = (
                right_ref[domain, :, start : start + size].astype(f32).T.astype(bf16)
            )


def near_kernel(plan, gain, lists_ref, state_ref, points_ref, out_ref, table, cs, rs, turned):
    own, near, listed = plan.own, plan.near, plan.listed
    core = lax.axis_index("core")
    base = pl.multiple_of(core * own, own)
    extent = own + 2 * listed
    table[...] = jnp.zeros_like(table)
    for i, source in enumerate((0, 1, 2, 6)):
        table[i, 0:own, :] = state_ref[source, pl.ds(base, own), :]
        for k in range(listed):
            table[i, pl.ds(own + (1 - core) * listed + k, 1), :] = state_ref[
                source, pl.ds(partner_tile(plan, lists_ref, core, k), 1), :
            ]
    coords = [table[i] for i in range(3)]
    store_rows(cs, centre_rows(coords, jnp.full_like(coords[0], pair_width)))
    store_rows(rs, pull_rows(coords, table[3]))
    for entry in range(table.shape[1]):
        turned[entry] = cs[entry].T.astype(bf16)
    for tile in range(own):
        points = points_ref[base + tile]
        sums = jnp.zeros((ROWS, plan.lanes), f32)
        for j in range(near):
            entry = lists_ref[4 + j, tile]
            entry = jnp.where(entry < 0, extent, entry)
            rows = rs[entry].astype(bf16)
            high, low = high_low(jnp.exp2(dot(turned[entry], points)))
            sums += dot(rows, high) + dot(rows, low)
        coords = [state_ref[i, pl.ds(base + tile, 1), :] for i in range(3)]
        strength = gain / pair_width * state_ref[6, pl.ds(base + tile, 1), :]
        for i, push in enumerate(squeeze_sums(coords, sums)):
            out_ref[i, tile : tile + 1, :] = strength * push


def far_pushes(plan, gain, lists_ref, state_ref, far, points_ref, out_ref, cs, rs):
    own, near, listed = plan.own, plan.near, plan.listed
    core = lax.axis_index("core")
    base = core * own
    coords = [far[i * listed : (i + 1) * listed] for i in range(3)]
    store_rows(cs, centre_rows(coords, jnp.full_like(coords[0], pair_width)))
    store_rows(rs, pull_rows(coords, far[3 * listed : 4 * listed]))
    turned = [cs[k].T.astype(bf16) for k in range(listed)]
    for tile in range(own):
        points = points_ref[base + tile]
        sums = jnp.zeros((ROWS, plan.lanes), f32)
        for k in range(listed):
            entry = own + core * listed + k
            named = lists_ref[4, tile] == entry
            for j in range(1, near):
                named = named | (lists_ref[4 + j, tile] == entry)
            rows = (rs[k] * jnp.where(named, 1.0, 0.0)).astype(bf16)
            high, low = high_low(jnp.exp2(dot(turned[k], points)))
            sums += dot(rows, high) + dot(rows, low)
        coords = [state_ref[i, pl.ds(base + tile, 1), :] for i in range(3)]
        strength = gain / pair_width * state_ref[6, pl.ds(base + tile, 1), :]
        for i, push in enumerate(squeeze_sums(coords, sums)):
            out_ref[i, pl.ds(base + tile, 1), :] += strength * push


def push_kernel(plan, gain, pair_gain, replicas, lists_ref, state_ref, comp_ref, sums_ref, far_ref,
                pair_ref, points_ref, turned_ref, out_ref, rs, rows, means, sums, far_cs, far_rs):
    domains, tiles = comp_ref.shape[0], plan.tiles
    mean = jnp.sum(sums_ref[:, 0:domains, 0 : plan.half], 0) / replicas
    for n in range(plan.half // plan.lanes):
        means[n] = mean[:, n * plan.lanes : (n + 1) * plan.lanes]
    error = comp_ref[:, 5, :]
    coefficient = gain * (mean - comp_ref[:, 4, :]) / (error * error) / comp_ref[:, 3, :]
    store_rows(rs, pull_rows([comp_ref[:, i, :] for i in range(3)], coefficient))
    rows[...] = rs[...].astype(bf16)
    sums[...] = jnp.zeros_like(sums)

    def one_pair(owner, first, second):
        points = jnp.concatenate([points_ref[first], points_ref[second]], 1)
        total = None
        for start, size in chunks(plan.half, 256):
            part = slice(start, start + size)
            high, low = high_low(jnp.exp2(dot(turned_ref[owner, part, :], points)))
            weights = rows[owner, :, part]
            term = dot(weights, high) + dot(weights, low)
            total = term if total is None else total + term
        sums[first] += total[:, : plan.lanes]
        sums[second] += total[:, plan.lanes :]

    for_pairs(lists_ref, one_pair)

    def added(row):
        return sums[0:tiles, row, :] + sums[0:tiles, row + 1, :] + sums[0:tiles, row + 2, :]

    strength = added(0)
    for i in range(3):
        out_ref[i] = state_ref[i] * strength - added(3 + 3 * i)
    for core in range(CORES):

        @pl.when(lax.axis_index("core") == core)
        def _():
            out_ref[0:3, core * plan.own : (core + 1) * plan.own, :] += pair_ref[...]

    far_rows = 4 * plan.listed
    if plan.one_phase:
        heights = lax.axis_size("z")
        turn = jnp.where(lax.axis_index("core") == 0, heights - 1, 1)
        row = lax.axis_index("rep") * heights + lax.rem(lax.axis_index("z") + turn, heights)
        far = far_ref[row, 0:far_rows, plan.half :]
    else:
        far = far_ref[0, 0:far_rows, plan.half :]
    far_pushes(plan, pair_gain, lists_ref, state_ref, far, points_ref, out_ref, far_cs, far_rs)

    pieces = plan.half // plan.lanes
    core = lax.axis_index("core")
    here = lax.axis_index("z") * CORES
    out_ref[3] = jnp.zeros_like(out_ref[3])
    for n in range(pieces):
        keep = means[n, pl.ds(here + core, 1), :]
        give = means[n, pl.ds(here + 1 - core, 1), :]
        out_ref[3, n : n + 1, :] = keep
        out_ref[3, pieces + n : pieces + n + 1, :] = give


VMEM = pl.BlockSpec(memory_space=pltpu.VMEM)
SMEM = pl.BlockSpec(memory_space=pltpu.SMEM)
HBM = pl.BlockSpec(memory_space=pltpu.HBM)


def shape(*dims, dtype=f32):
    return jax.ShapeDtypeStruct(dims, dtype)


def with_types(scratch):
    for entry in scratch:
        if not isinstance(entry, tuple):
            yield entry
        else:
            dims, dtype = entry if isinstance(entry[0], tuple) else (entry, f32)
            yield pltpu.VMEM(dims, dtype)


def call(name, kernel, lists, args, outs, scratch=(), limit=12, spaces=None, out_spaces=None):
    many = isinstance(outs, (list, tuple))
    return pl.pallas_call(
        kernel,
        out_shape=tuple(outs) if many else outs,
        in_specs=[SMEM] * len(lists) + (spaces or [VMEM] * len(args)),
        out_specs=tuple(out_spaces or [VMEM] * len(outs)) if many else (out_spaces or VMEM),
        scratch_shapes=list(with_types(scratch)),
        compiler_params=pltpu.CompilerParams(vmem_limit_bytes=limit and limit << 20),
        name=name,
    )(*lists, *args)


class Plan:
    pass


def swap_cores(value):
    return lax.ppermute(value, "core", [(0, 1), (1, 0)])


def local(
    positions,
    velocities,
    charge,
    inverse_mass,
    pair_tiles,
    halo_tiles,
    owners,
    centres,
    widths,
    map_density,
    map_error,
    partner,
    decision,
):
    replicas = lax.axis_size("rep")
    heights = lax.axis_size("z")
    domains = heights * CORES
    own, owned = owners.shape
    plan = Plan()
    plan.own, plan.owned, plan.tiles, plan.domains = own, owned, own * CORES, domains
    plan.lanes = positions.shape[2] // own
    plan.near, plan.listed = pair_tiles.shape[1], halo_tiles.shape[2]
    components = widths.shape[0]
    half = plan.half = components // CORES
    tiles, lanes, listed = plan.tiles, plan.lanes, plan.listed

    args = [
        positions.transpose(1, 0, 2),
        velocities.transpose(1, 0, 2),
        charge[None],
        inverse_mass[None],
        centres,
        widths[None],
        map_density[None],
        map_error[None],
        owners,
        halo_tiles,
    ]
    int_rows = -(-(own + halo_tiles.shape[1]) // 8) * 8
    state_own, comp_send, ints = call(
        "pack",
        pack_kernel,
        [],
        args,
        [shape(8, own * lanes), shape(domains, 6, half), shape(int_rows, lanes, dtype=jnp.int32)],
        [(arg.shape, arg.dtype) for arg in args] + [pltpu.SemaphoreType.DMA((len(args),))],
        limit=None,
        spaces=[HBM] * len(args),
    )
    comps = lax.all_to_all(comp_send, ("z", "core"), 0, 0, tiled=True)
    width = -(-((tiles * owned + domains) // 2 + UNROLL + 1) // lanes) * lanes
    lists = call(
        "lists",
        functools.partial(list_kernel, plan),
        [ints, swap_cores(ints), pair_tiles],
        [],
        shape(4 + plan.near, width, dtype=jnp.int32),
        [pltpu.SMEM((domains,), jnp.int32)],
        out_spaces=SMEM,
    )
    if replicas <= 4:
        others = [
            lax.ppermute(state_own, "rep", [(r, r ^ n) for r in range(replicas)])
            for n in range(1, replicas)
        ]
    else:
        others = [
            lax.all_to_all(
                jnp.broadcast_to(state_own[None], (replicas,) + state_own.shape),
                "rep", 0, 0, tiled=True,
            )
        ]
    chosen = call(
        "choose",
        choose_kernel,
        [partner, decision],
        [state_own] + others,
        shape(8, own * lanes),
    )
    chosen_other = swap_cores(chosen)

    map_gain = map_scale / (owned * components)
    scale = 1.0 / (owned * own * lanes)
    pair_gain = (plan.near * lanes) ** (-0.5)
    group = replicas * heights
    plan.one_phase = group * domains * half * 4 <= ONE_PHASE_BYTES
    copies = group if plan.one_phase else 1
    rim_rows = -(-4 * listed // 8) * 8
    onward = [(2 * i, (2 * i + 2) % domains) for i in range(heights)]
    onward += [((2 * i + 3) % domains, 2 * i + 1) for i in range(heights)]
    padded = -(-(own + 2 * listed + 1) // 8) * 8
    outs = [
        shape(copies, max(domains, rim_rows), half + lanes),
        shape(8, tiles, lanes),
        shape(tiles + 1, DEPTH, lanes, dtype=bf16),
    ]
    scratch = [(tiles + 1, DEPTH, lanes), (domains, 8, half), (rim_rows, lanes),
               ((tiles + 1, lanes, DEPTH), bf16)]
    for step in range(STEPS):
        if step == 0:
            partial, state, points, right = call(
                "first",
                functools.partial(first_kernel, plan, scale),
                [lists],
                [chosen, chosen_other, comps],
                outs + [shape(domains, DEPTH, half, dtype=bf16)],
                scratch + [(domains, DEPTH, half)],
            )
            turned = call("turn", turn_kernel, [], [right], shape(domains, half, DEPTH, dtype=bf16))
        else:
            partial, state, points = call(
                "next",
                functools.partial(next_kernel, plan, scale),
                [lists],
                [state, force, swapped, right],
                outs,
                scratch,
            )
        if plan.one_phase:
            sums = far = lax.all_to_all(partial, ("rep", "z"), 0, 0, tiled=True)
        else:
            far = lax.ppermute(partial, ("z", "core"), onward)
            pieces = lax.all_to_all(
                partial[0, :domains, :half].reshape(group, -1), ("rep", "z"), 0, 0, tiled=True
            )
            piece = jnp.sum(pieces, 0)
            sums = lax.all_to_all(
                jnp.broadcast_to(piece[None], (group,) + piece.shape), ("rep", "z"), 0, 0, tiled=True
            ).reshape(1, domains, half)
        pair = call(
            "near",
            functools.partial(near_kernel, plan, pair_gain),
            [lists],
            [state, points],
            shape(3, own, lanes),
            [(4, padded, lanes), (padded, DEPTH, lanes), (padded, ROWS, lanes),
             ((padded, lanes, DEPTH), bf16)],
        )
        force = call(
            "push",
            functools.partial(push_kernel, plan, map_gain, pair_gain, float(replicas)),
            [lists],
            [state, comps, sums, far, pair, points, turned],
            shape(4, tiles, lanes),
            [(domains, ROWS, half), ((domains, ROWS, half), bf16), (half // lanes, domains, lanes),
             (tiles + 1, ROWS, lanes), (listed, DEPTH, lanes), (listed, ROWS, lanes)],
        )
        swapped = swap_cores(force)

    new_x, new_v, model_map = call(
        "finish",
        functools.partial(finish_kernel, plan),
        [],
        [state, force, swapped],
        [shape(3, 1, own * lanes), shape(3, 1, own * lanes), shape(1, components)],
        [(6, tiles, lanes)],
    )
    return (new_x.transpose(1, 0, 2), new_v.transpose(1, 0, 2), model_map.reshape(components))


def solution(mesh):
    replicas, domains = mesh.devices.shape
    split = Mesh(
        mesh.devices.reshape(replicas, domains // CORES, CORES), ("rep", "z", "core")
    )
    dom = ("z", "core")
    placed = (
        P("rep", None, dom),
        P("rep", None, dom),
        P(dom),
        P(dom),
        P(dom, None),
        P(dom, None, None),
        P(dom, None),
        P(None, dom),
        P(dom),
        P(dom),
        P(dom),
        P(),
        P(),
    )
    return jax.shard_map(
        local,
        mesh=split,
        in_specs=placed,
        out_specs=(P("rep", None, dom), P("rep", None, dom), P(dom)),
        check_vma=False,
    )
```

```python
import functools
import math

import jax
import jax.numpy as jnp
from jax import lax
from jax.experimental import pallas as pl
from jax.experimental.pallas import tpu as pltpu
from jax.sharding import Mesh, PartitionSpec as P

STEPS = 2
CORES = 2
DEPTH = 32
ROWS = 16
CHUNK = 256
UNROLL = 2
FAR_SQUARE = 1048576.0

time_step = 0.5
pair_width = 1.0
map_scale = 2.0
log2e = math.log2(math.e)
f32 = jnp.float32
bf16 = jnp.bfloat16

LEFT_PARTS = (0, 0, 1, 1, 0, 2)
RIGHT_PARTS = (0, 1, 0, 1, 2, 0)


def split3(value):
    high = value.astype(bf16).astype(f32)
    rest = value - high
    middle = rest.astype(bf16).astype(f32)
    return high, middle, rest - middle


def point_rows(coords):
    rows = []
    for coord in coords:
        parts = split3(coord)
        rows += [parts[i] for i in LEFT_PARTS]
    parts = split3(coords[0] * coords[0] + coords[1] * coords[1] + coords[2] * coords[2])
    rows += [parts[i] for i in LEFT_PARTS]
    one = jnp.ones_like(coords[0])
    return rows + [one, one, one]


def nowhere(ref, tile):
    shape = ref.shape[1:]
    row = lax.broadcasted_iota(jnp.int32, shape, 0)
    square = len(LEFT_PARTS) * 3
    ref[tile] = jnp.where(row == square, FAR_SQUARE, 0.0)


def centre_rows(coords, extent):
    scale = log2e / extent
    rows = []
    for coord in coords:
        parts = split3(coord * scale)
        rows += [parts[i] for i in RIGHT_PARTS]
    parts = split3(-0.5 * scale)
    rows += [parts[i] for i in RIGHT_PARTS]
    square = coords[0] * coords[0] + coords[1] * coords[1] + coords[2] * coords[2]
    return rows + list(split3(-0.5 * scale * square))


def pull_rows(coords, weight):
    rows = list(split3(weight))
    for coord in coords:
        rows += list(split3(coord * weight))
    return rows


def squeeze_sums(coords, sums):
    def total(first):
        return sums[first : first + 1] + sums[first + 1 : first + 2] + sums[first + 2 : first + 3]

    strength = total(0)
    return [coords[i] * strength - total(3 + 3 * i) for i in range(3)]


def dot(left, right):
    return jnp.dot(left, right, preferred_element_type=f32)


def high_low(value):
    high = value.astype(bf16)
    return high, (value - high.astype(f32)).astype(bf16)


def store_rows(ref, rows):
    count, depth, width = rows[0].shape[0], ref.shape[1], ref.shape[2]
    for index, row in enumerate(rows):
        ref[0:count, index, :] = row
    if len(rows) < depth:
        ref[0:count, len(rows) : depth, :] = jnp.zeros((count, depth - len(rows), width), f32)


def chunks(total, wanted):
    size = wanted if total % wanted == 0 else total
    return [(start, size) for start in range(0, total, size)]


def pack_kernel(pos_hbm, vel_hbm, charge_hbm, mass_hbm, centre_hbm, width_hbm, density_hbm,
                error_hbm, owners_hbm, halo_hbm, state_ref, comp_ref, ints_ref, pos_ref, vel_ref,
                charge_ref, mass_ref, centre_ref, width_ref, density_ref, error_ref, owners_ref,
                halo_ref, sems):
    sources = (pos_hbm, vel_hbm, charge_hbm, mass_hbm, centre_hbm, width_hbm, density_hbm,
               error_hbm, owners_hbm, halo_hbm)
    targets = (pos_ref, vel_ref, charge_ref, mass_ref, centre_ref, width_ref, density_ref,
               error_ref, owners_ref, halo_ref)
    copies = [
        pltpu.make_async_copy(source, target, sems.at[n])
        for n, (source, target) in enumerate(zip(sources, targets))
    ]
    for copy in copies:
        copy.start()
    for copy in copies:
        copy.wait()
    half = comp_ref.shape[2]
    for i in range(3):
        state_ref[i : i + 1, :] = pos_ref[i]
        state_ref[3 + i : 4 + i, :] = vel_ref[i]
    state_ref[6:7, :] = charge_ref[...]
    state_ref[7:8, :] = mass_ref[...]
    owned, own = owners_ref.shape
    _, sides, listed = halo_ref.shape
    ints_ref[...] = jnp.zeros_like(ints_ref)
    ints_ref[0:owned, 0:own] = owners_ref[...]
    ints_ref[owned : owned + sides, 0:listed] = halo_ref[0]
    for row in range(comp_ref.shape[0]):
        part = pl.ds((row % CORES) * half, half)
        comp_ref[row, 0:3, :] = centre_ref[:, part]
        comp_ref[row, 3:4, :] = width_ref[:, part]
        comp_ref[row, 4:5, :] = density_ref[:, part]
        comp_ref[row, 5:6, :] = error_ref[:, part]


def choose_kernel(partner_ref, decision_ref, mine_ref, *refs):
    others, out_ref = refs[:-1], refs[-1]
    row = lax.axis_index("rep")
    source = jnp.where(decision_ref[row] == 1, partner_ref[row], row)
    if len(others) == 1:
        out_ref[...] = others[0][source]
        return
    out_ref[...] = mine_ref[...]
    for n, other_ref in enumerate(others):

        @pl.when(source == (row ^ (n + 1)))
        def _():
            out_ref[...] = other_ref[...]


def list_kernel(plan, mine_ref, theirs_ref, pairs_ref, out_ref, waiting):
    core = lax.axis_index("core")

    def clear(domain, carry):
        waiting[domain] = -1
        return carry

    lax.fori_loop(0, plan.domains, clear, 0)

    def one_tile(tile, count):
        row = lax.rem(tile, plan.own)
        here = lax.div(tile, plan.own) == core
        for j in range(plan.owned):
            owner = jnp.where(here, mine_ref[j, row], theirs_ref[j, row])
            first = waiting[owner]
            out_ref[0, count] = owner
            out_ref[1, count] = first
            out_ref[2, count] = tile
            count = count + jnp.where(first < 0, 0, 1)
            waiting[owner] = jnp.where(first < 0, tile, -1)
        return count

    count = lax.fori_loop(0, plan.tiles, one_tile, 0)

    def leftover(domain, count):
        first = waiting[domain]
        out_ref[0, count] = domain
        out_ref[1, count] = first
        out_ref[2, count] = plan.tiles
        return count + jnp.where(first < 0, 0, 1)

    count = lax.fori_loop(0, plan.domains, leftover, count)
    for extra in range(UNROLL - 1):
        out_ref[0, count + extra] = 0
        out_ref[1, count + extra] = plan.tiles
        out_ref[2, count + extra] = plan.tiles
    out_ref[3, 0] = lax.div(count + UNROLL - 1, UNROLL)
    for side in range(2):
        for k in range(plan.listed):
            out_ref[3, 1 + side * plan.listed + k] = theirs_ref[plan.owned + side, k]
    for tile in range(plan.own):
        for j in range(plan.near):
            out_ref[4 + j, tile] = pairs_ref[tile, j]


def partner_tile(plan, lists_ref, side, k):
    core = lax.axis_index("core")
    return (1 - core) * plan.own + lists_ref[3, 1 + side * plan.listed + k]


def for_pairs(lists_ref, body):
    def step(n, carry):
        for u in range(UNROLL):
            place = n * UNROLL + u
            body(place, lists_ref[0, place], lists_ref[1, place], lists_ref[2, place])
        return carry

    lax.fori_loop(0, lists_ref[3, 0], step, 0)


def sum_gaussians(plan, scale, lists_ref, state_ref, turned_ref, points_ref, out_ref, rim_ref, high_ref,
                  low_ref, xs, acc):
    tiles, listed, lanes = plan.tiles, plan.listed, plan.lanes
    store_rows(xs, point_rows([state_ref[i] for i in range(3)]))
    nowhere(xs, tiles)
    points_ref[...] = xs[...].astype(bf16)
    core = lax.axis_index("core")
    for k in range(listed):
        tile = partner_tile(plan, lists_ref, 1 - core, k)
        for i, row in enumerate((0, 1, 2, 6)):
            rim_ref[i * listed + k : i * listed + k + 1, :] = state_ref[row, pl.ds(tile, 1), :]
    acc[...] = jnp.zeros_like(acc)

    def one_pair(place, owner, first, second):
        points = jnp.concatenate([points_ref[first], points_ref[second]], 1)
        for start, size in chunks(plan.half, CHUNK):
            part = slice(start, start + size)
            g = jnp.exp2(dot(turned_ref[owner, part, :], points))
            acc[owner, part, :] += g[:, :lanes] + g[:, lanes:]
            high_ref[place, part, :], low_ref[place, part, :] = high_low(g)

    for_pairs(lists_ref, one_pair)
    for domain in range(plan.domains):
        for start, size in chunks(plan.half, lanes):
            total = jnp.sum(acc[domain, start : start + size, :].T, 0, keepdims=True)
            out_ref[domain : domain + 1, start : start + size] = total * scale


def first_kernel(plan, scale, lists_ref, mine_ref, theirs_ref, comp_ref,
                 out_ref, rim_ref, state_ref, points_ref, high_ref, low_ref, turned_ref, xs, acc, cs):
    core = lax.axis_index("core")
    for tile in range(plan.own):
        lanes = slice(tile * plan.lanes, (tile + 1) * plan.lanes)
        mine, theirs = mine_ref[:, lanes], theirs_ref[:, lanes]
        state_ref[:, tile, :] = jnp.where(core == 0, mine, theirs)
        state_ref[:, plan.own + tile, :] = jnp.where(core == 0, theirs, mine)
    store_rows(cs, centre_rows([comp_ref[:, i, :] for i in range(3)], comp_ref[:, 3, :]))
    for domain in range(plan.domains):
        for start, size in chunks(plan.half, 128):
            turned_ref[domain, start : start + size, :] = cs[
                domain, :, start : start + size
            ].T.astype(bf16)
    sum_gaussians(plan, scale, lists_ref, state_ref, turned_ref, points_ref, out_ref, rim_ref, high_ref,
                  low_ref, xs, acc)


def stepped(old_ref, mine_ref, theirs_ref):
    mass = time_step * old_ref[7]
    for i in range(3):
        v = old_ref[3 + i] + mass * (mine_ref[i] + theirs_ref[i])
        yield old_ref[i] + time_step * v, v


def next_kernel(plan, scale, lists_ref, old_ref, force_ref, swapped_ref, turned_ref,
                out_ref, rim_ref, state_ref, points_ref, high_ref, low_ref, xs, acc):
    for i, (x, v) in enumerate(stepped(old_ref, force_ref, swapped_ref)):
        state_ref[i] = x
        state_ref[3 + i] = v
    state_ref[6] = old_ref[6]
    state_ref[7] = old_ref[7]
    sum_gaussians(plan, scale, lists_ref, state_ref, turned_ref, points_ref, out_ref, rim_ref, high_ref,
                  low_ref, xs, acc)


def tree_sum(refs):
    values = [ref[...] for ref in refs]
    while len(values) > 1:
        values = [values[i] + values[i + 1] for i in range(0, len(values), 2)]
    return values[0]


def add_kernel(*refs):
    refs[-1][...] = tree_sum(refs[:-1])


def finish_kernel(plan, old_ref, mine_ref, theirs_ref, x_ref, v_ref, map_ref, state):
    for i, (x, v) in enumerate(stepped(old_ref, mine_ref, theirs_ref)):
        state[i] = x
        state[3 + i] = v
    core = lax.axis_index("core")
    base = core * plan.own
    for tile in range(plan.own):
        lanes = slice(tile * plan.lanes, (tile + 1) * plan.lanes)
        for i in range(3):
            x_ref[i, :, lanes] = state[i, pl.ds(base + tile, 1), :]
            v_ref[i, :, lanes] = state[3 + i, pl.ds(base + tile, 1), :]
    first = core == 0
    pieces = plan.half // plan.lanes
    for n in range(pieces):
        keep = mine_ref[3, n : n + 1, :]
        got = theirs_ref[3, pieces + n : pieces + n + 1, :]
        low = slice(n * plan.lanes, (n + 1) * plan.lanes)
        high = slice(plan.half + n * plan.lanes, plan.half + (n + 1) * plan.lanes)
        map_ref[:, low] = jnp.where(first, keep, got)
        map_ref[:, high] = jnp.where(first, got, keep)


def pair_kernel(plan, gain, lists_ref, state_ref, far_ref, points_ref, out_ref, table, cs, rs, rows,
                turned):
    own, near, listed = plan.own, plan.near, plan.listed
    core = lax.axis_index("core")
    base = pl.multiple_of(core * own, own)
    extent = own + 2 * listed
    table[...] = jnp.zeros_like(table)
    for i, source in enumerate((0, 1, 2, 6)):
        table[i, 0:own, :] = state_ref[source, pl.ds(base, own), :]
        for k in range(listed):
            table[i, pl.ds(own + (1 - core) * listed + k, 1), :] = state_ref[
                source, pl.ds(partner_tile(plan, lists_ref, core, k), 1), :
            ]
            table[i, pl.ds(own + core * listed + k, 1), :] = far_ref[
                i * listed + k : i * listed + k + 1, :
            ]
    coords = [table[i] for i in range(3)]
    store_rows(cs, centre_rows(coords, jnp.full_like(coords[0], pair_width)))
    store_rows(rs, pull_rows(coords, table[3]))
    rows[...] = rs[...].astype(bf16)
    for entry in range(extent + 1):
        turned[entry] = cs[entry].T.astype(bf16)
    for tile in range(own):
        points = points_ref[base + tile]
        entries = [lists_ref[4 + j, tile] for j in range(near)]
        entries = [jnp.where(entry < 0, extent, entry) for entry in entries]
        left = jnp.concatenate([turned[entry] for entry in entries], 0)
        weights = jnp.concatenate([rows[entry] for entry in entries], 1)
        high, low = high_low(jnp.exp2(dot(left, points)))
        sums = dot(weights, high) + dot(weights, low)
        coords = [state_ref[i, pl.ds(base + tile, 1), :] for i in range(3)]
        strength = gain / pair_width * state_ref[6, pl.ds(base + tile, 1), :]
        for i, push in enumerate(squeeze_sums(coords, sums)):
            out_ref[i, tile : tile + 1, :] = strength * push


def push_kernel(plan, gain, replicas, lists_ref, state_ref, comp_ref, pair_ref, high_ref, low_ref, *refs):
    parts, (out_ref, rs, rows, means, sums) = refs[:-5], refs[-5:]
    tiles, lanes = plan.tiles, plan.lanes
    mean = tree_sum(parts) / replicas
    for n in range(plan.half // lanes):
        means[n] = mean[:, n * lanes : (n + 1) * lanes]
    error = comp_ref[:, 5, :]
    coefficient = gain * (mean - comp_ref[:, 4, :]) / (error * error) / comp_ref[:, 3, :]
    store_rows(rs, pull_rows([comp_ref[:, i, :] for i in range(3)], coefficient))
    rows[...] = rs[...].astype(bf16)
    sums[...] = jnp.zeros_like(sums)

    def one_pair(place, owner, first, second):
        weights = rows[owner]
        total = dot(weights, high_ref[place]) + dot(weights, low_ref[place])
        sums[first] += total[:, :lanes]
        sums[second] += total[:, lanes:]

    for_pairs(lists_ref, one_pair)

    def added(row):
        return sums[0:tiles, row, :] + sums[0:tiles, row + 1, :] + sums[0:tiles, row + 2, :]

    strength = added(0)
    for i in range(3):
        out_ref[i] = state_ref[i] * strength - added(3 + 3 * i)
    core = lax.axis_index("core")
    own = pl.ds(pl.multiple_of(core * plan.own, plan.own), plan.own)
    for i in range(3):
        out_ref[i, own, :] += pair_ref[i]

    pieces = plan.half // lanes
    here = lax.axis_index("z") * CORES
    out_ref[3] = jnp.zeros_like(out_ref[3])
    for n in range(pieces):
        keep = means[n, pl.ds(here + core, 1), :]
        give = means[n, pl.ds(here + 1 - core, 1), :]
        out_ref[3, n : n + 1, :] = keep
        out_ref[3, pieces + n : pieces + n + 1, :] = give


VMEM = pl.BlockSpec(memory_space=pltpu.VMEM)
SMEM = pl.BlockSpec(memory_space=pltpu.SMEM)
HBM = pl.BlockSpec(memory_space=pltpu.HBM)


def shape(*dims, dtype=f32):
    return jax.ShapeDtypeStruct(dims, dtype)


def with_types(scratch):
    for entry in scratch:
        if not isinstance(entry, tuple):
            yield entry
        else:
            dims, dtype = entry if isinstance(entry[0], tuple) else (entry, f32)
            yield pltpu.VMEM(dims, dtype)


def call(name, kernel, lists, args, outs, scratch=(), limit=16, spaces=None, out_spaces=None):
    many = isinstance(outs, (list, tuple))
    return pl.pallas_call(
        kernel,
        out_shape=tuple(outs) if many else outs,
        in_specs=[SMEM] * len(lists) + (spaces or [VMEM] * len(args)),
        out_specs=tuple(out_spaces or [VMEM] * len(outs)) if many else (out_spaces or VMEM),
        scratch_shapes=list(with_types(scratch)),
        compiler_params=pltpu.CompilerParams(vmem_limit_bytes=limit and limit << 20),
        name=name,
    )(*lists, *args)


class Plan:
    pass


def swap_cores(value):
    return lax.ppermute(value, "core", [(0, 1), (1, 0)])


def exchange(value, axis):
    count = lax.axis_size(axis)
    return [
        lax.ppermute(value, axis, [(i, i ^ n) for i in range(count)]) for n in range(1, count)
    ]


def local(
    positions,
    velocities,
    charge,
    inverse_mass,
    pair_tiles,
    halo_tiles,
    owners,
    centres,
    widths,
    map_density,
    map_error,
    partner,
    decision,
):
    replicas = lax.axis_size("rep")
    heights = lax.axis_size("z")
    domains = heights * CORES
    own, owned = owners.shape
    plan = Plan()
    plan.own, plan.owned, plan.tiles, plan.domains = own, owned, own * CORES, domains
    plan.lanes = positions.shape[2] // own
    plan.near, plan.listed = pair_tiles.shape[1], halo_tiles.shape[2]
    components = widths.shape[0]
    half = plan.half = components // CORES
    tiles, lanes, listed = plan.tiles, plan.lanes, plan.listed

    args = [
        positions.transpose(1, 0, 2),
        velocities.transpose(1, 0, 2),
        charge[None],
        inverse_mass[None],
        centres,
        widths[None],
        map_density[None],
        map_error[None],
        owners.T,
        halo_tiles,
    ]
    int_rows = -(-(owned + halo_tiles.shape[1]) // 8) * 8
    state_own, comp_send, ints = call(
        "pack",
        pack_kernel,
        [],
        args,
        [shape(8, own * lanes), shape(domains, 6, half), shape(int_rows, lanes, dtype=jnp.int32)],
        [(arg.shape, arg.dtype) for arg in args] + [pltpu.SemaphoreType.DMA((len(args),))],
        limit=None,
        spaces=[HBM] * len(args),
    )
    comps = lax.all_to_all(comp_send, ("z", "core"), 0, 0, tiled=True)
    width = -(-((tiles * owned + domains) // 2 + UNROLL + 1) // lanes) * lanes
    lists = call(
        "lists",
        functools.partial(list_kernel, plan),
        [ints, swap_cores(ints), pair_tiles],
        [],
        shape(4 + plan.near, width, dtype=jnp.int32),
        [pltpu.SMEM((domains,), jnp.int32)],
        out_spaces=SMEM,
    )
    small = replicas in (1, 2, 4) and heights in (1, 2, 4)
    if small:
        others = exchange(state_own, "rep")
    else:
        others = [
            lax.all_to_all(
                jnp.broadcast_to(state_own[None], (replicas,) + state_own.shape),
                "rep", 0, 0, tiled=True,
            )
        ]
    chosen = call(
        "choose",
        choose_kernel,
        [partner, decision],
        [state_own] + others,
        shape(8, own * lanes),
    )
    chosen_other = swap_cores(chosen)

    map_gain = map_scale / (owned * components)
    scale = 1.0 / (owned * own * lanes)
    pair_gain = (plan.near * lanes) ** (-0.5)
    group = replicas * heights
    rim_rows = -(-4 * listed // 8) * 8
    onward = [(2 * i, (2 * i + 2) % domains) for i in range(heights)]
    onward += [((2 * i + 3) % domains, 2 * i + 1) for i in range(heights)]
    padded = -(-(own + 2 * listed + 1) // 8) * 8
    most = (tiles * owned + domains) // 2 + UNROLL
    kept = shape(most, half, 2 * lanes, dtype=bf16)
    outs = [
        shape(domains, half),
        shape(rim_rows, lanes),
        shape(8, tiles, lanes),
        shape(tiles + 1, DEPTH, lanes, dtype=bf16),
        kept,
        kept,
    ]
    scratch = [(tiles + 1, DEPTH, lanes), (domains, half, lanes)]
    for step in range(STEPS):
        if step == 0:
            partial, rim, state, points, high, low, turned = call(
                "first",
                functools.partial(first_kernel, plan, scale),
                [lists],
                [chosen, chosen_other, comps],
                outs + [shape(domains, half, DEPTH, dtype=bf16)],
                scratch + [(domains, DEPTH, half)],
            )
        else:
            partial, rim, state, points, high, low = call(
                "next",
                functools.partial(next_kernel, plan, scale),
                [lists],
                [state, force, swapped, turned],
                outs,
                scratch,
            )
        far = lax.ppermute(rim, ("z", "core"), onward)
        if small:
            partial = call(
                "add", add_kernel, [], [partial] + exchange(partial, "rep"), shape(domains, half)
            )
            parts = [partial] + exchange(partial, "z")
        else:
            pieces = lax.all_to_all(partial.reshape(group, -1), ("rep", "z"), 0, 0, tiled=True)
            piece = jnp.sum(pieces, 0)
            parts = [
                lax.all_to_all(
                    jnp.broadcast_to(piece[None], (group,) + piece.shape),
                    ("rep", "z"), 0, 0, tiled=True,
                ).reshape(domains, half)
            ]
        pair = call(
            "pair",
            functools.partial(pair_kernel, plan, pair_gain),
            [lists],
            [state, far, points],
            shape(3, own, lanes),
            [(4, padded, lanes), (padded, DEPTH, lanes), (padded, ROWS, lanes),
             ((padded, ROWS, lanes), bf16), ((padded, lanes, DEPTH), bf16)],
        )
        force = call(
            "push",
            functools.partial(push_kernel, plan, map_gain, float(replicas)),
            [lists],
            [state, comps, pair, high, low] + parts,
            shape(4, tiles, lanes),
            [(domains, ROWS, half), ((domains, ROWS, half), bf16), (half // lanes, domains, lanes),
             (tiles + 1, ROWS, lanes)],
        )
        swapped = swap_cores(force)

    new_x, new_v, model_map = call(
        "finish",
        functools.partial(finish_kernel, plan),
        [],
        [state, force, swapped],
        [shape(3, 1, own * lanes), shape(3, 1, own * lanes), shape(1, components)],
        [(6, tiles, lanes)],
    )
    return (new_x.transpose(1, 0, 2), new_v.transpose(1, 0, 2), model_map.reshape(components))


def solution(mesh):
    replicas, domains = mesh.devices.shape
    split = Mesh(
        mesh.devices.reshape(replicas, domains // CORES, CORES), ("rep", "z", "core")
    )
    dom = ("z", "core")
    placed = (
        P("rep", None, dom),
        P("rep", None, dom),
        P(dom),
        P(dom),
        P(dom, None),
        P(dom, None, None),
        P(dom, None),
        P(None, dom),
        P(dom),
        P(dom),
        P(dom),
        P(),
        P(),
    )
    return jax.shard_map(
        local,
        mesh=split,
        in_specs=placed,
        out_specs=(P("rep", None, dom), P("rep", None, dom), P(dom)),
        check_vma=False,
    )
```

```python
import functools
import math

import jax
import jax.numpy as jnp
from jax import lax
from jax.experimental import pallas as pl
from jax.experimental.pallas import tpu as pltpu
from jax.sharding import Mesh, PartitionSpec as P

STEPS = 2
CORES = 2
DEPTH = 32
ROWS = 16
CHUNK = 256
UNROLL = 2
FAR_SQUARE = 1048576.0

time_step = 0.5
pair_width = 1.0
map_scale = 2.0
log2e = math.log2(math.e)
f32 = jnp.float32
bf16 = jnp.bfloat16

LEFT_PARTS = (0, 0, 1, 1, 0, 2)
RIGHT_PARTS = (0, 1, 0, 1, 2, 0)


def split3(value):
    high = value.astype(bf16).astype(f32)
    rest = value - high
    middle = rest.astype(bf16).astype(f32)
    return high, middle, rest - middle


def point_rows(coords):
    rows = []
    for coord in coords:
        parts = split3(coord)
        rows += [parts[i] for i in LEFT_PARTS]
    parts = split3(coords[0] * coords[0] + coords[1] * coords[1] + coords[2] * coords[2])
    rows += [parts[i] for i in LEFT_PARTS]
    one = jnp.ones_like(coords[0])
    return rows + [one, one, one]


def nowhere(ref, tile):
    shape = ref.shape[1:]
    row = lax.broadcasted_iota(jnp.int32, shape, 0)
    square = len(LEFT_PARTS) * 3
    ref[tile] = jnp.where(row == square, FAR_SQUARE, 0.0)


def centre_rows(coords, extent):
    scale = log2e / extent
    rows = []
    for coord in coords:
        parts = split3(coord * scale)
        rows += [parts[i] for i in RIGHT_PARTS]
    parts = split3(-0.5 * scale)
    rows += [parts[i] for i in RIGHT_PARTS]
    square = coords[0] * coords[0] + coords[1] * coords[1] + coords[2] * coords[2]
    return rows + list(split3(-0.5 * scale * square))


def pull_rows(coords, weight):
    rows = list(split3(weight))
    for coord in coords:
        rows += list(split3(coord * weight))
    return rows


def squeeze_sums(coords, sums):
    def total(first):
        return sums[first : first + 1] + sums[first + 1 : first + 2] + sums[first + 2 : first + 3]

    strength = total(0)
    return [coords[i] * strength - total(3 + 3 * i) for i in range(3)]


def dot(left, right):
    return jnp.dot(left, right, preferred_element_type=f32)


def high_low(value):
    high = value.astype(bf16)
    return high, (value - high.astype(f32)).astype(bf16)


def store_rows(ref, rows):
    count, depth, width = rows[0].shape[0], ref.shape[1], ref.shape[2]
    for index, row in enumerate(rows):
        ref[0:count, index, :] = row
    if len(rows) < depth:
        ref[0:count, len(rows) : depth, :] = jnp.zeros((count, depth - len(rows), width), f32)


def chunks(total, wanted):
    size = wanted if total % wanted == 0 else total
    return [(start, size) for start in range(0, total, size)]


def pack_kernel(pos_hbm, vel_hbm, charge_hbm, mass_hbm, centre_hbm, width_hbm, density_hbm,
                error_hbm, owners_hbm, halo_hbm, pairs_hbm, partner_hbm, decision_hbm, state_ref,
                comp_ref, ints_ref, pos_ref, vel_ref, charge_ref, mass_ref, centre_ref, width_ref,
                density_ref, error_ref, owners_ref, halo_ref, pairs_ref, partner_ref, decision_ref,
                sems):
    sources = (pos_hbm, vel_hbm, charge_hbm, mass_hbm, centre_hbm, width_hbm, density_hbm,
               error_hbm, owners_hbm, halo_hbm, pairs_hbm, partner_hbm, decision_hbm)
    targets = (pos_ref, vel_ref, charge_ref, mass_ref, centre_ref, width_ref, density_ref,
               error_ref, owners_ref, halo_ref, pairs_ref, partner_ref, decision_ref)
    copies = [
        pltpu.make_async_copy(source, target, sems.at[n])
        for n, (source, target) in enumerate(zip(sources, targets))
    ]
    for copy in copies:
        copy.start()
    for copy in copies:
        copy.wait()
    half = comp_ref.shape[2]
    for i in range(3):
        state_ref[i : i + 1, :] = pos_ref[i]
        state_ref[3 + i : 4 + i, :] = vel_ref[i]
    state_ref[6:7, :] = charge_ref[...]
    state_ref[7:8, :] = mass_ref[...]
    owned, own = owners_ref.shape
    _, sides, listed = halo_ref.shape
    ints_ref[...] = jnp.zeros_like(ints_ref)
    ints_ref[0:owned, 0:own] = owners_ref[...]
    ints_ref[owned : owned + sides, 0:listed] = halo_ref[0]
    last = owned + sides
    ints_ref[last : last + 1, 0 : partner_ref.shape[1]] = partner_ref[...]
    ints_ref[last + 1 : last + 2, 0 : decision_ref.shape[1]] = decision_ref[...]
    rows, near = pairs_ref.shape
    ints_ref[last + 2 : last + 2 + rows, 0:near] = pairs_ref[...]
    for row in range(comp_ref.shape[0]):
        part = pl.ds((row % CORES) * half, half)
        comp_ref[row, 0:3, :] = centre_ref[:, part]
        comp_ref[row, 3:4, :] = width_ref[:, part]
        comp_ref[row, 4:5, :] = density_ref[:, part]
        comp_ref[row, 5:6, :] = error_ref[:, part]


def choose_kernel(plan, ints_ref, mine_ref, *refs):
    others, out_ref = refs[:-1], refs[-1]
    row = lax.axis_index("rep")
    last = plan.owned + 2
    source = jnp.where(ints_ref[last + 1, row] == 1, ints_ref[last, row], row)
    if len(others) == 1:
        out_ref[...] = others[0][source]
        return
    out_ref[...] = mine_ref[...]
    for n, other_ref in enumerate(others):

        @pl.when(source == (row ^ (n + 1)))
        def _():
            out_ref[...] = other_ref[...]


def list_kernel(plan, mine_ref, theirs_ref, out_ref, waiting):
    core = lax.axis_index("core")

    def clear(domain, carry):
        waiting[domain] = -1
        return carry

    lax.fori_loop(0, plan.domains, clear, 0)

    def one_tile(tile, count):
        row = lax.rem(tile, plan.own)
        here = lax.div(tile, plan.own) == core
        for j in range(plan.owned):
            owner = jnp.where(here, mine_ref[j, row], theirs_ref[j, row])
            first = waiting[owner]
            out_ref[0, count] = owner
            out_ref[1, count] = first
            out_ref[2, count] = tile
            count = count + jnp.where(first < 0, 0, 1)
            waiting[owner] = jnp.where(first < 0, tile, -1)
        return count

    count = lax.fori_loop(0, plan.tiles, one_tile, 0)

    def leftover(domain, count):
        first = waiting[domain]
        out_ref[0, count] = domain
        out_ref[1, count] = first
        out_ref[2, count] = plan.tiles
        return count + jnp.where(first < 0, 0, 1)

    count = lax.fori_loop(0, plan.domains, leftover, count)
    for extra in range(UNROLL - 1):
        out_ref[0, count + extra] = 0
        out_ref[1, count + extra] = plan.tiles
        out_ref[2, count + extra] = plan.tiles
    out_ref[3, 0] = lax.div(count + UNROLL - 1, UNROLL)
    for side in range(2):
        for k in range(plan.listed):
            out_ref[3, 1 + side * plan.listed + k] = theirs_ref[plan.owned + side, k]
    for tile in range(plan.own):
        for j in range(plan.near):
            out_ref[4 + j, tile] = mine_ref[plan.owned + 4 + tile, j]


def partner_tile(plan, lists_ref, side, k):
    core = lax.axis_index("core")
    return (1 - core) * plan.own + lists_ref[3, 1 + side * plan.listed + k]


def for_pairs(lists_ref, body):
    def step(n, carry):
        for u in range(UNROLL):
            place = n * UNROLL + u
            body(place, lists_ref[0, place], lists_ref[1, place], lists_ref[2, place])
        return carry

    lax.fori_loop(0, lists_ref[3, 0], step, 0)


def sum_gaussians(plan, scale, lists_ref, state_ref, turned_ref, points_ref, out_ref, rim_ref, kept_ref,
                  xs, acc):
    tiles, listed, lanes = plan.tiles, plan.listed, plan.lanes
    store_rows(xs, point_rows([state_ref[i] for i in range(3)]))
    nowhere(xs, tiles)
    points_ref[...] = xs[...].astype(bf16)
    core = lax.axis_index("core")
    for k in range(listed):
        tile = partner_tile(plan, lists_ref, 1 - core, k)
        for i, row in enumerate((0, 1, 2, 6)):
            rim_ref[i * listed + k : i * listed + k + 1, :] = state_ref[row, pl.ds(tile, 1), :]
    acc[...] = jnp.zeros_like(acc)

    def one_pair(place, owner, first, second):
        points = jnp.concatenate([points_ref[first], points_ref[second]], 1)
        for start, size in chunks(plan.half, CHUNK):
            part = slice(start, start + size)
            g = jnp.exp2(dot(turned_ref[owner, part, :], points))
            acc[owner, part, :] += g[:, :lanes] + g[:, lanes:]
            kept_ref[place, part, :] = g

    for_pairs(lists_ref, one_pair)
    for domain in range(plan.domains):
        for start, size in chunks(plan.half, lanes):
            total = jnp.sum(acc[domain, start : start + size, :].T, 0, keepdims=True)
            out_ref[domain : domain + 1, start : start + size] = total * scale


def first_kernel(plan, scale, lists_ref, mine_ref, theirs_ref, comp_ref,
                 out_ref, rim_ref, state_ref, points_ref, kept_ref, turned_ref, xs, acc, cs):
    core = lax.axis_index("core")
    for tile in range(plan.own):
        lanes = slice(tile * plan.lanes, (tile + 1) * plan.lanes)
        mine, theirs = mine_ref[:, lanes], theirs_ref[:, lanes]
        state_ref[:, tile, :] = jnp.where(core == 0, mine, theirs)
        state_ref[:, plan.own + tile, :] = jnp.where(core == 0, theirs, mine)
    store_rows(cs, centre_rows([comp_ref[:, i, :] for i in range(3)], comp_ref[:, 3, :]))
    for domain in range(plan.domains):
        for start, size in chunks(plan.half, 128):
            turned_ref[domain, start : start + size, :] = cs[
                domain, :, start : start + size
            ].T.astype(bf16)
    sum_gaussians(plan, scale, lists_ref, state_ref, turned_ref, points_ref, out_ref, rim_ref, kept_ref,
                  xs, acc)


def stepped(old_ref, mine_ref, theirs_ref):
    mass = time_step * old_ref[7]
    for i in range(3):
        v = old_ref[3 + i] + mass * (mine_ref[i] + theirs_ref[i])
        yield old_ref[i] + time_step * v, v


def next_kernel(plan, scale, lists_ref, old_ref, force_ref, swapped_ref, turned_ref,
                out_ref, rim_ref, state_ref, points_ref, kept_ref, xs, acc):
    for i, (x, v) in enumerate(stepped(old_ref, force_ref, swapped_ref)):
        state_ref[i] = x
        state_ref[3 + i] = v
    state_ref[6] = old_ref[6]
    state_ref[7] = old_ref[7]
    sum_gaussians(plan, scale, lists_ref, state_ref, turned_ref, points_ref, out_ref, rim_ref, kept_ref,
                  xs, acc)


def tree_sum(refs):
    values = [ref[...] for ref in refs]
    while len(values) > 1:
        values = [values[i] + values[i + 1] for i in range(0, len(values), 2)]
    return values[0]


def add_kernel(*refs):
    refs[-1][...] = tree_sum(refs[:-1])


def finish_kernel(plan, old_ref, mine_ref, theirs_ref, x_ref, v_ref, map_ref, state):
    for i, (x, v) in enumerate(stepped(old_ref, mine_ref, theirs_ref)):
        state[i] = x
        state[3 + i] = v
    core = lax.axis_index("core")
    base = core * plan.own
    for tile in range(plan.own):
        lanes = slice(tile * plan.lanes, (tile + 1) * plan.lanes)
        for i in range(3):
            x_ref[i, :, lanes] = state[i, pl.ds(base + tile, 1), :]
            v_ref[i, :, lanes] = state[3 + i, pl.ds(base + tile, 1), :]
    first = core == 0
    pieces = plan.half // plan.lanes
    for n in range(pieces):
        keep = mine_ref[3, n : n + 1, :]
        got = theirs_ref[3, pieces + n : pieces + n + 1, :]
        low = slice(n * plan.lanes, (n + 1) * plan.lanes)
        high = slice(plan.half + n * plan.lanes, plan.half + (n + 1) * plan.lanes)
        map_ref[:, low] = jnp.where(first, keep, got)
        map_ref[:, high] = jnp.where(first, got, keep)


def pair_kernel(plan, gain, lists_ref, state_ref, far_ref, points_ref, out_ref, table, cs, rs, rows,
                turned):
    own, near, listed = plan.own, plan.near, plan.listed
    core = lax.axis_index("core")
    base = pl.multiple_of(core * own, own)
    extent = own + 2 * listed
    table[...] = jnp.zeros_like(table)
    for i, source in enumerate((0, 1, 2, 6)):
        table[i, 0:own, :] = state_ref[source, pl.ds(base, own), :]
        for k in range(listed):
            table[i, pl.ds(own + (1 - core) * listed + k, 1), :] = state_ref[
                source, pl.ds(partner_tile(plan, lists_ref, core, k), 1), :
            ]
            table[i, pl.ds(own + core * listed + k, 1), :] = far_ref[
                i * listed + k : i * listed + k + 1, :
            ]
    coords = [table[i] for i in range(3)]
    store_rows(cs, centre_rows(coords, jnp.full_like(coords[0], pair_width)))
    store_rows(rs, pull_rows(coords, table[3]))
    rows[...] = rs[...].astype(bf16)
    for entry in range(extent + 1):
        turned[entry] = cs[entry].T.astype(bf16)
    for tile in range(own):
        points = points_ref[base + tile]
        entries = [lists_ref[4 + j, tile] for j in range(near)]
        entries = [jnp.where(entry < 0, extent, entry) for entry in entries]
        left = jnp.concatenate([turned[entry] for entry in entries], 0)
        weights = jnp.concatenate([rows[entry] for entry in entries], 1)
        high, low = high_low(jnp.exp2(dot(left, points)))
        sums = dot(weights, high) + dot(weights, low)
        coords = [state_ref[i, pl.ds(base + tile, 1), :] for i in range(3)]
        strength = gain / pair_width * state_ref[6, pl.ds(base + tile, 1), :]
        for i, push in enumerate(squeeze_sums(coords, sums)):
            out_ref[i, tile : tile + 1, :] = strength * push


def push_kernel(plan, gain, replicas, lists_ref, state_ref, comp_ref, pair_ref, kept_ref, *refs):
    parts, (out_ref, rs, rows, means, sums) = refs[:-5], refs[-5:]
    tiles, lanes = plan.tiles, plan.lanes
    mean = tree_sum(parts) / replicas
    for n in range(plan.half // lanes):
        means[n] = mean[:, n * lanes : (n + 1) * lanes]
    error = comp_ref[:, 5, :]
    coefficient = gain * (mean - comp_ref[:, 4, :]) / (error * error) / comp_ref[:, 3, :]
    store_rows(rs, pull_rows([comp_ref[:, i, :] for i in range(3)], coefficient))
    rows[...] = rs[...].astype(bf16)
    sums[...] = jnp.zeros_like(sums)

    def one_pair(place, owner, first, second):
        total = None
        for start, size in chunks(plan.half, CHUNK):
            part = slice(start, start + size)
            weights = rows[owner, :, part]
            high, low = high_low(kept_ref[place, part, :])
            term = dot(weights, high) + dot(weights, low)
            total = term if total is None else total + term
        sums[first] += total[:, :lanes]
        sums[second] += total[:, lanes:]

    for_pairs(lists_ref, one_pair)

    def added(row):
        return sums[0:tiles, row, :] + sums[0:tiles, row + 1, :] + sums[0:tiles, row + 2, :]

    strength = added(0)
    for i in range(3):
        out_ref[i] = state_ref[i] * strength - added(3 + 3 * i)
    core = lax.axis_index("core")
    own = pl.ds(pl.multiple_of(core * plan.own, plan.own), plan.own)
    for i in range(3):
        out_ref[i, own, :] += pair_ref[i]

    pieces = plan.half // lanes
    here = lax.axis_index("z") * CORES
    out_ref[3] = jnp.zeros_like(out_ref[3])
    for n in range(pieces):
        keep = means[n, pl.ds(here + core, 1), :]
        give = means[n, pl.ds(here + 1 - core, 1), :]
        out_ref[3, n : n + 1, :] = keep
        out_ref[3, pieces + n : pieces + n + 1, :] = give


VMEM = pl.BlockSpec(memory_space=pltpu.VMEM)
SMEM = pl.BlockSpec(memory_space=pltpu.SMEM)
HBM = pl.BlockSpec(memory_space=pltpu.HBM)


def shape(*dims, dtype=f32):
    return jax.ShapeDtypeStruct(dims, dtype)


def with_types(scratch):
    for entry in scratch:
        if not isinstance(entry, tuple):
            yield entry
        else:
            dims, dtype = entry if isinstance(entry[0], tuple) else (entry, f32)
            yield pltpu.VMEM(dims, dtype)


def call(kernel, lists, args, outs, scratch=(), limit=16, spaces=None, out_spaces=None):
    many = isinstance(outs, (list, tuple))
    return pallas(kernel, lists, args, outs, scratch, limit, spaces, out_spaces, many)


def pallas(kernel, lists, args, outs, scratch, limit, spaces, out_spaces, many):
    return pl.pallas_call(
        kernel,
        out_shape=tuple(outs) if many else outs,
        in_specs=[SMEM] * len(lists) + (spaces or [VMEM] * len(args)),
        out_specs=tuple(out_spaces or [VMEM] * len(outs)) if many else (out_spaces or VMEM),
        scratch_shapes=list(with_types(scratch)),
        compiler_params=pltpu.CompilerParams(vmem_limit_bytes=limit and limit << 20),
    )(*lists, *args)


class Plan:
    pass


def swap_cores(value):
    return lax.ppermute(value, "core", [(0, 1), (1, 0)])


def few(replicas, heights):
    return replicas in (2, 4) and heights in (2, 4)


def exchange(value, axis):
    count = lax.axis_size(axis)
    others = []
    for n in range(1, count):
        others.append(lax.ppermute(value, axis, [(i, i ^ n) for i in range(count)]))
    return others


def program(
    positions,
    velocities,
    charge,
    inverse_mass,
    pair_tiles,
    halo_tiles,
    owners,
    centres,
    widths,
    map_density,
    map_error,
    partner,
    decision,
):
    replicas = lax.axis_size("rep")
    heights = lax.axis_size("z")
    domains = heights * CORES
    own, owned = owners.shape
    plan = Plan()
    plan.own, plan.owned, plan.tiles, plan.domains = own, owned, own * CORES, domains
    plan.lanes = positions.shape[2] // own
    plan.near, plan.listed = pair_tiles.shape[1], halo_tiles.shape[2]
    components = widths.shape[0]
    half = plan.half = components // CORES
    tiles, lanes, listed = plan.tiles, plan.lanes, plan.listed

    args = [
        positions.transpose(1, 0, 2),
        velocities.transpose(1, 0, 2),
        charge[None],
        inverse_mass[None],
        centres,
        widths[None],
        map_density[None],
        map_error[None],
        owners.T,
        halo_tiles,
        pair_tiles,
        partner[None],
        decision[None],
    ]
    int_rows = -(-(owned + halo_tiles.shape[1] + 2 + own) // 8) * 8
    state_own, comp_send, ints = call(
        pack_kernel,
        [],
        args,
        [shape(8, own * lanes), shape(domains, 6, half), shape(int_rows, lanes, dtype=jnp.int32)],
        [(arg.shape, arg.dtype) for arg in args] + [pltpu.SemaphoreType.DMA((len(args),))],
        limit=60,
        spaces=[HBM] * len(args),
    )
    comps = lax.all_to_all(comp_send, ("z", "core"), 0, 0, tiled=True)
    other_ints = swap_cores(ints)
    width = -(-((tiles * owned + domains) // 2 + UNROLL + 1) // lanes) * lanes
    lists = call(
        functools.partial(list_kernel, plan),
        [ints, other_ints],
        [],
        shape(4 + plan.near, width, dtype=jnp.int32),
        [pltpu.SMEM((domains,), jnp.int32)],
        out_spaces=SMEM,
    )
    small = few(replicas, heights)
    if small:
        others = exchange(state_own, "rep")
    else:
        others = [
            lax.all_to_all(
                jnp.broadcast_to(state_own[None], (replicas,) + state_own.shape),
                "rep", 0, 0, tiled=True,
            )
        ]
    chosen = call(
        functools.partial(choose_kernel, plan), [ints], [state_own] + others, shape(8, own * lanes)
    )
    chosen_other = swap_cores(chosen)

    map_gain = map_scale / (owned * components)
    scale = 1.0 / (owned * own * lanes)
    pair_gain = (plan.near * lanes) ** (-0.5)
    group = replicas * heights
    rim_rows = -(-4 * listed // 8) * 8
    onward = [(2 * i, (2 * i + 2) % domains) for i in range(heights)]
    onward += [((2 * i + 3) % domains, 2 * i + 1) for i in range(heights)]
    padded = -(-(own + 2 * listed + 1) // 8) * 8
    most = (tiles * owned + domains) // 2 + UNROLL
    outs = [
        shape(domains, half),
        shape(rim_rows, lanes),
        shape(8, tiles, lanes),
        shape(tiles + 1, DEPTH, lanes, dtype=bf16),
        shape(most, half, 2 * lanes),
    ]
    scratch = [(tiles + 1, DEPTH, lanes), (domains, half, lanes)]
    for step in range(STEPS):
        if step == 0:
            partial, rim, state, points, kept, turned = call(
                functools.partial(first_kernel, plan, scale),
                [lists],
                [chosen, chosen_other, comps],
                outs + [shape(domains, half, DEPTH, dtype=bf16)],
                scratch + [(domains, DEPTH, half)],
            )
        else:
            partial, rim, state, points, kept = call(
                functools.partial(next_kernel, plan, scale),
                [lists],
                [state, force, swapped, turned],
                outs,
                scratch,
            )
        far = lax.ppermute(rim, ("z", "core"), onward)
        if small:
            partial = call(
                add_kernel, [], [partial] + exchange(partial, "rep"), shape(domains, half)
            )
            parts = [partial] + exchange(partial, "z")
        else:
            pieces = lax.all_to_all(partial.reshape(group, -1), ("rep", "z"), 0, 0, tiled=True)
            piece = jnp.sum(pieces, 0)
            parts = [
                lax.all_to_all(
                    jnp.broadcast_to(piece[None], (group,) + piece.shape),
                    ("rep", "z"), 0, 0, tiled=True,
                ).reshape(domains, half)
            ]
        pair = call(
            functools.partial(pair_kernel, plan, pair_gain),
            [lists],
            [state, far, points],
            shape(3, own, lanes),
            [(4, padded, lanes), (padded, DEPTH, lanes), (padded, ROWS, lanes),
             ((padded, ROWS, lanes), bf16), ((padded, lanes, DEPTH), bf16)],
        )
        force = call(
            functools.partial(push_kernel, plan, map_gain, float(replicas)),
            [lists],
            [state, comps, pair, kept] + parts,
            shape(4, tiles, lanes),
            [(domains, ROWS, half), ((domains, ROWS, half), bf16), (half // lanes, domains, lanes),
             (tiles + 1, ROWS, lanes)],
        )
        swapped = swap_cores(force)

    new_x, new_v, model_map = call(
        functools.partial(finish_kernel, plan),
        [],
        [state, force, swapped],
        [shape(3, 1, own * lanes), shape(3, 1, own * lanes), shape(1, components)],
        [(6, tiles, lanes)],
    )
    return (new_x.transpose(1, 0, 2), new_v.transpose(1, 0, 2), model_map.reshape(components))


def solution(mesh):
    replicas, domains = mesh.devices.shape
    split = Mesh(
        mesh.devices.reshape(replicas, domains // CORES, CORES), ("rep", "z", "core")
    )
    dom = ("z", "core")
    placed = (
        P("rep", None, dom),
        P("rep", None, dom),
        P(dom),
        P(dom),
        P(dom, None),
        P(dom, None, None),
        P(dom, None),
        P(None, dom),
        P(dom),
        P(dom),
        P(dom),
        P(),
        P(),
    )
    return jax.shard_map(
        program,
        mesh=split,
        in_specs=placed,
        out_specs=(P("rep", None, dom), P("rep", None, dom), P(dom)),
        check_vma=False,
    )
```

```python
import functools
import math

import jax
import jax.numpy as jnp
from jax import lax
from jax.experimental import pallas as pl
from jax.experimental.pallas import tpu as pltpu
from jax.sharding import Mesh, PartitionSpec as P

STEPS = 2
CORES = 2
DEPTH = 32
ROWS = 16
CHUNK = 256
UNROLL = 2
FAR_SQUARE = 1048576.0

time_step = 0.5
pair_width = 1.0
map_scale = 2.0
log2e = math.log2(math.e)
f32 = jnp.float32
bf16 = jnp.bfloat16

LEFT_PARTS = (0, 0, 1, 1, 0, 2)
RIGHT_PARTS = (0, 1, 0, 1, 2, 0)


def split3(value):
    high = value.astype(bf16).astype(f32)
    rest = value - high
    middle = rest.astype(bf16).astype(f32)
    return high, middle, rest - middle


def point_rows(coords):
    rows = []
    for coord in coords:
        parts = split3(coord)
        rows += [parts[i] for i in LEFT_PARTS]
    parts = split3(coords[0] * coords[0] + coords[1] * coords[1] + coords[2] * coords[2])
    rows += [parts[i] for i in LEFT_PARTS]
    one = jnp.ones_like(coords[0])
    return rows + [one, one, one]


def nowhere(ref, tile):
    shape = ref.shape[1:]
    row = lax.broadcasted_iota(jnp.int32, shape, 0)
    square = len(LEFT_PARTS) * 3
    ref[tile] = jnp.where(row == square, FAR_SQUARE, 0.0)


def centre_rows(coords, extent):
    scale = log2e / extent
    rows = []
    for coord in coords:
        parts = split3(coord * scale)
        rows += [parts[i] for i in RIGHT_PARTS]
    parts = split3(-0.5 * scale)
    rows += [parts[i] for i in RIGHT_PARTS]
    square = coords[0] * coords[0] + coords[1] * coords[1] + coords[2] * coords[2]
    return rows + list(split3(-0.5 * scale * square))


def pull_rows(coords, weight):
    rows = list(split3(weight))
    for coord in coords:
        rows += list(split3(coord * weight))
    return rows


def squeeze_sums(coords, sums):
    def total(first):
        return sums[first : first + 1] + sums[first + 1 : first + 2] + sums[first + 2 : first + 3]

    strength = total(0)
    return [coords[i] * strength - total(3 + 3 * i) for i in range(3)]


def dot(left, right):
    return jnp.dot(left, right, preferred_element_type=f32)


def high_low(value):
    high = value.astype(bf16)
    return high, (value - high.astype(f32)).astype(bf16)


def store_rows(ref, rows):
    count, depth, width = rows[0].shape[0], ref.shape[1], ref.shape[2]
    for index, row in enumerate(rows):
        ref[0:count, index, :] = row
    if len(rows) < depth:
        ref[0:count, len(rows) : depth, :] = jnp.zeros((count, depth - len(rows), width), f32)


def chunks(total, wanted):
    size = wanted if total % wanted == 0 else total
    return [(start, size) for start in range(0, total, size)]


def pack_kernel(pos_hbm, vel_hbm, charge_hbm, mass_hbm, centre_hbm, width_hbm, density_hbm,
                error_hbm, owners_hbm, halo_hbm, pairs_hbm, partner_hbm, decision_hbm, state_ref,
                comp_ref, ints_ref, pos_ref, vel_ref, charge_ref, mass_ref, centre_ref, width_ref,
                density_ref, error_ref, owners_ref, halo_ref, pairs_ref, partner_ref, decision_ref,
                sems):
    sources = (pos_hbm, vel_hbm, charge_hbm, mass_hbm, centre_hbm, width_hbm, density_hbm,
               error_hbm, owners_hbm, halo_hbm, pairs_hbm, partner_hbm, decision_hbm)
    targets = (pos_ref, vel_ref, charge_ref, mass_ref, centre_ref, width_ref, density_ref,
               error_ref, owners_ref, halo_ref, pairs_ref, partner_ref, decision_ref)
    copies = [
        pltpu.make_async_copy(source, target, sems.at[n])
        for n, (source, target) in enumerate(zip(sources, targets))
    ]
    for copy in copies:
        copy.start()
    for copy in copies:
        copy.wait()
    half = comp_ref.shape[2]
    for i in range(3):
        state_ref[i : i + 1, :] = pos_ref[i]
        state_ref[3 + i : 4 + i, :] = vel_ref[i]
    state_ref[6:7, :] = charge_ref[...]
    state_ref[7:8, :] = mass_ref[...]
    owned, own = owners_ref.shape
    _, sides, listed = halo_ref.shape
    ints_ref[...] = jnp.zeros_like(ints_ref)
    ints_ref[0:owned, 0:own] = owners_ref[...]
    ints_ref[owned : owned + sides, 0:listed] = halo_ref[0]
    last = owned + sides
    ints_ref[last : last + 1, 0 : partner_ref.shape[1]] = partner_ref[...]
    ints_ref[last + 1 : last + 2, 0 : decision_ref.shape[1]] = decision_ref[...]
    rows, near = pairs_ref.shape
    ints_ref[last + 2 : last + 2 + rows, 0:near] = pairs_ref[...]
    for row in range(comp_ref.shape[0]):
        part = pl.ds((row % CORES) * half, half)
        comp_ref[row, 0:3, :] = centre_ref[:, part]
        comp_ref[row, 3:4, :] = width_ref[:, part]
        comp_ref[row, 4:5, :] = density_ref[:, part]
        comp_ref[row, 5:6, :] = error_ref[:, part]


def choose_kernel(plan, ints_ref, mine_ref, *refs):
    others, out_ref = refs[:-1], refs[-1]
    row = lax.axis_index("rep")
    last = plan.owned + 2
    partner, decision = ints_ref[last : last + 1, :], ints_ref[last + 1 : last + 2, :]
    lane = lax.broadcasted_iota(jnp.int32, partner.shape, 1)
    sources = jnp.where(decision == 1, partner, lane)
    source = jnp.sum(jnp.where(lane == row, sources, 0).astype(f32), 1, keepdims=True)
    value = mine_ref[...]
    if len(others) == 1:
        for n in range(others[0].shape[0]):
            value = jnp.where(source == float(n), others[0][n], value)
    else:
        for n, other_ref in enumerate(others):
            other = jnp.bitwise_xor(row, n + 1).astype(f32)
            value = jnp.where(source == other, other_ref[...], value)
    out_ref[...] = value


def make_lists(plan, mine_ref, theirs_ref, out_ref, waiting):
    core = lax.axis_index("core")

    def clear(domain, carry):
        waiting[domain] = -1
        return carry

    lax.fori_loop(0, plan.domains, clear, 0)

    def one_tile(tile, count):
        row = lax.rem(tile, plan.own)
        here = lax.div(tile, plan.own) == core
        for j in range(plan.owned):
            owner = jnp.where(here, mine_ref[j, row], theirs_ref[j, row])
            first = waiting[owner]
            out_ref[0, count] = owner
            out_ref[1, count] = first
            out_ref[2, count] = tile
            count = count + jnp.where(first < 0, 0, 1)
            waiting[owner] = jnp.where(first < 0, tile, -1)
        return count

    count = lax.fori_loop(0, plan.tiles, one_tile, 0)

    def leftover(domain, count):
        first = waiting[domain]
        out_ref[0, count] = domain
        out_ref[1, count] = first
        out_ref[2, count] = plan.tiles
        return count + jnp.where(first < 0, 0, 1)

    count = lax.fori_loop(0, plan.domains, leftover, count)
    for extra in range(UNROLL - 1):
        out_ref[0, count + extra] = 0
        out_ref[1, count + extra] = plan.tiles
        out_ref[2, count + extra] = plan.tiles
    out_ref[3, 0] = lax.div(count + UNROLL - 1, UNROLL)
    for side in range(2):
        for k in range(plan.listed):
            out_ref[3, 1 + side * plan.listed + k] = theirs_ref[plan.owned + side, k]
    for tile in range(plan.own):
        for j in range(plan.near):
            out_ref[4 + j, tile] = mine_ref[plan.owned + 4 + tile, j]


def partner_tile(plan, lists_ref, side, k):
    core = lax.axis_index("core")
    return (1 - core) * plan.own + lists_ref[3, 1 + side * plan.listed + k]


def for_pairs(lists_ref, body):
    def step(n, carry):
        for u in range(UNROLL):
            place = n * UNROLL + u
            body(place, lists_ref[0, place], lists_ref[1, place], lists_ref[2, place])
        return carry

    lax.fori_loop(0, lists_ref[3, 0], step, 0)


def sum_gaussians(plan, scale, lists_ref, copy, state_ref, turned_ref, points_ref, out_ref, rim_ref, kept_ref,
                  xs, acc):
    tiles, listed, lanes = plan.tiles, plan.listed, plan.lanes
    store_rows(xs, point_rows([state_ref[i] for i in range(3)]))
    nowhere(xs, tiles)
    points_ref[...] = xs[...].astype(bf16)
    acc[...] = jnp.zeros_like(acc)
    if copy is not None:
        copy.wait()
    core = lax.axis_index("core")
    for k in range(listed):
        tile = partner_tile(plan, lists_ref, 1 - core, k)
        for i, row in enumerate((0, 1, 2, 6)):
            rim_ref[i * listed + k : i * listed + k + 1, :] = state_ref[row, pl.ds(tile, 1), :]

    def one_pair(place, owner, first, second):
        points = jnp.concatenate([points_ref[first], points_ref[second]], 1)
        for start, size in chunks(plan.half, CHUNK):
            part = slice(start, start + size)
            g = jnp.exp2(dot(turned_ref[owner, part, :], points))
            acc[owner, part, :] += g[:, :lanes] + g[:, lanes:]
            kept_ref[place, part, :] = g

    for_pairs(lists_ref, one_pair)
    for domain in range(plan.domains):
        for start, size in chunks(plan.half, lanes):
            total = jnp.sum(acc[domain, start : start + size, :].T, 0, keepdims=True)
            out_ref[domain : domain + 1, start : start + size] = total * scale


def first_kernel(plan, scale, ints_any, other_any, mine_ref, theirs_ref, comp_ref,
                 out_ref, rim_ref, state_ref, points_ref, kept_ref, turned_ref, lists_ref, xs, acc, cs,
                 ints, other_ints, waiting, sems):
    copies = [
        pltpu.make_async_copy(ints_any, ints, sems.at[0]),
        pltpu.make_async_copy(other_any, other_ints, sems.at[1]),
    ]
    for copy in copies:
        copy.start()
    core = lax.axis_index("core")
    for tile in range(plan.own):
        lanes = slice(tile * plan.lanes, (tile + 1) * plan.lanes)
        mine, theirs = mine_ref[:, lanes], theirs_ref[:, lanes]
        state_ref[:, tile, :] = jnp.where(core == 0, mine, theirs)
        state_ref[:, plan.own + tile, :] = jnp.where(core == 0, theirs, mine)
    store_rows(cs, centre_rows([comp_ref[:, i, :] for i in range(3)], comp_ref[:, 3, :]))
    for domain in range(plan.domains):
        for start, size in chunks(plan.half, 128):
            turned_ref[domain, start : start + size, :] = cs[
                domain, :, start : start + size
            ].T.astype(bf16)
    for copy in copies:
        copy.wait()
    make_lists(plan, ints, other_ints, lists_ref, waiting)
    sum_gaussians(plan, scale, lists_ref, None, state_ref, turned_ref, points_ref, out_ref, rim_ref, kept_ref,
                  xs, acc)


def stepped(old_ref, mine_ref, theirs_ref):
    mass = time_step * old_ref[7]
    for i in range(3):
        v = old_ref[3 + i] + mass * (mine_ref[i] + theirs_ref[i])
        yield old_ref[i] + time_step * v, v


def next_kernel(plan, scale, lists_any, old_ref, force_ref, swapped_ref, turned_ref,
                out_ref, rim_ref, state_ref, points_ref, kept_ref, xs, acc, lists_ref, sem):
    copy = pltpu.make_async_copy(lists_any, lists_ref, sem)
    copy.start()
    for i, (x, v) in enumerate(stepped(old_ref, force_ref, swapped_ref)):
        state_ref[i] = x
        state_ref[3 + i] = v
    state_ref[6] = old_ref[6]
    state_ref[7] = old_ref[7]
    sum_gaussians(plan, scale, lists_ref, copy, state_ref, turned_ref, points_ref, out_ref, rim_ref,
                  kept_ref, xs, acc)


def tree_sum(refs):
    values = [ref[...] for ref in refs]
    while len(values) > 1:
        values = [values[i] + values[i + 1] for i in range(0, len(values), 2)]
    return values[0]


def add_kernel(*refs):
    refs[-1][...] = tree_sum(refs[:-1])


def finish_kernel(plan, old_ref, mine_ref, theirs_ref, x_ref, v_ref, map_ref, state):
    for i, (x, v) in enumerate(stepped(old_ref, mine_ref, theirs_ref)):
        state[i] = x
        state[3 + i] = v
    core = lax.axis_index("core")
    base = core * plan.own
    for tile in range(plan.own):
        lanes = slice(tile * plan.lanes, (tile + 1) * plan.lanes)
        for i in range(3):
            x_ref[i, :, lanes] = state[i, pl.ds(base + tile, 1), :]
            v_ref[i, :, lanes] = state[3 + i, pl.ds(base + tile, 1), :]
    first = core == 0
    pieces = plan.half // plan.lanes
    for n in range(pieces):
        keep = mine_ref[3, n : n + 1, :]
        got = theirs_ref[3, pieces + n : pieces + n + 1, :]
        low = slice(n * plan.lanes, (n + 1) * plan.lanes)
        high = slice(plan.half + n * plan.lanes, plan.half + (n + 1) * plan.lanes)
        map_ref[:, low] = jnp.where(first, keep, got)
        map_ref[:, high] = jnp.where(first, got, keep)


def pair_kernel(plan, gain, lists_any, state_ref, far_ref, points_ref, out_ref, table, cs, rs, rows,
                turned, lists_ref, sem):
    copy = pltpu.make_async_copy(lists_any, lists_ref, sem)
    copy.start()
    own, near, listed = plan.own, plan.near, plan.listed
    core = lax.axis_index("core")
    base = pl.multiple_of(core * own, own)
    extent = own + 2 * listed
    table[...] = jnp.zeros_like(table)
    copy.wait()
    for i, source in enumerate((0, 1, 2, 6)):
        table[i, 0:own, :] = state_ref[source, pl.ds(base, own), :]
        for k in range(listed):
            table[i, pl.ds(own + (1 - core) * listed + k, 1), :] = state_ref[
                source, pl.ds(partner_tile(plan, lists_ref, core, k), 1), :
            ]
            table[i, pl.ds(own + core * listed + k, 1), :] = far_ref[
                i * listed + k : i * listed + k + 1, :
            ]
    coords = [table[i] for i in range(3)]
    store_rows(cs, centre_rows(coords, jnp.full_like(coords[0], pair_width)))
    store_rows(rs, pull_rows(coords, table[3]))
    rows[...] = rs[...].astype(bf16)
    for entry in range(extent + 1):
        turned[entry] = cs[entry].T.astype(bf16)
    for tile in range(own):
        points = points_ref[base + tile]
        entries = [lists_ref[4 + j, tile] for j in range(near)]
        entries = [jnp.where(entry < 0, extent, entry) for entry in entries]
        left = jnp.concatenate([turned[entry] for entry in entries], 0)
        weights = jnp.concatenate([rows[entry] for entry in entries], 1)
        high, low = high_low(jnp.exp2(dot(left, points)))
        sums = dot(weights, high) + dot(weights, low)
        coords = [state_ref[i, pl.ds(base + tile, 1), :] for i in range(3)]
        strength = gain / pair_width * state_ref[6, pl.ds(base + tile, 1), :]
        for i, push in enumerate(squeeze_sums(coords, sums)):
            out_ref[i, tile : tile + 1, :] = strength * push


def push_kernel(plan, gain, replicas, lists_any, state_ref, comp_ref, pair_ref, kept_ref, *refs):
    parts, (out_ref, rs, rows, means, sums, lists_ref, sem) = refs[:-7], refs[-7:]
    copy = pltpu.make_async_copy(lists_any, lists_ref, sem)
    copy.start()
    tiles, lanes = plan.tiles, plan.lanes
    mean = tree_sum(parts) / replicas
    for n in range(plan.half // lanes):
        means[n] = mean[:, n * lanes : (n + 1) * lanes]
    error = comp_ref[:, 5, :]
    coefficient = gain * (mean - comp_ref[:, 4, :]) / (error * error) / comp_ref[:, 3, :]
    store_rows(rs, pull_rows([comp_ref[:, i, :] for i in range(3)], coefficient))
    rows[...] = rs[...].astype(bf16)
    sums[...] = jnp.zeros_like(sums)
    copy.wait()

    def one_pair(place, owner, first, second):
        total = None
        for start, size in chunks(plan.half, CHUNK):
            part = slice(start, start + size)
            weights = rows[owner, :, part]
            high, low = high_low(kept_ref[place, part, :])
            term = dot(weights, high) + dot(weights, low)
            total = term if total is None else total + term
        sums[first] += total[:, :lanes]
        sums[second] += total[:, lanes:]

    for_pairs(lists_ref, one_pair)

    def added(row):
        return sums[0:tiles, row, :] + sums[0:tiles, row + 1, :] + sums[0:tiles, row + 2, :]

    strength = added(0)
    for i in range(3):
        out_ref[i] = state_ref[i] * strength - added(3 + 3 * i)
    core = lax.axis_index("core")
    own = pl.ds(pl.multiple_of(core * plan.own, plan.own), plan.own)
    for i in range(3):
        out_ref[i, own, :] += pair_ref[i]

    pieces = plan.half // lanes
    here = lax.axis_index("z") * CORES
    out_ref[3] = jnp.zeros_like(out_ref[3])
    for n in range(pieces):
        keep = means[n, pl.ds(here + core, 1), :]
        give = means[n, pl.ds(here + 1 - core, 1), :]
        out_ref[3, n : n + 1, :] = keep
        out_ref[3, pieces + n : pieces + n + 1, :] = give


VMEM = pl.BlockSpec(memory_space=pltpu.VMEM)
SMEM = pl.BlockSpec(memory_space=pltpu.SMEM)
HBM = pl.BlockSpec(memory_space=pltpu.HBM)
ANY = pl.BlockSpec(memory_space=pl.ANY)


def shape(*dims, dtype=f32):
    return jax.ShapeDtypeStruct(dims, dtype)


def with_types(scratch):
    for entry in scratch:
        if not isinstance(entry, tuple):
            yield entry
        else:
            dims, dtype = entry if isinstance(entry[0], tuple) else (entry, f32)
            yield pltpu.VMEM(dims, dtype)


def call(kernel, args, outs, scratch=(), limit=16, spaces=None, out_spaces=None):
    many = isinstance(outs, (list, tuple))
    return pl.pallas_call(
        kernel,
        out_shape=tuple(outs) if many else outs,
        in_specs=spaces or [VMEM] * len(args),
        out_specs=tuple(out_spaces or [VMEM] * len(outs)) if many else VMEM,
        scratch_shapes=list(with_types(scratch)),
        compiler_params=pltpu.CompilerParams(vmem_limit_bytes=limit << 20),
    )(*args)


class Plan:
    pass


def swap_cores(value):
    return lax.ppermute(value, "core", [(0, 1), (1, 0)])


def few(replicas, heights):
    return replicas in (2, 4) and heights in (2, 4)


def exchange(value, axis):
    count = lax.axis_size(axis)
    others = []
    for n in range(1, count):
        others.append(lax.ppermute(value, axis, [(i, i ^ n) for i in range(count)]))
    return others


def program(
    positions,
    velocities,
    charge,
    inverse_mass,
    pair_tiles,
    halo_tiles,
    owners,
    centres,
    widths,
    map_density,
    map_error,
    partner,
    decision,
):
    replicas = lax.axis_size("rep")
    heights = lax.axis_size("z")
    domains = heights * CORES
    own, owned = owners.shape
    plan = Plan()
    plan.own, plan.owned, plan.tiles, plan.domains = own, owned, own * CORES, domains
    plan.lanes = positions.shape[2] // own
    plan.near, plan.listed = pair_tiles.shape[1], halo_tiles.shape[2]
    components = widths.shape[0]
    half = plan.half = components // CORES
    tiles, lanes, listed = plan.tiles, plan.lanes, plan.listed

    args = [
        positions.transpose(1, 0, 2),
        velocities.transpose(1, 0, 2),
        charge[None],
        inverse_mass[None],
        centres,
        widths[None],
        map_density[None],
        map_error[None],
        owners.T,
        halo_tiles,
        pair_tiles,
        partner[None],
        decision[None],
    ]
    int_rows = -(-(owned + halo_tiles.shape[1] + 2 + own) // 8) * 8
    state_own, comp_send, ints = call(
        pack_kernel,
        [pltpu.with_memory_space_constraint(arg, pltpu.HBM) for arg in args],
        [shape(8, own * lanes), shape(domains, 6, half), shape(int_rows, lanes, dtype=jnp.int32)],
        [(arg.shape, arg.dtype) for arg in args] + [pltpu.SemaphoreType.DMA((len(args),))],
        limit=8,
        spaces=[HBM] * len(args),
    )
    comps = lax.all_to_all(comp_send, ("z", "core"), 0, 0, tiled=True)
    other_ints = swap_cores(ints)
    width = -(-((tiles * owned + domains) // 2 + UNROLL + 1) // lanes) * lanes
    lists_shape = shape(4 + plan.near, width, dtype=jnp.int32)
    scalars = [pltpu.SMEM(lists_shape.shape, jnp.int32), pltpu.SemaphoreType.DMA]
    small = few(replicas, heights)
    if small:
        others = exchange(state_own, "rep")
    else:
        others = [
            lax.all_to_all(
                jnp.broadcast_to(state_own[None], (replicas,) + state_own.shape),
                "rep", 0, 0, tiled=True,
            )
        ]
    chosen = call(
        functools.partial(choose_kernel, plan), [ints, state_own] + others, shape(8, own * lanes)
    )
    chosen_other = swap_cores(chosen)

    map_gain = map_scale / (owned * components)
    scale = 1.0 / (owned * own * lanes)
    pair_gain = (plan.near * lanes) ** (-0.5)
    group = replicas * heights
    rim_rows = -(-4 * listed // 8) * 8
    onward = [(2 * i, (2 * i + 2) % domains) for i in range(heights)]
    onward += [((2 * i + 3) % domains, 2 * i + 1) for i in range(heights)]
    padded = -(-(own + 2 * listed + 1) // 8) * 8
    most = (tiles * owned + domains) // 2 + UNROLL
    outs = [
        shape(domains, half),
        shape(rim_rows, lanes),
        shape(8, tiles, lanes),
        shape(tiles + 1, DEPTH, lanes, dtype=bf16),
        shape(most, half, 2 * lanes),
    ]
    scratch = [(tiles + 1, DEPTH, lanes), (domains, half, lanes)]
    for step in range(STEPS):
        if step == 0:
            partial, rim, state, points, kept, turned, lists = call(
                functools.partial(first_kernel, plan, scale),
                [ints, other_ints, chosen, chosen_other, comps],
                outs + [shape(domains, half, DEPTH, dtype=bf16), lists_shape],
                scratch
                + [(domains, DEPTH, half), pltpu.SMEM(ints.shape, jnp.int32),
                   pltpu.SMEM(ints.shape, jnp.int32), pltpu.SMEM((domains,), jnp.int32),
                   pltpu.SemaphoreType.DMA((2,))],
                spaces=[ANY, ANY] + [VMEM] * 3,
                out_spaces=[VMEM] * 6 + [SMEM],
            )
        else:
            partial, rim, state, points, kept = call(
                functools.partial(next_kernel, plan, scale),
                [lists, state, force, swapped, turned],
                outs,
                scratch + scalars,
                spaces=[ANY] + [VMEM] * 4,
            )
        far = lax.ppermute(rim, ("z", "core"), onward)
        if small:
            partial = call(add_kernel, [partial] + exchange(partial, "rep"), shape(domains, half))
            parts = [partial] + exchange(partial, "z")
        else:
            pieces = lax.all_to_all(partial.reshape(group, -1), ("rep", "z"), 0, 0, tiled=True)
            piece = jnp.sum(pieces, 0)
            parts = [
                lax.all_to_all(
                    jnp.broadcast_to(piece[None], (group,) + piece.shape),
                    ("rep", "z"), 0, 0, tiled=True,
                ).reshape(domains, half)
            ]
        pair = call(
            functools.partial(pair_kernel, plan, pair_gain),
            [lists, state, far, points],
            shape(3, own, lanes),
            [(4, padded, lanes), (padded, DEPTH, lanes), (padded, ROWS, lanes),
             ((padded, ROWS, lanes), bf16), ((padded, lanes, DEPTH), bf16)] + scalars,
            spaces=[ANY] + [VMEM] * 3,
        )
        force = call(
            functools.partial(push_kernel, plan, map_gain, float(replicas)),
            [lists, state, comps, pair, kept] + parts,
            shape(4, tiles, lanes),
            [(domains, ROWS, half), ((domains, ROWS, half), bf16), (half // lanes, domains, lanes),
             (tiles + 1, ROWS, lanes)] + scalars,
            spaces=[ANY] + [VMEM] * (4 + len(parts)),
        )
        swapped = swap_cores(force)

    new_x, new_v, model_map = call(
        functools.partial(finish_kernel, plan),
        [state, force, swapped],
        [shape(3, 1, own * lanes), shape(3, 1, own * lanes), shape(1, components)],
        [(6, tiles, lanes)],
    )
    return (new_x.transpose(1, 0, 2), new_v.transpose(1, 0, 2), model_map.reshape(components))


def solution(mesh):
    replicas, domains = mesh.devices.shape
    split = Mesh(
        mesh.devices.reshape(replicas, domains // CORES, CORES), ("rep", "z", "core")
    )
    dom = ("z", "core")
    placed = (
        P("rep", None, dom),
        P("rep", None, dom),
        P(dom),
        P(dom),
        P(dom, None),
        P(dom, None, None),
        P(dom, None),
        P(None, dom),
        P(dom),
        P(dom),
        P(dom),
        P(),
        P(),
    )
    return jax.shard_map(
        program,
        mesh=split,
        in_specs=placed,
        out_specs=(P("rep", None, dom), P("rep", None, dom), P(dom)),
        check_vma=False,
    )
```

```python
import functools
import math

import jax
import jax.numpy as jnp
from jax import lax
from jax.experimental import pallas as pl
from jax.experimental.pallas import tpu as pltpu
from jax.sharding import Mesh, PartitionSpec as P

STEPS = 2
CORES = 2
DEPTH = 32
ROWS = 16
CHUNK = 256
UNROLL = 4
FAR_SQUARE = 1048576.0

time_step = 0.5
pair_width = 1.0
map_scale = 2.0
log2e = math.log2(math.e)
f32 = jnp.float32
bf16 = jnp.bfloat16

LEFT_PARTS = (0, 0, 1, 1, 0, 2)
RIGHT_PARTS = (0, 1, 0, 1, 2, 0)


def split3(value):
    high = value.astype(bf16).astype(f32)
    rest = value - high
    middle = rest.astype(bf16).astype(f32)
    return high, middle, rest - middle


def point_rows(coords):
    rows = []
    for coord in coords:
        parts = split3(coord)
        rows += [parts[i] for i in LEFT_PARTS]
    parts = split3(coords[0] * coords[0] + coords[1] * coords[1] + coords[2] * coords[2])
    rows += [parts[i] for i in LEFT_PARTS]
    one = jnp.ones_like(coords[0])
    return rows + [one, one, one]


def nowhere(ref, tile):
    shape = ref.shape[1:]
    row = lax.broadcasted_iota(jnp.int32, shape, 0)
    square = len(LEFT_PARTS) * 3
    ref[tile] = jnp.where(row == square, FAR_SQUARE, 0.0)


def centre_rows(coords, extent):
    scale = log2e / extent
    rows = []
    for coord in coords:
        parts = split3(coord * scale)
        rows += [parts[i] for i in RIGHT_PARTS]
    parts = split3(-0.5 * scale)
    rows += [parts[i] for i in RIGHT_PARTS]
    square = coords[0] * coords[0] + coords[1] * coords[1] + coords[2] * coords[2]
    return rows + list(split3(-0.5 * scale * square))


def pull_rows(coords, weight):
    rows = list(split3(weight))
    for coord in coords:
        rows += list(split3(coord * weight))
    return rows


def squeeze_sums(coords, sums):
    def total(first):
        return sums[first : first + 1] + sums[first + 1 : first + 2] + sums[first + 2 : first + 3]

    strength = total(0)
    return [coords[i] * strength - total(3 + 3 * i) for i in range(3)]


def dot(left, right):
    return jnp.dot(left, right, preferred_element_type=f32)


def high_low(value):
    high = value.astype(bf16)
    return high, (value - high.astype(f32)).astype(bf16)


def store_rows(ref, rows):
    count, depth, width = rows[0].shape[0], ref.shape[1], ref.shape[2]
    for index, row in enumerate(rows):
        ref[0:count, index, :] = row
    if len(rows) < depth:
        ref[0:count, len(rows) : depth, :] = jnp.zeros((count, depth - len(rows), width), f32)


def chunks(total, wanted):
    size = wanted if total % wanted == 0 else total
    return [(start, size) for start in range(0, total, size)]


def pack_kernel(pos_hbm, vel_hbm, charge_hbm, mass_hbm, centre_hbm, width_hbm, density_hbm,
                error_hbm, owners_hbm, halo_hbm, pairs_hbm, partner_hbm, decision_hbm, keep_ref,
                give_ref, ints_ref, pos_ref, vel_ref, charge_ref, mass_ref, centre_ref, width_ref,
                density_ref, error_ref, owners_ref, halo_ref, pairs_ref, partner_ref, decision_ref,
                sems):
    sources = (pos_hbm, vel_hbm, charge_hbm, mass_hbm, centre_hbm, width_hbm, density_hbm,
               error_hbm, owners_hbm, halo_hbm, pairs_hbm, partner_hbm, decision_hbm)
    targets = (pos_ref, vel_ref, charge_ref, mass_ref, centre_ref, width_ref, density_ref,
               error_ref, owners_ref, halo_ref, pairs_ref, partner_ref, decision_ref)
    copies = [
        pltpu.make_async_copy(source, target, sems.at[n])
        for n, (source, target) in enumerate(zip(sources, targets))
    ]
    for copy in copies:
        copy.start()
    for copy in copies:
        copy.wait()
    owned, own = owners_ref.shape
    _, sides, listed = halo_ref.shape
    ints_ref[...] = jnp.zeros_like(ints_ref)
    ints_ref[0:owned, 0:own] = owners_ref[...]
    ints_ref[owned : owned + sides, 0:listed] = halo_ref[0]
    last = owned + sides
    ints_ref[last : last + 1, 0 : partner_ref.shape[1]] = partner_ref[...]
    ints_ref[last + 1 : last + 2, 0 : decision_ref.shape[1]] = decision_ref[...]
    rows, near = pairs_ref.shape
    ints_ref[last + 2 : last + 2 + rows, 0:near] = pairs_ref[...]
    core = lax.axis_index("core")
    atoms, half = pos_ref.shape[2], centre_ref.shape[1] // CORES
    for out_ref, part in ((keep_ref, core), (give_ref, 1 - core)):
        for i in range(3):
            out_ref[i : i + 1, 0:atoms] = pos_ref[i]
            out_ref[3 + i : 4 + i, 0:atoms] = vel_ref[i]
        out_ref[6:7, 0:atoms] = charge_ref[...]
        out_ref[7:8, 0:atoms] = mass_ref[...]
        for core_of_half in range(CORES):

            @pl.when(part == core_of_half)
            def _():
                lanes = slice(core_of_half * half, (core_of_half + 1) * half)
                out_ref[0:3, atoms : atoms + half] = centre_ref[:, lanes]
                out_ref[3:4, atoms : atoms + half] = width_ref[:, lanes]
                out_ref[4:5, atoms : atoms + half] = density_ref[:, lanes]
                out_ref[5:6, atoms : atoms + half] = error_ref[:, lanes]
                out_ref[6:8, atoms : atoms + half] = jnp.zeros((2, half), f32)

        for block in range(ints_ref.shape[0] // 8):
            first = atoms + half + block * ints_ref.shape[1]
            out_ref[:, first : first + ints_ref.shape[1]] = ints_ref[
                block * 8 : (block + 1) * 8, :
            ].astype(f32)


def join_kernel(keep_ref, got_ref, state_ref, comp_ref, other_ref):
    core = lax.axis_index("core")
    atoms, half, lanes = state_ref.shape[2], comp_ref.shape[2], other_ref.shape[1]
    for place in range(CORES):
        mine = core == place
        state_ref[place] = jnp.where(mine, keep_ref[:, 0:atoms], got_ref[:, 0:atoms])
        part = slice(atoms, atoms + half)
        comp_ref[place] = jnp.where(mine, keep_ref[:, part], got_ref[:, part])
    for block in range(other_ref.shape[0] // 8):
        first = atoms + half + block * lanes
        other_ref[block * 8 : (block + 1) * 8, :] = got_ref[:, first : first + lanes].astype(jnp.int32)


def chosen(plan, ints_ref, refs):
    mine_ref, others = refs[0], refs[1:]
    row = lax.axis_index("rep")
    last = plan.owned + 2
    partner, decision = ints_ref[last : last + 1, :], ints_ref[last + 1 : last + 2, :]
    lane = lax.broadcasted_iota(jnp.int32, partner.shape, 1)
    sources = jnp.where(decision == 1, partner, lane)
    source = jnp.sum(jnp.where(lane == row, sources, 0).astype(f32), 1, keepdims=True)

    def read(*place):
        value = mine_ref[place]
        if plan.few:
            for n, other_ref in enumerate(others):
                other = jnp.bitwise_xor(row, n + 1).astype(f32)
                value = jnp.where(source == other, other_ref[place], value)
        else:
            for n in range(others[0].shape[0]):
                value = jnp.where(source == float(n), others[0][(n,) + place], value)
        return value

    return read


def make_lists(plan, mine_ref, theirs_ref, out_ref, waiting):
    core = lax.axis_index("core")

    def clear(domain, carry):
        waiting[domain] = -1
        return carry

    lax.fori_loop(0, plan.domains, clear, 0)

    def one_tile(tile, count):
        row = lax.rem(tile, plan.own)
        here = lax.div(tile, plan.own) == core
        for j in range(plan.owned):
            owner = jnp.where(here, mine_ref[j, row], theirs_ref[j, row])
            first = waiting[owner]
            out_ref[0, count] = owner
            out_ref[1, count] = first
            out_ref[2, count] = tile
            count = count + jnp.where(first < 0, 0, 1)
            waiting[owner] = jnp.where(first < 0, tile, -1)
        return count

    count = lax.fori_loop(0, plan.tiles, one_tile, 0)

    def leftover(domain, count):
        first = waiting[domain]
        out_ref[0, count] = domain
        out_ref[1, count] = first
        out_ref[2, count] = plan.tiles
        return count + jnp.where(first < 0, 0, 1)

    count = lax.fori_loop(0, plan.domains, leftover, count)
    for extra in range(UNROLL - 1):
        out_ref[0, count + extra] = 0
        out_ref[1, count + extra] = plan.tiles
        out_ref[2, count + extra] = plan.tiles
    out_ref[3, 0] = lax.div(count + UNROLL - 1, UNROLL)
    for side in range(2):
        for k in range(plan.listed):
            out_ref[3, 1 + side * plan.listed + k] = theirs_ref[plan.owned + side, k]
    for tile in range(plan.own):
        for j in range(plan.near):
            out_ref[4 + j, tile] = mine_ref[plan.owned + 4 + tile, j]


def partner_tile(plan, lists_ref, side, k):
    core = lax.axis_index("core")
    return (1 - core) * plan.own + lists_ref[3, 1 + side * plan.listed + k]


def for_pairs(lists_ref, body):
    def step(n, carry):
        for u in range(UNROLL):
            place = n * UNROLL + u
            body(place, lists_ref[0, place], lists_ref[1, place], lists_ref[2, place])
        return carry

    lax.fori_loop(0, lists_ref[3, 0], step, 0)


def sum_gaussians(plan, scale, lists_ref, copy, state_ref, turned_ref, points_ref, out_ref, rim_ref, kept_ref,
                  xs, acc):
    tiles, listed, lanes = plan.tiles, plan.listed, plan.lanes
    store_rows(xs, point_rows([state_ref[i] for i in range(3)]))
    nowhere(xs, tiles)
    points_ref[...] = xs[...].astype(bf16)
    acc[...] = jnp.zeros_like(acc)
    copy.wait()
    core = lax.axis_index("core")
    for k in range(listed):
        tile = partner_tile(plan, lists_ref, 1 - core, k)
        for i, row in enumerate((0, 1, 2, 6)):
            rim_ref[i * listed + k : i * listed + k + 1, :] = state_ref[row, pl.ds(tile, 1), :]

    def one_pair(place, owner, first, second):
        points = jnp.concatenate([points_ref[first], points_ref[second]], 1)
        for start, size in chunks(plan.half, CHUNK):
            part = slice(start, start + size)
            g = jnp.exp2(dot(turned_ref[owner, part, :], points))
            acc[owner, part, :] += g[:, :lanes] + g[:, lanes:]
            kept_ref[place, part, :] = g

    for_pairs(lists_ref, one_pair)
    square = (lanes, lanes)
    diagonal = lax.broadcasted_iota(jnp.int32, square, 0) == lax.broadcasted_iota(jnp.int32, square, 1)
    for domain in range(plan.domains):
        for start, size in chunks(plan.half, lanes):
            column = jnp.sum(acc[domain, start : start + size, :], 1, keepdims=True)
            total = jnp.sum(jnp.where(diagonal, column, 0.0), 0, keepdims=True)
            out_ref[domain : domain + 1, start : start + size] = total * scale


def prepare_kernel(plan, ints_any, other_any, *refs):
    parts, (comp_ref, turned_ref, lists_ref, cs, ints, other_ints, waiting, sems) = refs[:-8], refs[-8:]
    copies = [
        pltpu.make_async_copy(ints_any, ints, sems.at[0]),
        pltpu.make_async_copy(other_any, other_ints, sems.at[1]),
    ]
    for copy in copies:
        copy.start()
    height = lax.axis_index("z")
    for core in range(CORES):
        if plan.few:
            for n, part_ref in enumerate(parts):
                comp_ref[jnp.bitwise_xor(height, n) * CORES + core] = part_ref[core]
        else:
            for n in range(parts[1].shape[0]):
                comp_ref[n * CORES + core] = parts[1][n, core]
    store_rows(cs, centre_rows([comp_ref[:, i, :] for i in range(3)], comp_ref[:, 3, :]))
    for domain in range(plan.domains):
        for start, size in chunks(plan.half, 128):
            turned_ref[domain, start : start + size, :] = cs[
                domain, :, start : start + size
            ].T.astype(bf16)
    for copy in copies:
        copy.wait()
    make_lists(plan, ints, other_ints, lists_ref, waiting)


def first_kernel(plan, scale, lists_any, ints_ref, turned_ref, *refs):
    copies_of_state, refs = refs[:-9], refs[-9:]
    out_ref, rim_ref, state_ref, points_ref, kept_ref, xs, acc, lists_ref, sem = refs
    copy = pltpu.make_async_copy(lists_any, lists_ref, sem)
    copy.start()
    read = chosen(plan, ints_ref, copies_of_state)
    for core in range(CORES):
        for tile in range(plan.own):
            lanes = slice(tile * plan.lanes, (tile + 1) * plan.lanes)
            state_ref[:, core * plan.own + tile, :] = read(core, slice(None), lanes)
    sum_gaussians(plan, scale, lists_ref, copy, state_ref, turned_ref, points_ref, out_ref, rim_ref,
                  kept_ref, xs, acc)


def stepped(old_ref, mine_ref, theirs_ref):
    mass = time_step * old_ref[7]
    for i in range(3):
        v = old_ref[3 + i] + mass * (mine_ref[i] + theirs_ref[i])
        yield old_ref[i] + time_step * v, v


def next_kernel(plan, scale, lists_any, old_ref, force_ref, swapped_ref, turned_ref,
                out_ref, rim_ref, state_ref, points_ref, kept_ref, xs, acc, lists_ref, sem):
    copy = pltpu.make_async_copy(lists_any, lists_ref, sem)
    copy.start()
    for i, (x, v) in enumerate(stepped(old_ref, force_ref, swapped_ref)):
        state_ref[i] = x
        state_ref[3 + i] = v
    state_ref[6] = old_ref[6]
    state_ref[7] = old_ref[7]
    sum_gaussians(plan, scale, lists_ref, copy, state_ref, turned_ref, points_ref, out_ref, rim_ref,
                  kept_ref, xs, acc)


def tree_sum(refs):
    values = [ref[...] for ref in refs]
    while len(values) > 1:
        values = [values[i] + values[i + 1] for i in range(0, len(values), 2)]
    return values[0]


def add_kernel(*refs):
    refs[-1][...] = tree_sum(refs[:-1])


def finish_kernel(plan, old_ref, mine_ref, theirs_ref, x_ref, v_ref, map_ref, state):
    for i, (x, v) in enumerate(stepped(old_ref, mine_ref, theirs_ref)):
        state[i] = x
        state[3 + i] = v
    core = lax.axis_index("core")
    base = core * plan.own
    for tile in range(plan.own):
        lanes = slice(tile * plan.lanes, (tile + 1) * plan.lanes)
        for i in range(3):
            x_ref[i, :, lanes] = state[i, pl.ds(base + tile, 1), :]
            v_ref[i, :, lanes] = state[3 + i, pl.ds(base + tile, 1), :]
    first = core == 0
    pieces = plan.half // plan.lanes
    for n in range(pieces):
        keep = mine_ref[3, n : n + 1, :]
        got = theirs_ref[3, pieces + n : pieces + n + 1, :]
        low = slice(n * plan.lanes, (n + 1) * plan.lanes)
        high = slice(plan.half + n * plan.lanes, plan.half + (n + 1) * plan.lanes)
        map_ref[:, low] = jnp.where(first, keep, got)
        map_ref[:, high] = jnp.where(first, got, keep)


def pair_kernel(plan, gain, lists_any, state_ref, far_ref, points_ref, out_ref, table, cs, rs, rows,
                turned, lists_ref, sem):
    copy = pltpu.make_async_copy(lists_any, lists_ref, sem)
    copy.start()
    own, near, listed = plan.own, plan.near, plan.listed
    core = lax.axis_index("core")
    base = pl.multiple_of(core * own, own)
    extent = own + 2 * listed
    table[...] = jnp.zeros_like(table)
    copy.wait()
    for i, source in enumerate((0, 1, 2, 6)):
        table[i, 0:own, :] = state_ref[source, pl.ds(base, own), :]
        for k in range(listed):
            table[i, pl.ds(own + (1 - core) * listed + k, 1), :] = state_ref[
                source, pl.ds(partner_tile(plan, lists_ref, core, k), 1), :
            ]
            table[i, pl.ds(own + core * listed + k, 1), :] = far_ref[
                i * listed + k : i * listed + k + 1, :
            ]
    coords = [table[i] for i in range(3)]
    store_rows(cs, centre_rows(coords, jnp.full_like(coords[0], pair_width)))
    store_rows(rs, pull_rows(coords, table[3]))
    rows[...] = rs[...].astype(bf16)
    for entry in range(extent + 1):
        turned[entry] = cs[entry].T.astype(bf16)
    for tile in range(own):
        points = points_ref[base + tile]
        entries = [lists_ref[4 + j, tile] for j in range(near)]
        entries = [jnp.where(entry < 0, extent, entry) for entry in entries]
        left = jnp.concatenate([turned[entry] for entry in entries], 0)
        weights = jnp.concatenate([rows[entry] for entry in entries], 1)
        high, low = high_low(jnp.exp2(dot(left, points)))
        sums = dot(weights, high) + dot(weights, low)
        coords = [state_ref[i, pl.ds(base + tile, 1), :] for i in range(3)]
        strength = gain / pair_width * state_ref[6, pl.ds(base + tile, 1), :]
        for i, push in enumerate(squeeze_sums(coords, sums)):
            out_ref[i, tile : tile + 1, :] = strength * push


def push_kernel(plan, gain, replicas, lists_any, state_ref, comp_ref, pair_ref, kept_ref, *refs):
    parts, (out_ref, rs, rows, means, sums, lists_ref, sem) = refs[:-7], refs[-7:]
    copy = pltpu.make_async_copy(lists_any, lists_ref, sem)
    copy.start()
    tiles, lanes = plan.tiles, plan.lanes
    mean = tree_sum(parts) / replicas
    for n in range(plan.half // lanes):
        means[n] = mean[:, n * lanes : (n + 1) * lanes]
    error = comp_ref[:, 5, :]
    coefficient = gain * (mean - comp_ref[:, 4, :]) / (error * error) / comp_ref[:, 3, :]
    store_rows(rs, pull_rows([comp_ref[:, i, :] for i in range(3)], coefficient))
    rows[...] = rs[...].astype(bf16)
    sums[...] = jnp.zeros_like(sums)
    copy.wait()

    def one_pair(place, owner, first, second):
        total = None
        for start, size in chunks(plan.half, CHUNK):
            part = slice(start, start + size)
            weights = rows[owner, :, part]
            high, low = high_low(kept_ref[place, part, :])
            term = dot(weights, high) + dot(weights, low)
            total = term if total is None else total + term
        sums[first] += total[:, :lanes]
        sums[second] += total[:, lanes:]

    for_pairs(lists_ref, one_pair)

    def added(row):
        return sums[0:tiles, row, :] + sums[0:tiles, row + 1, :] + sums[0:tiles, row + 2, :]

    strength = added(0)
    for i in range(3):
        out_ref[i] = state_ref[i] * strength - added(3 + 3 * i)
    core = lax.axis_index("core")
    own = pl.ds(pl.multiple_of(core * plan.own, plan.own), plan.own)
    for i in range(3):
        out_ref[i, own, :] += pair_ref[i]

    pieces = plan.half // lanes
    here = lax.axis_index("z") * CORES
    out_ref[3] = jnp.zeros_like(out_ref[3])
    for n in range(pieces):
        keep = means[n, pl.ds(here + core, 1), :]
        give = means[n, pl.ds(here + 1 - core, 1), :]
        out_ref[3, n : n + 1, :] = keep
        out_ref[3, pieces + n : pieces + n + 1, :] = give


VMEM = pl.BlockSpec(memory_space=pltpu.VMEM)
SMEM = pl.BlockSpec(memory_space=pltpu.SMEM)
HBM = pl.BlockSpec(memory_space=pltpu.HBM)
ANY = pl.BlockSpec(memory_space=pl.ANY)


def shape(*dims, dtype=f32):
    return jax.ShapeDtypeStruct(dims, dtype)


def with_types(scratch):
    for entry in scratch:
        if not isinstance(entry, tuple):
            yield entry
        else:
            dims, dtype = entry if isinstance(entry[0], tuple) else (entry, f32)
            yield pltpu.VMEM(dims, dtype)


def call(kernel, args, outs, scratch=(), limit=16, spaces=None, out_spaces=None):
    many = isinstance(outs, (list, tuple))
    return pl.pallas_call(
        kernel,
        out_shape=tuple(outs) if many else outs,
        in_specs=spaces or [VMEM] * len(args),
        out_specs=tuple(out_spaces or [VMEM] * len(outs)) if many else VMEM,
        scratch_shapes=list(with_types(scratch)),
        compiler_params=pltpu.CompilerParams(vmem_limit_bytes=limit << 20),
    )(*args)


class Plan:
    pass


def swap_cores(value):
    return lax.ppermute(value, "core", [(0, 1), (1, 0)])


def few(replicas, heights):
    return replicas in (2, 4) and heights in (2, 4)


def stages(replicas, heights):
    return [("rep", list(range(1, replicas))), ("z", list(range(1, heights)))]


def exchange(value, axis, places):
    count = lax.axis_size(axis)
    others = []
    for n in places:
        others.append(lax.ppermute(value, axis, [(i, i ^ n) for i in range(count)]))
    return others


def everywhere(value, axis):
    copies = jnp.broadcast_to(value[None], (lax.axis_size(axis),) + value.shape)
    return lax.all_to_all(copies, axis, 0, 0, tiled=True)


def program(
    positions,
    velocities,
    charge,
    inverse_mass,
    pair_tiles,
    halo_tiles,
    owners,
    centres,
    widths,
    map_density,
    map_error,
    partner,
    decision,
):
    replicas = lax.axis_size("rep")
    heights = lax.axis_size("z")
    domains = heights * CORES
    own, owned = owners.shape
    plan = Plan()
    plan.own, plan.owned, plan.tiles, plan.domains = own, owned, own * CORES, domains
    plan.lanes = positions.shape[2] // own
    plan.near, plan.listed = pair_tiles.shape[1], halo_tiles.shape[2]
    components = widths.shape[0]
    half = plan.half = components // CORES
    tiles, lanes, listed = plan.tiles, plan.lanes, plan.listed

    args = [
        positions.transpose(1, 0, 2),
        velocities.transpose(1, 0, 2),
        charge[None],
        inverse_mass[None],
        centres,
        widths[None],
        map_density[None],
        map_error[None],
        owners.T,
        halo_tiles,
        pair_tiles,
        partner[None],
        decision[None],
    ]
    int_rows = -(-(owned + halo_tiles.shape[1] + 2 + own) // 8) * 8
    wide = own * lanes + half + int_rows // 8 * lanes
    keep, give, ints = call(
        pack_kernel,
        [pltpu.with_memory_space_constraint(arg, pltpu.HBM) for arg in args],
        [shape(8, wide), shape(8, wide), shape(int_rows, lanes, dtype=jnp.int32)],
        [(arg.shape, arg.dtype) for arg in args] + [pltpu.SemaphoreType.DMA((len(args),))],
        limit=8,
        spaces=[HBM] * len(args),
    )
    both_state, both_comps, other_ints = call(
        join_kernel,
        [keep, swap_cores(give)],
        [shape(CORES, 8, own * lanes), shape(CORES, 8, half),
         shape(int_rows, lanes, dtype=jnp.int32)],
    )
    plan.few = few(replicas, heights)
    if plan.few:
        comp_parts = [both_comps] + exchange(both_comps, "z", range(1, heights))
        states = [both_state] + exchange(both_state, "rep", range(1, replicas))
    else:
        comp_parts = [both_comps, everywhere(both_comps, "z")]
        states = [both_state, everywhere(both_state, "rep")]
    width = -(-((tiles * owned + domains) // 2 + UNROLL + 1) // lanes) * lanes
    lists_shape = shape(4 + plan.near, width, dtype=jnp.int32)
    scalars = [pltpu.SMEM(lists_shape.shape, jnp.int32), pltpu.SemaphoreType.DMA]
    comps, turned, lists = call(
        functools.partial(prepare_kernel, plan),
        [ints, other_ints] + comp_parts,
        [shape(domains, 8, half), shape(domains, half, DEPTH, dtype=bf16), lists_shape],
        [(domains, DEPTH, half), pltpu.SMEM(ints.shape, jnp.int32),
         pltpu.SMEM(ints.shape, jnp.int32), pltpu.SMEM((domains,), jnp.int32),
         pltpu.SemaphoreType.DMA((2,))],
        spaces=[ANY, ANY] + [VMEM] * len(comp_parts),
        out_spaces=[VMEM, VMEM, SMEM],
    )

    map_gain = map_scale / (owned * components)
    scale = 1.0 / (owned * own * lanes)
    pair_gain = (plan.near * lanes) ** (-0.5)
    group = replicas * heights
    rim_rows = -(-4 * listed // 8) * 8
    onward = [(2 * i, (2 * i + 2) % domains) for i in range(heights)]
    onward += [((2 * i + 3) % domains, 2 * i + 1) for i in range(heights)]
    padded = -(-(own + 2 * listed + 1) // 8) * 8
    most = (tiles * owned + domains) // 2 + UNROLL
    outs = [
        shape(domains, half),
        shape(rim_rows, lanes),
        shape(8, tiles, lanes),
        shape(tiles + 1, DEPTH, lanes, dtype=bf16),
        shape(most, half, 2 * lanes),
    ]
    scratch = [(tiles + 1, DEPTH, lanes), (domains, half, lanes)]
    for step in range(STEPS):
        if step == 0:
            partial, rim, state, points, kept = call(
                functools.partial(first_kernel, plan, scale),
                [lists, ints, turned] + states,
                outs,
                scratch + scalars,
                spaces=[ANY] + [VMEM] * (2 + len(states)),
            )
        else:
            partial, rim, state, points, kept = call(
                functools.partial(next_kernel, plan, scale),
                [lists, state, force, swapped, turned],
                outs,
                scratch + scalars,
                spaces=[ANY] + [VMEM] * 4,
            )
        far = lax.ppermute(rim, ("z", "core"), onward)
        if plan.few:
            for number, (axis, places) in enumerate(stages(replicas, heights)):
                if number > 0:
                    partial = call(add_kernel, parts, shape(domains, half))
                parts = [partial] + exchange(partial, axis, places)
        else:
            pieces = lax.all_to_all(partial.reshape(group, -1), ("rep", "z"), 0, 0, tiled=True)
            piece = jnp.sum(pieces, 0)
            parts = [
                lax.all_to_all(
                    jnp.broadcast_to(piece[None], (group,) + piece.shape),
                    ("rep", "z"), 0, 0, tiled=True,
                ).reshape(domains, half)
            ]
        pair = call(
            functools.partial(pair_kernel, plan, pair_gain),
            [lists, state, far, points],
            shape(3, own, lanes),
            [(4, padded, lanes), (padded, DEPTH, lanes), (padded, ROWS, lanes),
             ((padded, ROWS, lanes), bf16), ((padded, lanes, DEPTH), bf16)] + scalars,
            spaces=[ANY] + [VMEM] * 3,
        )
        force = call(
            functools.partial(push_kernel, plan, map_gain, float(replicas)),
            [lists, state, comps, pair, kept] + parts,
            shape(4, tiles, lanes),
            [(domains, ROWS, half), ((domains, ROWS, half), bf16), (half // lanes, domains, lanes),
             (tiles + 1, ROWS, lanes)] + scalars,
            spaces=[ANY] + [VMEM] * (4 + len(parts)),
        )
        swapped = swap_cores(force)

    new_x, new_v, model_map = call(
        functools.partial(finish_kernel, plan),
        [state, force, swapped],
        [shape(3, 1, own * lanes), shape(3, 1, own * lanes), shape(1, components)],
        [(6, tiles, lanes)],
    )
    return (new_x.transpose(1, 0, 2), new_v.transpose(1, 0, 2), model_map.reshape(components))


def solution(mesh):
    replicas, domains = mesh.devices.shape
    split = Mesh(
        mesh.devices.reshape(replicas, domains // CORES, CORES), ("rep", "z", "core")
    )
    dom = ("z", "core")
    placed = (
        P("rep", None, dom),
        P("rep", None, dom),
        P(dom),
        P(dom),
        P(dom, None),
        P(dom, None, None),
        P(dom, None),
        P(None, dom),
        P(dom),
        P(dom),
        P(dom),
        P(),
        P(),
    )
    return jax.shard_map(
        program,
        mesh=split,
        in_specs=placed,
        out_specs=(P("rep", None, dom), P("rep", None, dom), P(dom)),
        check_vma=False,
    )
```

```python
import functools
import math

import jax
import jax.numpy as jnp
from jax import lax
from jax.experimental import pallas as pl
from jax.experimental.pallas import tpu as pltpu
from jax.sharding import Mesh, PartitionSpec as P

STEPS = 2
CORES = 2
DEPTH = 32
ROWS = 16
CHUNK = 256
UNROLL = 4
FAR_SQUARE = 1048576.0

time_step = 0.5
pair_width = 1.0
map_scale = 2.0
log2e = math.log2(math.e)
f32 = jnp.float32
bf16 = jnp.bfloat16

LEFT_PARTS = (0, 0, 1, 1, 0, 2)
RIGHT_PARTS = (0, 1, 0, 1, 2, 0)


def split3(value):
    high = value.astype(bf16).astype(f32)
    rest = value - high
    middle = rest.astype(bf16).astype(f32)
    return high, middle, rest - middle


def point_rows(coords):
    rows = []
    for coord in coords:
        parts = split3(coord)
        rows += [parts[i] for i in LEFT_PARTS]
    parts = split3(coords[0] * coords[0] + coords[1] * coords[1] + coords[2] * coords[2])
    rows += [parts[i] for i in LEFT_PARTS]
    one = jnp.ones_like(coords[0])
    return rows + [one, one, one]


def nowhere(ref, tile):
    shape = ref.shape[1:]
    row = lax.broadcasted_iota(jnp.int32, shape, 0)
    square = len(LEFT_PARTS) * 3
    ref[tile] = jnp.where(row == square, FAR_SQUARE, 0.0)


def centre_rows(coords, extent):
    scale = log2e / extent
    rows = []
    for coord in coords:
        parts = split3(coord * scale)
        rows += [parts[i] for i in RIGHT_PARTS]
    parts = split3(-0.5 * scale)
    rows += [parts[i] for i in RIGHT_PARTS]
    square = coords[0] * coords[0] + coords[1] * coords[1] + coords[2] * coords[2]
    return rows + list(split3(-0.5 * scale * square))


def pull_rows(coords, weight):
    rows = list(split3(weight))
    for coord in coords:
        rows += list(split3(coord * weight))
    return rows


def squeeze_sums(coords, sums):
    def total(first):
        return sums[first : first + 1] + sums[first + 1 : first + 2] + sums[first + 2 : first + 3]

    strength = total(0)
    return [coords[i] * strength - total(3 + 3 * i) for i in range(3)]


def dot(left, right):
    return jnp.dot(left, right, preferred_element_type=f32)


def high_low(value):
    high = value.astype(bf16)
    return high, (value - high.astype(f32)).astype(bf16)


def store_rows(ref, rows):
    count, depth, width = rows[0].shape[0], ref.shape[1], ref.shape[2]
    for index, row in enumerate(rows):
        ref[0:count, index, :] = row
    if len(rows) < depth:
        ref[0:count, len(rows) : depth, :] = jnp.zeros((count, depth - len(rows), width), f32)


def chunks(total, wanted):
    size = wanted if total % wanted == 0 else total
    return [(start, size) for start in range(0, total, size)]


def pack_kernel(pos_hbm, vel_hbm, charge_hbm, mass_hbm, centre_hbm, width_hbm, density_hbm,
                error_hbm, owners_hbm, halo_hbm, pairs_hbm, partner_hbm, decision_hbm, keep_ref,
                give_ref, ints_ref, pos_ref, vel_ref, charge_ref, mass_ref, centre_ref, width_ref,
                density_ref, error_ref, owners_ref, halo_ref, pairs_ref, partner_ref, decision_ref,
                sems):
    sources = (pos_hbm, vel_hbm, charge_hbm, mass_hbm, centre_hbm, width_hbm, density_hbm,
               error_hbm, owners_hbm, halo_hbm, pairs_hbm, partner_hbm, decision_hbm)
    targets = (pos_ref, vel_ref, charge_ref, mass_ref, centre_ref, width_ref, density_ref,
               error_ref, owners_ref, halo_ref, pairs_ref, partner_ref, decision_ref)
    copies = [
        pltpu.make_async_copy(source, target, sems.at[n])
        for n, (source, target) in enumerate(zip(sources, targets))
    ]
    for copy in copies:
        copy.start()
    for copy in copies:
        copy.wait()
    owned, own = owners_ref.shape
    _, sides, listed = halo_ref.shape
    ints_ref[...] = jnp.zeros_like(ints_ref)
    ints_ref[0:owned, 0:own] = owners_ref[...]
    ints_ref[owned : owned + sides, 0:listed] = halo_ref[0]
    last = owned + sides
    ints_ref[last : last + 1, 0 : partner_ref.shape[1]] = partner_ref[...]
    ints_ref[last + 1 : last + 2, 0 : decision_ref.shape[1]] = decision_ref[...]
    rows, near = pairs_ref.shape
    ints_ref[last + 2 : last + 2 + rows, 0:near] = pairs_ref[...]
    core = lax.axis_index("core")
    atoms, half = pos_ref.shape[2], centre_ref.shape[1] // CORES
    for out_ref, part in ((keep_ref, core), (give_ref, 1 - core)):
        for i in range(3):
            out_ref[i : i + 1, 0:atoms] = pos_ref[i]
            out_ref[3 + i : 4 + i, 0:atoms] = vel_ref[i]
        out_ref[6:7, 0:atoms] = charge_ref[...]
        out_ref[7:8, 0:atoms] = mass_ref[...]
        for core_of_half in range(CORES):

            @pl.when(part == core_of_half)
            def _():
                lanes = slice(core_of_half * half, (core_of_half + 1) * half)
                out_ref[0:3, atoms : atoms + half] = centre_ref[:, lanes]
                out_ref[3:4, atoms : atoms + half] = width_ref[:, lanes]
                out_ref[4:5, atoms : atoms + half] = density_ref[:, lanes]
                out_ref[5:6, atoms : atoms + half] = error_ref[:, lanes]
                out_ref[6:8, atoms : atoms + half] = jnp.zeros((2, half), f32)

        for block in range(ints_ref.shape[0] // 8):
            first = atoms + half + block * ints_ref.shape[1]
            out_ref[:, first : first + ints_ref.shape[1]] = ints_ref[
                block * 8 : (block + 1) * 8, :
            ].astype(f32)


def join_kernel(keep_ref, got_ref, state_ref, comp_ref, other_ref):
    core = lax.axis_index("core")
    atoms, half, lanes = state_ref.shape[2], comp_ref.shape[2], other_ref.shape[1]
    for place in range(CORES):
        mine = core == place
        state_ref[place] = jnp.where(mine, keep_ref[:, 0:atoms], got_ref[:, 0:atoms])
        part = slice(atoms, atoms + half)
        comp_ref[place] = jnp.where(mine, keep_ref[:, part], got_ref[:, part])
    for block in range(other_ref.shape[0] // 8):
        first = atoms + half + block * lanes
        other_ref[block * 8 : (block + 1) * 8, :] = got_ref[:, first : first + lanes].astype(jnp.int32)


def chosen(plan, ints_ref, refs):
    mine_ref, others = refs[0], refs[1:]
    row = lax.axis_index("rep")
    last = plan.owned + 2
    partner, decision = ints_ref[last : last + 1, :], ints_ref[last + 1 : last + 2, :]
    lane = lax.broadcasted_iota(jnp.int32, partner.shape, 1)
    sources = jnp.where(decision == 1, partner, lane)
    source = jnp.sum(jnp.where(lane == row, sources, 0).astype(f32), 1, keepdims=True)

    def read(*place):
        value = mine_ref[place]
        if plan.few:
            for n, other_ref in enumerate(others):
                other = jnp.bitwise_xor(row, n + 1).astype(f32)
                value = jnp.where(source == other, other_ref[place], value)
        else:
            for n in range(others[0].shape[0]):
                value = jnp.where(source == float(n), others[0][(n,) + place], value)
        return value

    return read


def make_lists(plan, mine_ref, theirs_ref, out_ref, waiting):
    core = lax.axis_index("core")

    def clear(domain, carry):
        waiting[domain] = -1
        return carry

    lax.fori_loop(0, plan.domains, clear, 0)

    def one_tile(tile, count):
        row = lax.rem(tile, plan.own)
        here = lax.div(tile, plan.own) == core
        for j in range(plan.owned):
            owner = jnp.where(here, mine_ref[j, row], theirs_ref[j, row])
            first = waiting[owner]
            out_ref[0, count] = owner
            out_ref[1, count] = first
            out_ref[2, count] = tile
            count = count + jnp.where(first < 0, 0, 1)
            waiting[owner] = jnp.where(first < 0, tile, -1)
        return count

    count = lax.fori_loop(0, plan.tiles, one_tile, 0)

    def leftover(domain, count):
        first = waiting[domain]
        out_ref[0, count] = domain
        out_ref[1, count] = first
        out_ref[2, count] = plan.tiles
        return count + jnp.where(first < 0, 0, 1)

    count = lax.fori_loop(0, plan.domains, leftover, count)
    for extra in range(UNROLL - 1):
        out_ref[0, count + extra] = 0
        out_ref[1, count + extra] = plan.tiles
        out_ref[2, count + extra] = plan.tiles
    out_ref[3, 0] = lax.div(count + UNROLL - 1, UNROLL)
    for side in range(2):
        for k in range(plan.listed):
            out_ref[3, 1 + side * plan.listed + k] = theirs_ref[plan.owned + side, k]
    for tile in range(plan.own):
        for j in range(plan.near):
            out_ref[4 + j, tile] = mine_ref[plan.owned + 4 + tile, j]


def partner_tile(plan, lists_ref, side, k):
    core = lax.axis_index("core")
    return (1 - core) * plan.own + lists_ref[3, 1 + side * plan.listed + k]


def for_pairs(lists_ref, body):
    def step(n, carry):
        for u in range(UNROLL):
            place = n * UNROLL + u
            body(place, lists_ref[0, place], lists_ref[1, place], lists_ref[2, place])
        return carry

    lax.fori_loop(0, lists_ref[3, 0], step, 0)


def sum_gaussians(plan, scale, lists_ref, state_ref, turned_ref, points_ref, out_ref, rim_ref, kept_ref,
                  xs, acc):
    tiles, listed, lanes = plan.tiles, plan.listed, plan.lanes
    store_rows(xs, point_rows([state_ref[i] for i in range(3)]))
    nowhere(xs, tiles)
    points_ref[...] = xs[...].astype(bf16)
    acc[...] = jnp.zeros_like(acc)
    core = lax.axis_index("core")
    for k in range(listed):
        tile = partner_tile(plan, lists_ref, 1 - core, k)
        for i, row in enumerate((0, 1, 2, 6)):
            rim_ref[i * listed + k : i * listed + k + 1, :] = state_ref[row, pl.ds(tile, 1), :]

    def one_pair(place, owner, first, second):
        points = jnp.concatenate([points_ref[first], points_ref[second]], 1)
        for start, size in chunks(plan.half, CHUNK):
            part = slice(start, start + size)
            g = jnp.exp2(dot(turned_ref[owner, part, :], points))
            acc[owner, part, :] += g[:, :lanes] + g[:, lanes:]
            kept_ref[place, part, :] = g

    for_pairs(lists_ref, one_pair)
    square = (lanes, lanes)
    diagonal = lax.broadcasted_iota(jnp.int32, square, 0) == lax.broadcasted_iota(jnp.int32, square, 1)
    for domain in range(plan.domains):
        for start, size in chunks(plan.half, lanes):
            column = jnp.sum(acc[domain, start : start + size, :], 1, keepdims=True)
            total = jnp.sum(jnp.where(diagonal, column, 0.0), 0, keepdims=True)
            out_ref[domain : domain + 1, start : start + size] = total * scale


def prepare_kernel(plan, ints_any, other_any, *refs):
    parts, refs = refs[:-8], refs[-8:]
    comp_ref, turned_ref, lists_ref, cs, ints, other_ints, waiting, sems = refs
    copies = [
        pltpu.make_async_copy(ints_any, ints, sems.at[0]),
        pltpu.make_async_copy(other_any, other_ints, sems.at[1]),
    ]
    for copy in copies:
        copy.start()
    height = lax.axis_index("z")
    for core in range(CORES):
        if plan.few:
            for n, part_ref in enumerate(parts):
                comp_ref[jnp.bitwise_xor(height, n) * CORES + core] = part_ref[core]
        else:
            for n in range(parts[1].shape[0]):
                comp_ref[n * CORES + core] = parts[1][n, core]
    store_rows(cs, centre_rows([comp_ref[:, i, :] for i in range(3)], comp_ref[:, 3, :]))
    for copy in copies:
        copy.wait()
    make_lists(plan, ints, other_ints, lists_ref, waiting)
    for domain in range(plan.domains):
        for start, size in chunks(plan.half, 128):
            turned_ref[domain, start : start + size, :] = cs[
                domain, :, start : start + size
            ].T.astype(bf16)


def first_kernel(plan, scale, lists_ref, ints_ref, turned_ref, *refs):
    copies_of_state, refs = refs[:-7], refs[-7:]
    out_ref, rim_ref, state_ref, points_ref, kept_ref, xs, acc = refs
    read = chosen(plan, ints_ref, copies_of_state)
    for core in range(CORES):
        for tile in range(plan.own):
            lanes = slice(tile * plan.lanes, (tile + 1) * plan.lanes)
            state_ref[:, core * plan.own + tile, :] = read(core, slice(None), lanes)
    sum_gaussians(plan, scale, lists_ref, state_ref, turned_ref, points_ref, out_ref, rim_ref,
                  kept_ref, xs, acc)


def stepped(old_ref, mine_ref, theirs_ref):
    mass = time_step * old_ref[7]
    for i in range(3):
        v = old_ref[3 + i] + mass * (mine_ref[i] + theirs_ref[i])
        yield old_ref[i] + time_step * v, v


def next_kernel(plan, scale, lists_ref, old_ref, force_ref, swapped_ref, turned_ref,
                out_ref, rim_ref, state_ref, points_ref, kept_ref, xs, acc):
    for i, (x, v) in enumerate(stepped(old_ref, force_ref, swapped_ref)):
        state_ref[i] = x
        state_ref[3 + i] = v
    state_ref[6] = old_ref[6]
    state_ref[7] = old_ref[7]
    sum_gaussians(plan, scale, lists_ref, state_ref, turned_ref, points_ref, out_ref, rim_ref,
                  kept_ref, xs, acc)


def tree_sum(refs):
    values = [ref[...] for ref in refs]
    while len(values) > 1:
        values = [values[i] + values[i + 1] for i in range(0, len(values), 2)]
    return values[0]


def add_kernel(*refs):
    refs[-1][...] = tree_sum(refs[:-1])


def finish_kernel(plan, old_ref, mine_ref, theirs_ref, x_ref, v_ref, map_ref, state):
    for i, (x, v) in enumerate(stepped(old_ref, mine_ref, theirs_ref)):
        state[i] = x
        state[3 + i] = v
    core = lax.axis_index("core")
    base = core * plan.own
    for tile in range(plan.own):
        lanes = slice(tile * plan.lanes, (tile + 1) * plan.lanes)
        for i in range(3):
            x_ref[i, :, lanes] = state[i, pl.ds(base + tile, 1), :]
            v_ref[i, :, lanes] = state[3 + i, pl.ds(base + tile, 1), :]
    first = core == 0
    pieces = plan.half // plan.lanes
    for n in range(pieces):
        keep = mine_ref[3, n : n + 1, :]
        got = theirs_ref[3, pieces + n : pieces + n + 1, :]
        low = slice(n * plan.lanes, (n + 1) * plan.lanes)
        high = slice(plan.half + n * plan.lanes, plan.half + (n + 1) * plan.lanes)
        map_ref[:, low] = jnp.where(first, keep, got)
        map_ref[:, high] = jnp.where(first, got, keep)


def pair_kernel(plan, gain, lists_ref, state_ref, far_ref, points_ref, out_ref, table, cs, rs, rows,
                turned):
    own, near, listed = plan.own, plan.near, plan.listed
    core = lax.axis_index("core")
    base = pl.multiple_of(core * own, own)
    extent = own + 2 * listed
    table[...] = jnp.zeros_like(table)
    for i, source in enumerate((0, 1, 2, 6)):
        table[i, 0:own, :] = state_ref[source, pl.ds(base, own), :]
        for k in range(listed):
            table[i, pl.ds(own + (1 - core) * listed + k, 1), :] = state_ref[
                source, pl.ds(partner_tile(plan, lists_ref, core, k), 1), :
            ]
            table[i, pl.ds(own + core * listed + k, 1), :] = far_ref[
                i * listed + k : i * listed + k + 1, :
            ]
    coords = [table[i] for i in range(3)]
    store_rows(cs, centre_rows(coords, jnp.full_like(coords[0], pair_width)))
    store_rows(rs, pull_rows(coords, table[3]))
    rows[...] = rs[...].astype(bf16)
    for entry in range(extent + 1):
        turned[entry] = cs[entry].T.astype(bf16)
    for tile in range(own):
        points = points_ref[base + tile]
        entries = [lists_ref[4 + j, tile] for j in range(near)]
        entries = [jnp.where(entry < 0, extent, entry) for entry in entries]
        left = jnp.concatenate([turned[entry] for entry in entries], 0)
        weights = jnp.concatenate([rows[entry] for entry in entries], 1)
        high, low = high_low(jnp.exp2(dot(left, points)))
        sums = dot(weights, high) + dot(weights, low)
        coords = [state_ref[i, pl.ds(base + tile, 1), :] for i in range(3)]
        strength = gain / pair_width * state_ref[6, pl.ds(base + tile, 1), :]
        for i, push in enumerate(squeeze_sums(coords, sums)):
            out_ref[i, tile : tile + 1, :] = strength * push


def push_kernel(plan, gain, replicas, lists_ref, state_ref, comp_ref, pair_ref, kept_ref, *refs):
    parts, (out_ref, rs, rows, means, sums) = refs[:-5], refs[-5:]
    tiles, lanes = plan.tiles, plan.lanes
    mean = tree_sum(parts) / replicas
    for n in range(plan.half // lanes):
        means[n] = mean[:, n * lanes : (n + 1) * lanes]
    error = comp_ref[:, 5, :]
    coefficient = gain * (mean - comp_ref[:, 4, :]) / (error * error) / comp_ref[:, 3, :]
    store_rows(rs, pull_rows([comp_ref[:, i, :] for i in range(3)], coefficient))
    rows[...] = rs[...].astype(bf16)
    sums[...] = jnp.zeros_like(sums)

    def one_pair(place, owner, first, second):
        total = None
        for start, size in chunks(plan.half, CHUNK):
            part = slice(start, start + size)
            weights = rows[owner, :, part]
            high, low = high_low(kept_ref[place, part, :])
            term = dot(weights, high) + dot(weights, low)
            total = term if total is None else total + term
        sums[first] += total[:, :lanes]
        sums[second] += total[:, lanes:]

    for_pairs(lists_ref, one_pair)

    def added(row):
        return sums[0:tiles, row, :] + sums[0:tiles, row + 1, :] + sums[0:tiles, row + 2, :]

    strength = added(0)
    for i in range(3):
        out_ref[i] = state_ref[i] * strength - added(3 + 3 * i)
    core = lax.axis_index("core")
    own = pl.ds(pl.multiple_of(core * plan.own, plan.own), plan.own)
    for i in range(3):
        out_ref[i, own, :] += pair_ref[i]

    pieces = plan.half // lanes
    here = lax.axis_index("z") * CORES
    out_ref[3] = jnp.zeros_like(out_ref[3])
    for n in range(pieces):
        keep = means[n, pl.ds(here + core, 1), :]
        give = means[n, pl.ds(here + 1 - core, 1), :]
        out_ref[3, n : n + 1, :] = keep
        out_ref[3, pieces + n : pieces + n + 1, :] = give


VMEM = pl.BlockSpec(memory_space=pltpu.VMEM)
SMEM = pl.BlockSpec(memory_space=pltpu.SMEM)
HBM = pl.BlockSpec(memory_space=pltpu.HBM)
ANY = pl.BlockSpec(memory_space=pl.ANY)


def shape(*dims, dtype=f32):
    return jax.ShapeDtypeStruct(dims, dtype)


def with_types(scratch):
    for entry in scratch:
        if not isinstance(entry, tuple):
            yield entry
        else:
            dims, dtype = entry if isinstance(entry[0], tuple) else (entry, f32)
            yield pltpu.VMEM(dims, dtype)


def call(kernel, args, outs, scratch=(), limit=16, spaces=None, out_spaces=None):
    many = isinstance(outs, (list, tuple))
    return pl.pallas_call(
        kernel,
        out_shape=tuple(outs) if many else outs,
        in_specs=spaces or [VMEM] * len(args),
        out_specs=tuple(out_spaces or [VMEM] * len(outs)) if many else VMEM,
        scratch_shapes=list(with_types(scratch)),
        compiler_params=pltpu.CompilerParams(vmem_limit_bytes=limit << 20),
    )(*args)


class Plan:
    pass


def swap_cores(value):
    return lax.ppermute(value, "core", [(0, 1), (1, 0)])


def few(replicas, heights):
    return replicas in (2, 4) and heights in (2, 4)


def stages(replicas, heights):
    return [("rep", list(range(1, replicas))), ("z", list(range(1, heights)))]


def exchange(value, axis, places):
    count = lax.axis_size(axis)
    others = []
    for n in places:
        others.append(lax.ppermute(value, axis, [(i, i ^ n) for i in range(count)]))
    return others


def everywhere(value, axis):
    copies = jnp.broadcast_to(value[None], (lax.axis_size(axis),) + value.shape)
    return lax.all_to_all(copies, axis, 0, 0, tiled=True)


def program(
    positions,
    velocities,
    charge,
    inverse_mass,
    pair_tiles,
    halo_tiles,
    owners,
    centres,
    widths,
    map_density,
    map_error,
    partner,
    decision,
):
    replicas = lax.axis_size("rep")
    heights = lax.axis_size("z")
    domains = heights * CORES
    own, owned = owners.shape
    plan = Plan()
    plan.own, plan.owned, plan.tiles, plan.domains = own, owned, own * CORES, domains
    plan.lanes = positions.shape[2] // own
    plan.near, plan.listed = pair_tiles.shape[1], halo_tiles.shape[2]
    components = widths.shape[0]
    half = plan.half = components // CORES
    tiles, lanes, listed = plan.tiles, plan.lanes, plan.listed

    args = [
        positions.transpose(1, 0, 2),
        velocities.transpose(1, 0, 2),
        charge[None],
        inverse_mass[None],
        centres,
        widths[None],
        map_density[None],
        map_error[None],
        owners.T,
        halo_tiles,
        pair_tiles,
        partner[None],
        decision[None],
    ]
    int_rows = -(-(owned + halo_tiles.shape[1] + 2 + own) // 8) * 8
    wide = own * lanes + half + int_rows // 8 * lanes
    keep, give, ints = call(
        pack_kernel,
        [pltpu.with_memory_space_constraint(arg, pltpu.HBM) for arg in args],
        [shape(8, wide), shape(8, wide), shape(int_rows, lanes, dtype=jnp.int32)],
        [(arg.shape, arg.dtype) for arg in args] + [pltpu.SemaphoreType.DMA((len(args),))],
        limit=8,
        spaces=[HBM] * len(args),
    )
    both_state, both_comps, other_ints = call(
        join_kernel,
        [keep, swap_cores(give)],
        [shape(CORES, 8, own * lanes), shape(CORES, 8, half),
         shape(int_rows, lanes, dtype=jnp.int32)],
    )
    plan.few = few(replicas, heights)
    if plan.few:
        comp_parts = [both_comps] + exchange(both_comps, "z", range(1, heights))
        states = [both_state] + exchange(both_state, "rep", range(1, replicas))
    else:
        comp_parts = [both_comps, everywhere(both_comps, "z")]
        states = [both_state, everywhere(both_state, "rep")]
    width = -(-((tiles * owned + domains) // 2 + UNROLL + 1) // lanes) * lanes
    lists_kept = pltpu.SMEM((4 + plan.near, width), jnp.int32)
    comps, turned, lists = call(
        functools.partial(prepare_kernel, plan),
        [ints, other_ints] + comp_parts,
        [shape(domains, 8, half), shape(domains, half, DEPTH, dtype=bf16), lists_kept],
        [(domains, DEPTH, half), pltpu.SMEM(ints.shape, jnp.int32),
         pltpu.SMEM(ints.shape, jnp.int32), pltpu.SMEM((domains,), jnp.int32),
         pltpu.SemaphoreType.DMA((2,))],
        spaces=[ANY, ANY] + [VMEM] * len(comp_parts),
        out_spaces=[VMEM, VMEM, SMEM],
    )
    lists = pltpu.with_memory_space_constraint(lists, pltpu.SMEM)

    map_gain = map_scale / (owned * components)
    scale = 1.0 / (owned * own * lanes)
    pair_gain = (plan.near * lanes) ** (-0.5)
    group = replicas * heights
    rim_rows = -(-4 * listed // 8) * 8
    onward = [(2 * i, (2 * i + 2) % domains) for i in range(heights)]
    onward += [((2 * i + 3) % domains, 2 * i + 1) for i in range(heights)]
    padded = -(-(own + 2 * listed + 1) // 8) * 8
    most = (tiles * owned + domains) // 2 + UNROLL
    outs = [
        shape(domains, half),
        shape(rim_rows, lanes),
        shape(8, tiles, lanes),
        shape(tiles + 1, DEPTH, lanes, dtype=bf16),
        shape(most, half, 2 * lanes),
    ]
    scratch = [(tiles + 1, DEPTH, lanes), (domains, half, lanes)]
    for step in range(STEPS):
        if step == 0:
            partial, rim, state, points, kept = call(
                functools.partial(first_kernel, plan, scale),
                [lists, ints, turned] + states,
                outs,
                scratch,
                spaces=[SMEM] + [VMEM] * (2 + len(states)),
            )
        else:
            partial, rim, state, points, kept = call(
                functools.partial(next_kernel, plan, scale),
                [lists, state, force, swapped, turned],
                outs,
                scratch,
                spaces=[SMEM] + [VMEM] * 4,
            )
        far = lax.ppermute(rim, ("z", "core"), onward)
        if plan.few:
            for number, (axis, places) in enumerate(stages(replicas, heights)):
                if number > 0:
                    partial = call(add_kernel, parts, shape(domains, half))
                parts = [partial] + exchange(partial, axis, places)
        else:
            pieces = lax.all_to_all(partial.reshape(group, -1), ("rep", "z"), 0, 0, tiled=True)
            piece = jnp.sum(pieces, 0)
            parts = [
                lax.all_to_all(
                    jnp.broadcast_to(piece[None], (group,) + piece.shape),
                    ("rep", "z"), 0, 0, tiled=True,
                ).reshape(domains, half)
            ]
        pair = call(
            functools.partial(pair_kernel, plan, pair_gain),
            [lists, state, far, points],
            shape(3, own, lanes),
            [(4, padded, lanes), (padded, DEPTH, lanes), (padded, ROWS, lanes),
             ((padded, ROWS, lanes), bf16), ((padded, lanes, DEPTH), bf16)],
            spaces=[SMEM] + [VMEM] * 3,
        )
        force = call(
            functools.partial(push_kernel, plan, map_gain, float(replicas)),
            [lists, state, comps, pair, kept] + parts,
            shape(4, tiles, lanes),
            [(domains, ROWS, half), ((domains, ROWS, half), bf16), (half // lanes, domains, lanes),
             (tiles + 1, ROWS, lanes)],
            spaces=[SMEM] + [VMEM] * (4 + len(parts)),
        )
        swapped = swap_cores(force)

    new_x, new_v, model_map = call(
        functools.partial(finish_kernel, plan),
        [state, force, swapped],
        [shape(3, 1, own * lanes), shape(3, 1, own * lanes), shape(1, components)],
        [(6, tiles, lanes)],
    )
    return (new_x.transpose(1, 0, 2), new_v.transpose(1, 0, 2), model_map.reshape(components))


def solution(mesh):
    replicas, domains = mesh.devices.shape
    split = Mesh(
        mesh.devices.reshape(replicas, domains // CORES, CORES), ("rep", "z", "core")
    )
    dom = ("z", "core")
    placed = (
        P("rep", None, dom),
        P("rep", None, dom),
        P(dom),
        P(dom),
        P(dom, None),
        P(dom, None, None),
        P(dom, None),
        P(None, dom),
        P(dom),
        P(dom),
        P(dom),
        P(),
        P(),
    )
    return jax.shard_map(
        program,
        mesh=split,
        in_specs=placed,
        out_specs=(P("rep", None, dom), P("rep", None, dom), P(dom)),
        check_vma=False,
    )
```

```python
import functools
import math

import jax
import jax.numpy as jnp
from jax import lax
from jax.experimental import pallas as pl
from jax.experimental.pallas import tpu as pltpu
from jax.sharding import Mesh, PartitionSpec as P

STEPS = 2
CORES = 2
DEPTH = 32
ROWS = 16
CHUNK = 128
UNROLL = 36
FAR_SQUARE = 1048576.0

time_step = 0.5
pair_width = 1.0
map_scale = 2.0
log2e = math.log2(math.e)
f32 = jnp.float32
bf16 = jnp.bfloat16

LEFT_PARTS = (0, 0, 1, 1, 0, 2)
RIGHT_PARTS = (0, 1, 0, 1, 2, 0)


def split3(value):
    high = value.astype(bf16).astype(f32)
    rest = value - high
    middle = rest.astype(bf16).astype(f32)
    return high, middle, rest - middle


def point_rows(coords):
    rows = []
    for coord in coords:
        parts = split3(coord)
        rows += [parts[i] for i in LEFT_PARTS]
    parts = split3(coords[0] * coords[0] + coords[1] * coords[1] + coords[2] * coords[2])
    rows += [parts[i] for i in LEFT_PARTS]
    one = jnp.ones_like(coords[0])
    return rows + [one, one, one]


def nowhere(ref, tile):
    shape = ref.shape[1:]
    row = lax.broadcasted_iota(jnp.int32, shape, 0)
    square = len(LEFT_PARTS) * 3
    ref[tile] = jnp.where(row == square, FAR_SQUARE, 0.0)


def centre_rows(coords, extent):
    scale = log2e / extent
    rows = []
    for coord in coords:
        parts = split3(coord * scale)
        rows += [parts[i] for i in RIGHT_PARTS]
    parts = split3(-0.5 * scale)
    rows += [parts[i] for i in RIGHT_PARTS]
    square = coords[0] * coords[0] + coords[1] * coords[1] + coords[2] * coords[2]
    return rows + list(split3(-0.5 * scale * square))


def pull_rows(coords, weight):
    rows = list(split3(weight))
    for coord in coords:
        rows += list(split3(coord * weight))
    return rows


def squeeze_sums(coords, sums):
    def total(first):
        return sums[first : first + 1] + sums[first + 1 : first + 2] + sums[first + 2 : first + 3]

    strength = total(0)
    return [coords[i] * strength - total(3 + 3 * i) for i in range(3)]


def dot(left, right):
    return jnp.dot(left, right, preferred_element_type=f32)


def high_low(value):
    high = value.astype(bf16)
    return high, (value - high.astype(f32)).astype(bf16)


def store_rows(ref, rows):
    count, depth, width = rows[0].shape[0], ref.shape[1], ref.shape[2]
    for index, row in enumerate(rows):
        ref[0:count, index, :] = row
    if len(rows) < depth:
        ref[0:count, len(rows) : depth, :] = jnp.zeros((count, depth - len(rows), width), f32)


def chunks(total, wanted):
    size = wanted if total % wanted == 0 else total
    return [(start, size) for start in range(0, total, size)]


def pack_kernel(pos_hbm, vel_hbm, charge_hbm, mass_hbm, centre_hbm, width_hbm, density_hbm,
                error_hbm, owners_hbm, halo_hbm, pairs_hbm, partner_hbm, decision_hbm, keep_ref,
                give_ref, ints_ref, pos_ref, vel_ref, charge_ref, mass_ref, centre_ref, width_ref,
                density_ref, error_ref, owners_ref, halo_ref, pairs_ref, partner_ref, decision_ref,
                sems):
    sources = (pos_hbm, vel_hbm, charge_hbm, mass_hbm, centre_hbm, width_hbm, density_hbm,
               error_hbm, owners_hbm, halo_hbm, pairs_hbm, partner_hbm, decision_hbm)
    targets = (pos_ref, vel_ref, charge_ref, mass_ref, centre_ref, width_ref, density_ref,
               error_ref, owners_ref, halo_ref, pairs_ref, partner_ref, decision_ref)
    copies = [
        pltpu.make_async_copy(source, target, sems.at[n])
        for n, (source, target) in enumerate(zip(sources, targets))
    ]
    for copy in copies:
        copy.start()
    for copy in copies:
        copy.wait()
    owned, own = owners_ref.shape
    _, sides, listed = halo_ref.shape
    ints_ref[...] = jnp.zeros_like(ints_ref)
    ints_ref[0:owned, 0:own] = owners_ref[...]
    ints_ref[owned : owned + sides, 0:listed] = halo_ref[0]
    last = owned + sides
    ints_ref[last : last + 1, 0 : partner_ref.shape[1]] = partner_ref[...]
    ints_ref[last + 1 : last + 2, 0 : decision_ref.shape[1]] = decision_ref[...]
    rows, near = pairs_ref.shape
    ints_ref[last + 2 : last + 2 + rows, 0:near] = pairs_ref[...]
    core = lax.axis_index("core")
    atoms, half = pos_ref.shape[2], centre_ref.shape[1] // CORES
    for out_ref, part in ((keep_ref, core), (give_ref, 1 - core)):
        for i in range(3):
            out_ref[i : i + 1, 0:atoms] = pos_ref[i]
            out_ref[3 + i : 4 + i, 0:atoms] = vel_ref[i]
        out_ref[6:7, 0:atoms] = charge_ref[...]
        out_ref[7:8, 0:atoms] = mass_ref[...]
        for core_of_half in range(CORES):

            @pl.when(part == core_of_half)
            def _():
                lanes = slice(core_of_half * half, (core_of_half + 1) * half)
                out_ref[0:3, atoms : atoms + half] = centre_ref[:, lanes]
                out_ref[3:4, atoms : atoms + half] = width_ref[:, lanes]
                out_ref[4:5, atoms : atoms + half] = density_ref[:, lanes]
                out_ref[5:6, atoms : atoms + half] = error_ref[:, lanes]
                out_ref[6:8, atoms : atoms + half] = jnp.zeros((2, half), f32)

        for block in range(ints_ref.shape[0] // 8):
            first = atoms + half + block * ints_ref.shape[1]
            out_ref[:, first : first + ints_ref.shape[1]] = ints_ref[
                block * 8 : (block + 1) * 8, :
            ].astype(f32)


def join_kernel(keep_ref, got_ref, state_ref, comp_ref, other_ref):
    core = lax.axis_index("core")
    atoms, half, lanes = state_ref.shape[2], comp_ref.shape[2], other_ref.shape[1]
    for place in range(CORES):
        mine = core == place
        state_ref[place] = jnp.where(mine, keep_ref[:, 0:atoms], got_ref[:, 0:atoms])
        part = slice(atoms, atoms + half)
        comp_ref[place] = jnp.where(mine, keep_ref[:, part], got_ref[:, part])
    for block in range(other_ref.shape[0] // 8):
        first = atoms + half + block * lanes
        other_ref[block * 8 : (block + 1) * 8, :] = got_ref[:, first : first + lanes].astype(jnp.int32)


def chosen(plan, ints_ref, refs):
    mine_ref, others = refs[0], refs[1:]
    row = lax.axis_index("rep")
    last = plan.owned + 2
    partner, decision = ints_ref[last : last + 1, :], ints_ref[last + 1 : last + 2, :]
    lane = lax.broadcasted_iota(jnp.int32, partner.shape, 1)
    sources = jnp.where(decision == 1, partner, lane)
    source = jnp.sum(jnp.where(lane == row, sources, 0).astype(f32), 1, keepdims=True)

    def read(*place):
        value = mine_ref[place]
        if plan.few:
            for n, other_ref in enumerate(others):
                other = jnp.bitwise_xor(row, n + 1).astype(f32)
                value = jnp.where(source == other, other_ref[place], value)
        else:
            for n in range(others[0].shape[0]):
                value = jnp.where(source == float(n), others[0][(n,) + place], value)
        return value

    return read


def make_lists(plan, mine_ref, theirs_ref, out_ref, waiting):
    core = lax.axis_index("core")

    def clear(domain, carry):
        waiting[domain] = -1
        return carry

    lax.fori_loop(0, plan.domains, clear, 0)

    def one_tile(tile, count):
        row = lax.rem(tile, plan.own)
        here = lax.div(tile, plan.own) == core
        for j in range(plan.owned):
            owner = jnp.where(here, mine_ref[j, row], theirs_ref[j, row])
            first = waiting[owner]
            out_ref[0, count] = owner
            out_ref[1, count] = first
            out_ref[2, count] = tile
            count = count + jnp.where(first < 0, 0, 1)
            waiting[owner] = jnp.where(first < 0, tile, -1)
        return count

    count = lax.fori_loop(0, plan.tiles, one_tile, 0)

    def leftover(domain, count):
        first = waiting[domain]
        out_ref[0, count] = domain
        out_ref[1, count] = first
        out_ref[2, count] = plan.tiles
        return count + jnp.where(first < 0, 0, 1)

    count = lax.fori_loop(0, plan.domains, leftover, count)
    for extra in range(UNROLL - 1):
        out_ref[0, count + extra] = 0
        out_ref[1, count + extra] = plan.tiles
        out_ref[2, count + extra] = plan.tiles
    out_ref[3, 0] = lax.div(count + UNROLL - 1, UNROLL)
    for side in range(2):
        for k in range(plan.listed):
            out_ref[3, 1 + side * plan.listed + k] = theirs_ref[plan.owned + side, k]
    for tile in range(plan.own):
        for j in range(plan.near):
            out_ref[4 + j, tile] = mine_ref[plan.owned + 4 + tile, j]


def partner_tile(plan, lists_ref, side, k):
    core = lax.axis_index("core")
    return (1 - core) * plan.own + lists_ref[3, 1 + side * plan.listed + k]


def for_pairs(plan, lists_ref, body):
    def step(n, carry):
        for u in range(UNROLL):
            entry = n * UNROLL + u
            place = jnp.minimum(entry, plan.most)
            body(place, lists_ref[0, entry], lists_ref[1, entry], lists_ref[2, entry])
        return carry

    lax.fori_loop(0, lists_ref[3, 0], step, 0)


def sum_gaussians(plan, scale, lists_ref, state_ref, turned_ref, points_ref, out_ref, rim_ref, kept_ref,
                  xs, acc):
    tiles, listed, lanes = plan.tiles, plan.listed, plan.lanes
    store_rows(xs, point_rows([state_ref[i] for i in range(3)]))
    nowhere(xs, tiles)
    points_ref[...] = xs[...].astype(bf16)
    acc[...] = jnp.zeros_like(acc)
    core = lax.axis_index("core")
    for k in range(listed):
        tile = partner_tile(plan, lists_ref, 1 - core, k)
        for i, row in enumerate((0, 1, 2, 6)):
            rim_ref[i * listed + k : i * listed + k + 1, :] = state_ref[row, pl.ds(tile, 1), :]

    def one_pair(place, owner, first, second):
        points = jnp.concatenate([points_ref[first], points_ref[second]], 1)
        for start, size in chunks(plan.half, CHUNK):
            part = slice(start, start + size)
            g = jnp.exp2(dot(turned_ref[owner, part, :], points))
            acc[owner, part, :] += g[:, :lanes] + g[:, lanes:]
            kept_ref[place, part, :] = g

    for_pairs(plan, lists_ref, one_pair)
    square = (lanes, lanes)
    diagonal = lax.broadcasted_iota(jnp.int32, square, 0) == lax.broadcasted_iota(jnp.int32, square, 1)
    for domain in range(plan.domains):
        for start, size in chunks(plan.half, lanes):
            column = jnp.sum(acc[domain, start : start + size, :], 1, keepdims=True)
            total = jnp.sum(jnp.where(diagonal, column, 0.0), 0, keepdims=True)
            out_ref[domain : domain + 1, start : start + size] = total * scale


def prepare_kernel(plan, ints_any, other_any, *refs):
    parts, refs = refs[:-8], refs[-8:]
    comp_ref, turned_ref, lists_ref, cs, ints, other_ints, waiting, sems = refs
    copies = [
        pltpu.make_async_copy(ints_any, ints, sems.at[0]),
        pltpu.make_async_copy(other_any, other_ints, sems.at[1]),
    ]
    for copy in copies:
        copy.start()
    height = lax.axis_index("z")
    for core in range(CORES):
        if plan.few:
            for n, part_ref in enumerate(parts):
                comp_ref[jnp.bitwise_xor(height, n) * CORES + core] = part_ref[core]
        else:
            for n in range(parts[1].shape[0]):
                comp_ref[n * CORES + core] = parts[1][n, core]
    store_rows(cs, centre_rows([comp_ref[:, i, :] for i in range(3)], comp_ref[:, 3, :]))
    for copy in copies:
        copy.wait()
    make_lists(plan, ints, other_ints, lists_ref, waiting)
    for domain in range(plan.domains):
        for start, size in chunks(plan.half, 128):
            turned_ref[domain, start : start + size, :] = cs[
                domain, :, start : start + size
            ].T.astype(bf16)


def first_kernel(plan, scale, lists_ref, ints_ref, turned_ref, *refs):
    copies_of_state, refs = refs[:-7], refs[-7:]
    out_ref, rim_ref, state_ref, points_ref, kept_ref, xs, acc = refs
    read = chosen(plan, ints_ref, copies_of_state)
    for core in range(CORES):
        for tile in range(plan.own):
            lanes = slice(tile * plan.lanes, (tile + 1) * plan.lanes)
            state_ref[:, core * plan.own + tile, :] = read(core, slice(None), lanes)
    sum_gaussians(plan, scale, lists_ref, state_ref, turned_ref, points_ref, out_ref, rim_ref,
                  kept_ref, xs, acc)


def stepped(old_ref, mine_ref, theirs_ref):
    mass = time_step * old_ref[7]
    for i in range(3):
        v = old_ref[3 + i] + mass * (mine_ref[i] + theirs_ref[i])
        yield old_ref[i] + time_step * v, v


def next_kernel(plan, scale, lists_ref, old_ref, force_ref, swapped_ref, turned_ref,
                out_ref, rim_ref, state_ref, points_ref, kept_ref, xs, acc):
    for i, (x, v) in enumerate(stepped(old_ref, force_ref, swapped_ref)):
        state_ref[i] = x
        state_ref[3 + i] = v
    state_ref[6] = old_ref[6]
    state_ref[7] = old_ref[7]
    sum_gaussians(plan, scale, lists_ref, state_ref, turned_ref, points_ref, out_ref, rim_ref,
                  kept_ref, xs, acc)


def tree_sum(refs):
    values = [ref[...] for ref in refs]
    while len(values) > 1:
        values = [values[i] + values[i + 1] for i in range(0, len(values), 2)]
    return values[0]


def add_kernel(*refs):
    refs[-1][...] = tree_sum(refs[:-1])


def finish_kernel(plan, old_ref, mine_ref, theirs_ref, x_ref, v_ref, map_ref, state):
    for i, (x, v) in enumerate(stepped(old_ref, mine_ref, theirs_ref)):
        state[i] = x
        state[3 + i] = v
    core = lax.axis_index("core")
    base = core * plan.own
    for tile in range(plan.own):
        lanes = slice(tile * plan.lanes, (tile + 1) * plan.lanes)
        for i in range(3):
            x_ref[i, :, lanes] = state[i, pl.ds(base + tile, 1), :]
            v_ref[i, :, lanes] = state[3 + i, pl.ds(base + tile, 1), :]
    first = core == 0
    pieces = plan.half // plan.lanes
    for n in range(pieces):
        keep = mine_ref[3, n : n + 1, :]
        got = theirs_ref[3, pieces + n : pieces + n + 1, :]
        low = slice(n * plan.lanes, (n + 1) * plan.lanes)
        high = slice(plan.half + n * plan.lanes, plan.half + (n + 1) * plan.lanes)
        map_ref[:, low] = jnp.where(first, keep, got)
        map_ref[:, high] = jnp.where(first, got, keep)


def pair_kernel(plan, gain, lists_ref, state_ref, far_ref, points_ref, out_ref, table, cs, rs, rows,
                turned):
    own, near, listed = plan.own, plan.near, plan.listed
    core = lax.axis_index("core")
    base = pl.multiple_of(core * own, own)
    extent = own + 2 * listed
    table[...] = jnp.zeros_like(table)
    for i, source in enumerate((0, 1, 2, 6)):
        table[i, 0:own, :] = state_ref[source, pl.ds(base, own), :]
        for k in range(listed):
            table[i, pl.ds(own + (1 - core) * listed + k, 1), :] = state_ref[
                source, pl.ds(partner_tile(plan, lists_ref, core, k), 1), :
            ]
            table[i, pl.ds(own + core * listed + k, 1), :] = far_ref[
                i * listed + k : i * listed + k + 1, :
            ]
    coords = [table[i] for i in range(3)]
    store_rows(cs, centre_rows(coords, jnp.full_like(coords[0], pair_width)))
    store_rows(rs, pull_rows(coords, table[3]))
    rows[...] = rs[...].astype(bf16)
    for entry in range(extent + 1):
        turned[entry] = cs[entry].T.astype(bf16)
    for tile in range(own):
        points = points_ref[base + tile]
        entries = [lists_ref[4 + j, tile] for j in range(near)]
        entries = [jnp.where(entry < 0, extent, entry) for entry in entries]
        left = jnp.concatenate([turned[entry] for entry in entries], 0)
        weights = jnp.concatenate([rows[entry] for entry in entries], 1)
        high, low = high_low(jnp.exp2(dot(left, points)))
        sums = dot(weights, high) + dot(weights, low)
        coords = [state_ref[i, pl.ds(base + tile, 1), :] for i in range(3)]
        strength = gain / pair_width * state_ref[6, pl.ds(base + tile, 1), :]
        for i, push in enumerate(squeeze_sums(coords, sums)):
            out_ref[i, tile : tile + 1, :] = strength * push


def push_kernel(plan, gain, replicas, lists_ref, state_ref, comp_ref, pair_ref, kept_ref, *refs):
    parts, (out_ref, rs, rows, means, sums) = refs[:-5], refs[-5:]
    tiles, lanes = plan.tiles, plan.lanes
    mean = tree_sum(parts) / replicas
    for n in range(plan.half // lanes):
        means[n] = mean[:, n * lanes : (n + 1) * lanes]
    error = comp_ref[:, 5, :]
    coefficient = gain * (mean - comp_ref[:, 4, :]) / (error * error) / comp_ref[:, 3, :]
    store_rows(rs, pull_rows([comp_ref[:, i, :] for i in range(3)], coefficient))
    rows[...] = rs[...].astype(bf16)
    sums[...] = jnp.zeros_like(sums)

    def one_pair(place, owner, first, second):
        total = None
        for start, size in chunks(plan.half, CHUNK):
            part = slice(start, start + size)
            weights = rows[owner, :, part]
            high, low = high_low(kept_ref[place, part, :])
            term = dot(weights, high) + dot(weights, low)
            total = term if total is None else total + term
        sums[first] += total[:, :lanes]
        sums[second] += total[:, lanes:]

    for_pairs(plan, lists_ref, one_pair)

    def added(row):
        return sums[0:tiles, row, :] + sums[0:tiles, row + 1, :] + sums[0:tiles, row + 2, :]

    strength = added(0)
    for i in range(3):
        out_ref[i] = state_ref[i] * strength - added(3 + 3 * i)
    core = lax.axis_index("core")
    own = pl.ds(pl.multiple_of(core * plan.own, plan.own), plan.own)
    for i in range(3):
        out_ref[i, own, :] += pair_ref[i]

    pieces = plan.half // lanes
    here = lax.axis_index("z") * CORES
    out_ref[3] = jnp.zeros_like(out_ref[3])
    for n in range(pieces):
        keep = means[n, pl.ds(here + core, 1), :]
        give = means[n, pl.ds(here + 1 - core, 1), :]
        out_ref[3, n : n + 1, :] = keep
        out_ref[3, pieces + n : pieces + n + 1, :] = give


VMEM = pl.BlockSpec(memory_space=pltpu.VMEM)
SMEM = pl.BlockSpec(memory_space=pltpu.SMEM)
HBM = pl.BlockSpec(memory_space=pltpu.HBM)
ANY = pl.BlockSpec(memory_space=pl.ANY)


def shape(*dims, dtype=f32):
    return jax.ShapeDtypeStruct(dims, dtype)


def with_types(scratch):
    for entry in scratch:
        if not isinstance(entry, tuple):
            yield entry
        else:
            dims, dtype = entry if isinstance(entry[0], tuple) else (entry, f32)
            yield pltpu.VMEM(dims, dtype)


def call(kernel, args, outs, scratch=(), limit=16, spaces=None, out_spaces=None):
    many = isinstance(outs, (list, tuple))
    return pl.pallas_call(
        kernel,
        out_shape=tuple(outs) if many else outs,
        in_specs=spaces or [VMEM] * len(args),
        out_specs=tuple(out_spaces or [VMEM] * len(outs)) if many else VMEM,
        scratch_shapes=list(with_types(scratch)),
        compiler_params=pltpu.CompilerParams(vmem_limit_bytes=limit << 20),
    )(*args)


class Plan:
    pass


def swap_cores(value):
    return lax.ppermute(value, "core", [(0, 1), (1, 0)])


def few(replicas, heights):
    return replicas in (2, 4) and heights in (2, 4)


def stages(replicas, heights):
    return [("rep", list(range(1, replicas))), ("z", list(range(1, heights)))]


def exchange(value, axis, places):
    count = lax.axis_size(axis)
    others = []
    for n in places:
        others.append(lax.ppermute(value, axis, [(i, i ^ n) for i in range(count)]))
    return others


def everywhere(value, axis):
    copies = jnp.broadcast_to(value[None], (lax.axis_size(axis),) + value.shape)
    return lax.all_to_all(copies, axis, 0, 0, tiled=True)


def program(
    positions,
    velocities,
    charge,
    inverse_mass,
    pair_tiles,
    halo_tiles,
    owners,
    centres,
    widths,
    map_density,
    map_error,
    partner,
    decision,
):
    replicas = lax.axis_size("rep")
    heights = lax.axis_size("z")
    domains = heights * CORES
    own, owned = owners.shape
    plan = Plan()
    plan.own, plan.owned, plan.tiles, plan.domains = own, owned, own * CORES, domains
    plan.lanes = positions.shape[2] // own
    plan.near, plan.listed = pair_tiles.shape[1], halo_tiles.shape[2]
    components = widths.shape[0]
    half = plan.half = components // CORES
    tiles, lanes, listed = plan.tiles, plan.lanes, plan.listed

    args = [
        positions.transpose(1, 0, 2),
        velocities.transpose(1, 0, 2),
        charge[None],
        inverse_mass[None],
        centres,
        widths[None],
        map_density[None],
        map_error[None],
        owners.T,
        halo_tiles,
        pair_tiles,
        partner[None],
        decision[None],
    ]
    int_rows = -(-(owned + halo_tiles.shape[1] + 2 + own) // 8) * 8
    wide = own * lanes + half + int_rows // 8 * lanes
    keep, give, ints = call(
        pack_kernel,
        [pltpu.with_memory_space_constraint(arg, pltpu.HBM) for arg in args],
        [shape(8, wide), shape(8, wide), shape(int_rows, lanes, dtype=jnp.int32)],
        [(arg.shape, arg.dtype) for arg in args] + [pltpu.SemaphoreType.DMA((len(args),))],
        limit=8,
        spaces=[HBM] * len(args),
    )
    both_state, both_comps, other_ints = call(
        join_kernel,
        [keep, swap_cores(give)],
        [shape(CORES, 8, own * lanes), shape(CORES, 8, half),
         shape(int_rows, lanes, dtype=jnp.int32)],
    )
    plan.few = few(replicas, heights)
    if plan.few:
        comp_parts = [both_comps] + exchange(both_comps, "z", range(1, heights))
        states = [both_state] + exchange(both_state, "rep", range(1, replicas))
    else:
        comp_parts = [both_comps, everywhere(both_comps, "z")]
        states = [both_state, everywhere(both_state, "rep")]
    width = -(-((tiles * owned + domains) // 2 + UNROLL + 1) // lanes) * lanes
    lists_kept = pltpu.SMEM((4 + plan.near, width), jnp.int32)
    comps, turned, lists = call(
        functools.partial(prepare_kernel, plan),
        [ints, other_ints] + comp_parts,
        [shape(domains, 8, half), shape(domains, half, DEPTH, dtype=bf16), lists_kept],
        [(domains, DEPTH, half), pltpu.SMEM(ints.shape, jnp.int32),
         pltpu.SMEM(ints.shape, jnp.int32), pltpu.SMEM((domains,), jnp.int32),
         pltpu.SemaphoreType.DMA((2,))],
        spaces=[ANY, ANY] + [VMEM] * len(comp_parts),
        out_spaces=[VMEM, VMEM, SMEM],
    )
    lists = pltpu.with_memory_space_constraint(lists, pltpu.SMEM)

    map_gain = map_scale / (owned * components)
    scale = 1.0 / (owned * own * lanes)
    pair_gain = (plan.near * lanes) ** (-0.5)
    group = replicas * heights
    rim_rows = -(-4 * listed // 8) * 8
    onward = [(2 * i, (2 * i + 2) % domains) for i in range(heights)]
    onward += [((2 * i + 3) % domains, 2 * i + 1) for i in range(heights)]
    padded = -(-(own + 2 * listed + 1) // 8) * 8
    plan.most = (tiles * owned + domains) // 2
    outs = [
        shape(domains, half),
        shape(rim_rows, lanes),
        shape(8, tiles, lanes),
        shape(tiles + 1, DEPTH, lanes, dtype=bf16),
        shape(plan.most + 1, half, 2 * lanes),
    ]
    scratch = [(tiles + 1, DEPTH, lanes), (domains, half, lanes)]
    for step in range(STEPS):
        if step == 0:
            partial, rim, state, points, kept = call(
                functools.partial(first_kernel, plan, scale),
                [lists, ints, turned] + states,
                outs,
                scratch,
                spaces=[SMEM] + [VMEM] * (2 + len(states)),
            )
        else:
            partial, rim, state, points, kept = call(
                functools.partial(next_kernel, plan, scale),
                [lists, state, force, swapped, turned],
                outs,
                scratch,
                spaces=[SMEM] + [VMEM] * 4,
            )
        far = lax.ppermute(rim, ("z", "core"), onward)
        if plan.few:
            for number, (axis, places) in enumerate(stages(replicas, heights)):
                if number > 0:
                    partial = call(add_kernel, parts, shape(domains, half))
                parts = [partial] + exchange(partial, axis, places)
        else:
            pieces = lax.all_to_all(partial.reshape(group, -1), ("rep", "z"), 0, 0, tiled=True)
            piece = jnp.sum(pieces, 0)
            parts = [
                lax.all_to_all(
                    jnp.broadcast_to(piece[None], (group,) + piece.shape),
                    ("rep", "z"), 0, 0, tiled=True,
                ).reshape(domains, half)
            ]
        pair = call(
            functools.partial(pair_kernel, plan, pair_gain),
            [lists, state, far, points],
            shape(3, own, lanes),
            [(4, padded, lanes), (padded, DEPTH, lanes), (padded, ROWS, lanes),
             ((padded, ROWS, lanes), bf16), ((padded, lanes, DEPTH), bf16)],
            spaces=[SMEM] + [VMEM] * 3,
        )
        force = call(
            functools.partial(push_kernel, plan, map_gain, float(replicas)),
            [lists, state, comps, pair, kept] + parts,
            shape(4, tiles, lanes),
            [(domains, ROWS, half), ((domains, ROWS, half), bf16), (half // lanes, domains, lanes),
             (tiles + 1, ROWS, lanes)],
            spaces=[SMEM] + [VMEM] * (4 + len(parts)),
        )
        swapped = swap_cores(force)

    new_x, new_v, model_map = call(
        functools.partial(finish_kernel, plan),
        [state, force, swapped],
        [shape(3, 1, own * lanes), shape(3, 1, own * lanes), shape(1, components)],
        [(6, tiles, lanes)],
    )
    return (new_x.transpose(1, 0, 2), new_v.transpose(1, 0, 2), model_map.reshape(components))


def solution(mesh):
    replicas, domains = mesh.devices.shape
    split = Mesh(
        mesh.devices.reshape(replicas, domains // CORES, CORES), ("rep", "z", "core")
    )
    dom = ("z", "core")
    placed = (
        P("rep", None, dom),
        P("rep", None, dom),
        P(dom),
        P(dom),
        P(dom, None),
        P(dom, None, None),
        P(dom, None),
        P(None, dom),
        P(dom),
        P(dom),
        P(dom),
        P(),
        P(),
    )
    return jax.shard_map(
        program,
        mesh=split,
        in_specs=placed,
        out_specs=(P("rep", None, dom), P("rep", None, dom), P(dom)),
        check_vma=False,
    )
```
